512 devices in a mesh: dp: 16 (over y_lo, z), gx: 8 (over x, core), gy: 4 (over y_hi).
Axes of the slice: x: 4, y: 8 (y_hi: 4, y_lo: 2; y = y_hi * 2 + y_lo), z: 8, core: 2. Of those that a mesh axis runs over, the one named last changes fastest.
Arguments:
- fields: bfloat16 [16, 20, 32, 16384], P('dp', None, None, ('gx', 'gy')), may hold values from -6 to 6
- cotangent: bfloat16 [16, 20, 32, 16384], P('dp', None, None, ('gx', 'gy')), may hold values from -6 to 6
- mix_weight: bfloat16 [20, 20], replicated, may hold values from -1.25 to 1.25
- spectral_weight: bfloat16 [288, 2, 20, 20], P(('gx', 'gy')), may hold values from -1 to 1
Outputs:
- output: bfloat16 [16, 20, 32, 16384], P('dp', None, None, ('gx', 'gy'))
- spectral_grad: float32 [288, 2, 20, 20], P(('gx', 'gy'))
- mixing_grad: float32 [20, 20], replicated
The draws below stay inside these ranges and needn't reach their ends.
All inputs are finite; a program needn't handle non-finite values.
Results may differ from the reference program's by a relative error of at most 0.0031.
Values may be sent and summed in bfloat16 or wider, within the bound.
A program may use at most 64 MiB of HBM per device.

```python
import math
import jax
import jax.numpy as jnp
from jax import lax

C = 20
NX = 128
NY = 128
KX = 24
KY = 12
P_SIZE = 32
MODES = 288
CELLS = 16384
SAMPLES = 16


def block_scale(stream_key, extent, pieces, smallest, largest):
    def one(position, parts):
        draws = jax.random.uniform(jax.random.fold_in(jax.random.fold_in(stream_key, 6), position), (parts,), jnp.float32, smallest / len(pieces), largest / len(pieces))
        return jnp.repeat(jnp.exp(draws), extent[position] // parts).reshape((-1,) + (1,) * (len(extent) - position - 1))

    factor_of = one(*pieces[0])
    for cut in pieces[1:]:
        factor_of = factor_of * one(*cut)
    return factor_of


def normal_values(rng, extent, width, limit, pieces=(), kind=jnp.bfloat16):
    drawn = width * jax.random.normal(rng, extent, jnp.float32)
    if pieces:
        drawn = drawn * block_scale(rng, extent, pieces, -0.22, 0.18)
    return jnp.clip(drawn, -limit, limit).astype(kind)


def setup_inputs(seed: int = 0) -> dict:
    keys = jax.random.split(jax.random.key(seed), 5)
    fields = normal_values(keys[0], (SAMPLES, C, P_SIZE, CELLS), 1.0, 6.0, ((0, 16), (3, 32)))
    cotangent = normal_values(keys[1], (SAMPLES, C, P_SIZE, CELLS), 1.0, 6.0, ((0, 16), (3, 32)))
    mix_weight = normal_values(keys[2], (C, C), C ** -0.5, 1.25)
    spectral_weight = normal_values(keys[3], (MODES, 2, C, C), (2 * C) ** -0.5, 1.0, ((0, 32),))
    return {"fields": fields, "cotangent": cotangent, "mix_weight": mix_weight, "spectral_weight": spectral_weight}


HI = lax.Precision.HIGHEST

def gelu_value(h):
    k = math.sqrt(2.0 / math.pi)
    t = jnp.tanh(k * (h + 0.044715 * h * h * h))
    return 0.5 * h * (1.0 + t)

def gelu_slope(h):
    k = math.sqrt(2.0 / math.pi)
    t = jnp.tanh(k * (h + 0.044715 * h * h * h))
    return 0.5 * (1.0 + t) + 0.5 * h * (1.0 - t * t) * k * (1.0 + 3.0 * 0.044715 * h * h)

def axis_table(waves, n):
    cells = jnp.arange(n, dtype=jnp.int32)
    angle = 2.0 * math.pi / n * (waves[:, None] * cells[None, :] % n).astype(jnp.float32)
    return (jnp.cos(angle), jnp.sin(angle))

def tables():
    index = jnp.arange(KX, dtype=jnp.int32)
    waves_x = jnp.where(index < KX // 2, index, NX - KX + index).astype(jnp.int32)
    cos_x, sin_x = axis_table(waves_x, NX)
    cos_y, sin_y = axis_table(jnp.arange(KY, dtype=jnp.int32), NY)
    return (cos_x, sin_x, cos_y, sin_y)

def forward_dft(data, scale):
    cos_x, sin_x, cos_y, sin_y = tables()
    a_re = jnp.einsum('cpxy,ky->cpxk', data, cos_y, precision=HI)
    a_im = -jnp.einsum('cpxy,ky->cpxk', data, sin_y, precision=HI)
    s_re = jnp.einsum('cpxk,jx->jkcp', a_re, cos_x, precision=HI) + jnp.einsum('cpxk,jx->jkcp', a_im, sin_x, precision=HI)
    s_im = jnp.einsum('cpxk,jx->jkcp', a_im, cos_x, precision=HI) - jnp.einsum('cpxk,jx->jkcp', a_re, sin_x, precision=HI)
    chans, planes = (data.shape[0], data.shape[1])
    return scale * jnp.stack([s_re.reshape(MODES, chans, planes), s_im.reshape(MODES, chans, planes)], axis=1)

def inverse_dft(vals, scale):
    cos_x, sin_x, cos_y, sin_y = tables()
    chans, planes = (vals.shape[2], vals.shape[3])
    v_re = vals[:, 0].reshape(KX, KY, chans, planes)
    v_im = vals[:, 1].reshape(KX, KY, chans, planes)
    b_re = jnp.einsum('jkdp,jx->dpxk', v_re, cos_x, precision=HI) - jnp.einsum('jkdp,jx->dpxk', v_im, sin_x, precision=HI)
    b_im = jnp.einsum('jkdp,jx->dpxk', v_re, sin_x, precision=HI) + jnp.einsum('jkdp,jx->dpxk', v_im, cos_x, precision=HI)
    return scale * (jnp.einsum('dpxk,ky->dpxy', b_re, cos_y, precision=HI) - jnp.einsum('dpxk,ky->dpxy', b_im, sin_y, precision=HI))

def spectral_mix(spec, weight):
    w = weight.astype(jnp.float32)
    v_re = jnp.einsum('mcp,mcd->mdp', spec[:, 0], w[:, 0], precision=HI) - jnp.einsum('mcp,mcd->mdp', spec[:, 1], w[:, 1], precision=HI)
    v_im = jnp.einsum('mcp,mcd->mdp', spec[:, 0], w[:, 1], precision=HI) + jnp.einsum('mcp,mcd->mdp', spec[:, 1], w[:, 0], precision=HI)
    return jnp.stack([v_re, v_im], axis=1)

def grads_of(spec, gspec):
    g_re = jnp.einsum('mcp,mdp->mcd', spec[:, 0], gspec[:, 0], precision=HI) + jnp.einsum('mcp,mdp->mcd', spec[:, 1], gspec[:, 1], precision=HI)
    g_im = jnp.einsum('mcp,mdp->mcd', spec[:, 0], gspec[:, 1], precision=HI) - jnp.einsum('mcp,mdp->mcd', spec[:, 1], gspec[:, 0], precision=HI)
    return jnp.stack([g_re, g_im], axis=1)

def reference(fields, cotangent, mix_weight, spectral_weight):
    norm_in = 1.0 / math.sqrt(NX * NY)
    norm_out = 1.0 / math.sqrt(MODES)
    mixing = mix_weight.astype(jnp.float32)

    def one_sample(pair):
        chans, planes = (pair[0].shape[0], pair[0].shape[1])
        field = pair[0].astype(jnp.float32).reshape(chans, planes, NX, NY)
        grad_out = pair[1].astype(jnp.float32).reshape(chans, planes, NX, NY)
        spec = forward_dft(field, norm_in)
        vals = spectral_mix(spec, spectral_weight)
        branch = inverse_dft(vals, norm_out)
        pre = branch + jnp.einsum('cpxy,cd->dpxy', field, mixing, precision=HI)
        result = gelu_value(pre).astype(jnp.bfloat16).reshape(chans, planes, NX * NY)
        back = (grad_out * gelu_slope(pre)).astype(jnp.bfloat16).astype(jnp.float32)
        gspec = forward_dft(back, norm_out)
        spec_grad = grads_of(spec, gspec)
        mix_grad = jnp.einsum('cpxy,dpxy->cd', field, back, precision=HI)
        return (result, spec_grad, mix_grad)
    output, spec_grads, mix_grads = lax.map(one_sample, (fields, cotangent))
    spectral_grad = lax.optimization_barrier(jnp.sum(spec_grads, axis=0)) / math.sqrt(SAMPLES * P_SIZE)
    mixing_grad = lax.optimization_barrier(jnp.sum(mix_grads, axis=0)) / math.sqrt(SAMPLES * P_SIZE * NX * NY)
    return (output, spectral_grad, mixing_grad)
```

```python
import functools
import math

import jax
import jax.numpy as jnp
import numpy as np
from jax import lax
from jax.experimental import pallas as pl
from jax.experimental.pallas import tpu as pltpu
from jax.sharding import PartitionSpec as P

MESH = pl.DeviceIdType.MESH
F32 = jnp.float32
BF16 = jnp.bfloat16

C = 20
NY = 128
KY = 12
GY = 4
XL = 4
PL_OWN = 4
TILES = 12


def split(table):
    table = np.asarray(table, np.float32)
    hi = table.astype(BF16)
    lo = (table - hi.astype(np.float32)).astype(BF16)
    return np.stack([hi, lo])


@functools.lru_cache(None)
def tables(G):
    nx, kxn = 16 * G, 3 * G
    norm_in = 1.0 / math.sqrt(nx * NY)
    norm_out = 1.0 / math.sqrt(kxn * KY)
    y = np.arange(NY)
    tyf = np.zeros((XL * NY, 128))
    tyi = np.zeros((128, XL * NY))
    for kk in range(3):
        for ks in range(4):
            ang = 2 * np.pi * ((3 * ks + kk) * y % NY) / NY
            for x in range(XL):
                col = kk * 32 + ks * 8 + x * 2
                tyf[x * NY : (x + 1) * NY, col] = np.cos(ang) * norm_in
                tyf[x * NY : (x + 1) * NY, col + 1] = -np.sin(ang) * norm_in
                tyi[col, x * NY : (x + 1) * NY] = np.cos(ang)
                tyi[col + 1, x * NY : (x + 1) * NY] = -np.sin(ang)
    wxp = np.zeros((GY, GY * 6 * G, 32 * G))
    wxi = np.zeros((GY, 32 * G, GY * 8 * G))
    for gy in range(GY):
        for go in range(GY):
            for tri in range(3):
                jj, ks = divmod(3 * go + tri, 4)
                for gq in range(G):
                    j = 3 * gq + jj
                    kx = j if j < kxn // 2 else nx - kxn + j
                    rp = go * 6 * G + gq * 6 + tri * 2
                    ci = go * 8 * G + gq * 8 + tri
                    for gx in range(G):
                        for x in range(XL):
                            ang = 2 * np.pi * (kx * (4 * (gx * GY + gy) + x) % nx) / nx
                            c, s = np.cos(ang), np.sin(ang)
                            k = gx * 32 + ks * 8 + x * 2
                            wxp[gy, rp, k], wxp[gy, rp, k + 1] = c, s
                            wxp[gy, rp + 1, k], wxp[gy, rp + 1, k + 1] = -s, c
                            wxi[gy, k, ci], wxi[gy, k, ci + 4] = c * norm_out, -s * norm_out
                            wxi[gy, k + 1, ci], wxi[gy, k + 1, ci + 4] = s * norm_out, c * norm_out
    px = np.zeros((16 * G, 6 * G))
    pab = np.zeros((3, 16 * G, 32 * G))
    for gq in range(G):
        for ri in range(2):
            for tri in range(3):
                row = gq * 8 + ri * 4 + tri
                px[row, gq * 6 + tri * 2 + ri] = 1
                px[8 * G + row, gq * 6 + tri * 2 + 1 - ri] = 1
                for kk in range(3):
                    src = gq * 32 + kk * 8
                    pab[kk, row, src + tri] = 1
                    pab[kk, 8 * G + row, src + 4 + tri] = -1 if ri == 0 else 1
    selw = np.zeros((32, 18 * 24))
    for kk in range(3):
        for ri in range(2):
            for tri in range(3):
                q = (tri * 3 + kk) * 2 + ri
                selw[kk * 8 + ri * 4 + tri, q * 24 : q * 24 + C] = 1
    lane = np.arange(256)
    ok = lane < 240
    kk, c, i = lane // 80, lane % 80 // 4, lane % 4
    e1 = ((np.arange(24)[:, None] == c[None]) & ok[None]).astype(np.float32)
    same = (kk[:, None] == kk[None]) & (i[:, None] == i[None]) & ok[:, None] & ok[None]
    gmask = np.concatenate([same, same], axis=1).astype(np.float32)
    e2 = np.zeros((512, 128))
    for r in range(2):
        for l in range(240):
            e2[r * 256 + l, r * 60 + kk[l] * 20 + c[l]] = 1
    b = lambda a: np.asarray(a, np.float32).astype(BF16)
    return dict(
        tyf=split(tyf),
        tyi=split(tyi),
        wxp=np.stack([split(w) for w in wxp]),
        wxi=np.stack([split(w) for w in wxi]),
        px=b(px),
        pab=b(pab.reshape(48 * G, 32 * G)),
        selw=b(selw),
        e1=b(e1),
        e2=b(e2),
        gmask=b(gmask),
    )


def mm(a, b):
    return jnp.dot(a, b, preferred_element_type=F32)


def mm_nt(a, b):
    return lax.dot_general(a, b, (((1,), (1,)), ((), ())), preferred_element_type=F32)


def hilo(a):
    hi = a.astype(BF16)
    return hi, (a - hi.astype(F32)).astype(BF16)


def mm_tab(tab, x):
    hi, lo = hilo(x)
    return mm(tab[0], hi) + (mm(tab[0], lo) + mm(tab[1], hi))


def iota(shape, dim):
    return lax.broadcasted_iota(jnp.int32, shape, dim)


def onehot(cond):
    return jnp.where(cond, 1.0, 0.0).astype(BF16)


def gelu_parts(h):
    k = math.sqrt(2.0 / math.pi)
    hh = h * h
    t = jnp.tanh(k * (h + 0.044715 * (hh * h)))
    value = 0.5 * h * (1.0 + t)
    slope = 0.5 * (1.0 + t) + 0.5 * h * (1.0 - t * t) * (k * (1.0 + 3.0 * 0.044715 * hh))
    return value, slope


def kernel(
    G, D, f_ref, mix_ref, w_ref, tyf_ref, px_ref, pab_ref, selw_ref, e1_ref, e2_ref, gmask_ref,
    cot_hbm, tyi_hbm, wxp_hbm, wxi_hbm,
    out_ref, sg_ref, mg_ref,
    cot, tyi, wxp, wxi, a3, mixed, mixpad, backb,
    sx1, rx1, sx3, rx3, sy1, ry1, sy3, ry3, sy2, ry2, sx2, rx2,
    ws, rw, wst, rq, bc, sspec, rspec, sgs, rgs, stt,
    mgx_s, mgx_r, mgy_s, mgy_r, part, rsbuf, agbuf, agsrc,
    lsem, bx_s, bx_r, by_s, by_r, dp_s, dp_r,
):
    rows = C * 4 * G
    planes = 4 * G
    gx = lax.axis_index("gx")
    gy = lax.axis_index("gy")
    dp = lax.axis_index("dp")
    tpr = max(1, -(-TILES // D))
    nred = TILES // tpr

    barrier = pltpu.get_barrier_semaphore()
    for k in range(1, G):
        pl.semaphore_signal(barrier, inc=1, device_id={"gx": lax.rem(gx + k, G)}, device_id_type=MESH)
    for k in range(1, GY):
        pl.semaphore_signal(barrier, inc=1, device_id={"gy": lax.rem(gy + k, GY)}, device_id_type=MESH)
    for k in range(1, D):
        pl.semaphore_signal(barrier, inc=1, device_id={"dp": lax.rem(dp + k, D)}, device_id_type=MESH)

    loads = [
        pltpu.make_async_copy(wxp_hbm.at[gy], wxp, lsem.at[0]),
        pltpu.make_async_copy(cot_hbm, cot, lsem.at[1]),
        pltpu.make_async_copy(tyi_hbm, tyi, lsem.at[2]),
        pltpu.make_async_copy(wxi_hbm.at[gy], wxi, lsem.at[3]),
    ]
    for copy in loads:
        copy.start()

    pending = []

    def exchange(axis, size, me, src_of, dst, sems_s, sems_r, ex):
        def one(k):
            peer = lax.rem(me + k, size)
            return pltpu.make_async_remote_copy(
                src_ref=src_of(peer),
                dst_ref=dst.at[me],
                send_sem=sems_s.at[ex, k],
                recv_sem=sems_r.at[ex, k],
                device_id={axis: peer},
                device_id_type=MESH,
            )

        copies = [one(k) for k in range(1, size)]
        for copy in copies:
            copy.start()
        pending.extend(copies)

        def wait():
            for copy in copies:
                copy.wait_recv()

        return wait

    def ex_x(src_of, dst, ex):
        return exchange("gx", G, gx, src_of, dst, bx_s, bx_r, ex)

    def ex_y(src_of, dst, ex):
        return exchange("gy", GY, gy, src_of, dst, by_s, by_r, ex)

    chunk = min(128, rows)
    starts = list(range(0, rows, chunk))

    def y_forward(data, r0, n):
        a = mm(data, tyf_ref[0]) + mm(data, tyf_ref[1])
        a3[r0 : r0 + n, :] = a
        a3[rows + r0 : rows + r0 + n, :] = pltpu.roll(a, 96, 1)
        a3[2 * rows + r0 : 2 * rows + r0 + n, :] = pltpu.roll(a, 64, 1)

    def to_groups(dst):
        for g in range(G):
            block = a3[pl.ds(g, 240, stride=G), :]
            block = jnp.concatenate([block, jnp.zeros((16, 128), F32)], axis=0)
            dst[g] = block.T[:32]

    for r0 in starts:
        n = min(chunk, rows - r0)
        y_forward(f_ref[r0 : r0 + n, :], r0, n)
    to_groups(sx1)
    pl.semaphore_wait(barrier, G - 1 + GY - 1 + D - 1)
    wait_x1 = ex_x(lambda peer: sx1.at[peer], rx1, 0)
    rx1[gx] = sx1[gx]

    wst[...] = jnp.zeros_like(wst)
    for m in range(9):
        for ri in range(2):
            q = (m * 2 + ri) * 24
            wst[q : q + C, 0:C] = w_ref[m, ri].astype(F32)
    ohd = onehot(iota((128, 640), 0) == (iota((128, 640), 1) & 31))
    wexp = mm(wst[...].astype(BF16), ohd)
    wparts = []
    for q in range(18):
        piece = wexp[q * 24 : q * 24 + 24]
        cond = iota((24, 640), 0) == (iota((24, 640), 1) >> 5)
        wparts.append(jnp.where(cond, piece, 0.0))
    wmasked = jnp.concatenate(wparts, axis=0).astype(BF16)
    ws[...] = mm(selw_ref[...], wmasked).astype(BF16)
    wait_w = ex_x(lambda peer: ws, rw, 1)
    rw[gx] = ws[...]

    mixpad[...] = jnp.zeros_like(mixpad)
    mixpad[0:C, 0:C] = mix_ref[...].astype(F32)
    mixb = mixpad[...].astype(BF16)
    shift = int(math.log2(planes))
    ecol = onehot((iota((128, rows), 1) >> shift) == iota((128, rows), 0))
    for r0 in starts:
        n = min(chunk, rows - r0)
        erow = onehot(((iota((n, 128), 0) + r0) >> shift) == iota((n, 128), 1))
        kron = mm(mm_nt(erow, mixb).astype(BF16), ecol)
        diag = ((iota((n, rows), 0) + r0) & (planes - 1)) == (iota((n, rows), 1) & (planes - 1))
        kron = jnp.where(diag, kron, 0.0).astype(BF16)
        mixed[r0 : r0 + n, :] = mm(kron, f_ref[...])

    for q in range(5):
        lanes = iota((128, 512), 1)
        bc[q] = onehot(iota((128, 512), 0) == ((lanes >> 7) + 4 * q) * 4 + (lanes & 3))
    lanes = iota((128, 512), 1)
    ohr = onehot(iota((128, 512), 0) == (lanes >> 7) * 32 + ((lanes & 127) >> 2))

    def x_forward(recv, send):
        r = recv[...].reshape(32 * G, 256)
        hi, lo = hilo(r)
        p = mm(wxp[0], hi) + (mm(wxp[0], lo) + mm(wxp[1], hi))
        send[...] = p.reshape(GY, 6 * G, 256)

    def y_sum(recv):
        return (recv[0] + recv[1]) + (recv[2] + recv[3])

    loads[0].wait()
    wait_x1()
    x_forward(rx1, sy1)
    wait_y1 = ex_y(lambda peer: sy1.at[peer], ry1, 0)
    ry1[gy] = sy1[gy]

    wait_w()
    rab = mm(pab_ref[...], rw[...].reshape(32 * G, 640)).astype(BF16)
    for q in range(5):
        rq[q] = mm(rab[:, q * 128 : (q + 1) * 128], ohr)

    wait_y1()
    shi, slo = hilo(y_sum(ry1))
    both = mm(px_ref[...], shi) + mm(px_ref[...], slo)
    sspec[...] = both[: 8 * G].reshape(G, 8, 256)

    parts = [both[:, :128]] + [pltpu.roll(both, 256 - 80 * kk, 1)[:, :128] for kk in (1, 2)]
    stacked = jnp.concatenate(parts, axis=0)
    xhi, xlo = hilo(stacked)
    acc = jnp.zeros((48 * G, 128), F32)
    for q in range(5):
        spread = (mm(xhi, bc[q]) + mm(xlo, bc[q])) * rq[q]
        acc += (spread[:, :128] + spread[:, 128:256]) + (spread[:, 256:384] + spread[:, 384:])
    acc = acc.reshape(3, 2, 8 * G, 128)
    acc = acc[:, 0] + acc[:, 1]
    zero = jnp.zeros((8 * G, 128), F32)
    wide = [jnp.concatenate([acc[kk], zero], axis=1) for kk in range(3)]
    vals = wide[0] + pltpu.roll(wide[1], 80, 1) + pltpu.roll(wide[2], 160, 1)
    sy2[...] = vals.astype(BF16)
    wait_y2 = ex_y(lambda peer: sy2, ry2, 1)
    ry2[gy] = sy2[...]

    wait_spec = ex_x(lambda peer: sspec.at[peer], rspec, 2)
    rspec[gx] = sspec[gx]

    loads[3].wait()
    wait_y2()
    v = ry2[...].reshape(32 * G, 256)
    b = mm(wxi[0], v) + mm(wxi[1], v)
    sx2[...] = b.astype(BF16).reshape(G, 32, 256)
    wait_x2 = ex_x(lambda peer: sx2.at[peer], rx2, 3)
    rx2[gx] = sx2[gx]

    wait_spec()
    for tri in range(3):
        s0 = rspec[:, tri : tri + 1, :].reshape(G, 256)
        s1 = rspec[:, 4 + tri : 5 + tri, :].reshape(G, 256)
        block = jnp.concatenate([s0, s1, jnp.zeros((128 - 2 * G, 256), F32)], axis=0)
        stt[tri] = block.T

    loads[1].wait()
    loads[2].wait()
    wait_x2()
    for g in range(G):
        block = rx2[g].astype(F32)
        block = jnp.concatenate([block, jnp.zeros((96, 256), F32)], axis=0)
        a3[pl.ds(g, 240, stride=G), :] = block.T[:240]
    for r0 in starts:
        n = min(chunk, rows - r0)
        bb = a3[r0 : r0 + n, :]
        bb += pltpu.roll(a3[rows + r0 : rows + r0 + n, :], 32, 1)
        bb += pltpu.roll(a3[2 * rows + r0 : 2 * rows + r0 + n, :], 64, 1)
        bb = bb.astype(BF16)
        pre = (mm(bb, tyi[0]) + mm(bb, tyi[1])) + mixed[r0 : r0 + n, :]
        value, slope = gelu_parts(pre)
        out_ref[r0 : r0 + n, :] = value.astype(BF16)
        back = (cot[r0 : r0 + n, :].astype(F32) * slope).astype(BF16)
        backb[r0 : r0 + n, :] = back
        y_forward(back, r0, n)
    to_groups(sx3)
    wait_x3 = ex_x(lambda peer: sx3.at[peer], rx3, 4)
    rx3[gx] = sx3[gx]

    gmix = jnp.zeros((24, 128), F32)
    ecol_t = onehot((iota((rows, 128), 0) >> shift) == iota((rows, 128), 1))
    for r0 in starts:
        n = min(chunk, rows - r0)
        full = mm_nt(f_ref[r0 : r0 + n, :], backb[...])
        diag = ((iota((n, rows), 0) + r0) & (planes - 1)) == (iota((n, rows), 1) & (planes - 1))
        hi, lo = hilo(jnp.where(diag, full, 0.0))
        cols = mm(hi, ecol_t) + mm(lo, ecol_t)
        erow_t = onehot(((iota((24, n), 1) + r0) >> shift) == iota((24, n), 0))
        hi, lo = hilo(cols)
        gmix += mm(erow_t, hi) + mm(erow_t, lo)
    mgx_s[...] = gmix
    wait_mgx = ex_x(lambda peer: mgx_s, mgx_r, 5)
    mgx_r[gx] = gmix

    wait_x3()
    x_forward(rx3, sy3)
    wait_y3 = ex_y(lambda peer: sy3.at[peer], ry3, 2)
    ry3[gy] = sy3[gy]

    wait_mgx()
    total = mgx_r[0]
    for k in range(1, G):
        total += mgx_r[k]
    mgy_s[...] = total
    wait_mgy = ex_y(lambda peer: mgy_s, mgy_r, 3)
    mgy_r[gy] = total

    wait_y3()
    ghi, glo = hilo(y_sum(ry3))
    half = px_ref[0 : 8 * G, :]
    sgs[...] = (mm(half, ghi) + mm(half, glo)).reshape(G, 8, 256)
    wait_gs = ex_x(lambda peer: sgs.at[peer], rgs, 6)
    rgs[gx] = sgs[gx]

    wait_mgy()
    mix_scale = 1.0 / math.sqrt(D * planes * 16 * G * NY)
    part[9:12] = (((mgy_r[0] + mgy_r[1]) + (mgy_r[2] + mgy_r[3])) * mix_scale).reshape(3, 8, 128)

    norm_in = 1.0 / math.sqrt(16 * G * NY)
    norm_out = 1.0 / math.sqrt(36 * G)
    spec_scale = norm_out / norm_in / math.sqrt(D * planes)
    wait_gs()
    gm = gmask_ref[...].astype(F32)
    for tri in range(3):
        g0 = rgs[:, tri : tri + 1, :].reshape(G, 256)
        g1 = rgs[:, 4 + tri : 5 + tri, :].reshape(G, 256)
        top = jnp.concatenate([g0, g1], axis=1)
        bot = jnp.concatenate([g1, -g0], axis=1)
        gg = jnp.concatenate([top, bot, jnp.zeros((128 - 2 * G, 512), F32)], axis=0)
        ahi, alo = hilo(stt[tri])
        bhi, blo = hilo(gg)
        outer = (mm(ahi, bhi) + (mm(ahi, blo) + mm(alo, bhi))) * gm
        ohi, olo = hilo(outer)
        fold = mm(e1_ref[...], ohi) + mm(e1_ref[...], olo)
        fhi, flo = hilo(fold)
        grad = (mm(fhi, e2_ref[...]) + mm(flo, e2_ref[...])) * spec_scale
        part[3 * tri : 3 * tri + 3] = grad.reshape(3, 8, 128)

    def rs_copy(k, to):
        return pltpu.make_async_remote_copy(
            src_ref=part.at[pl.ds(to * tpr, tpr)],
            dst_ref=rsbuf.at[dp],
            send_sem=dp_s.at[0, k],
            recv_sem=dp_r.at[0, k],
            device_id={"dp": to},
            device_id_type=MESH,
        )

    def ag_copy(k, to, slot):
        return pltpu.make_async_remote_copy(
            src_ref=agsrc,
            dst_ref=agbuf.at[slot],
            send_sem=dp_s.at[1, k],
            recv_sem=dp_r.at[1, k],
            device_id={"dp": to},
            device_id_type=MESH,
        )

    for k in range(1, D):
        to = lax.rem(dp + k, D)

        @pl.when(to < nred)
        def _():
            rs_copy(k, to).start()

    @pl.when(dp < nred)
    def _():
        rsbuf[dp] = part[pl.ds(dp * tpr, tpr)]
        for k in range(1, D):
            rs_copy(k, dp).wait_recv()
        tile = rsbuf[0]
        for k in range(1, D):
            tile += rsbuf[k]
        agsrc[...] = tile
        for k in range(1, D):
            ag_copy(k, lax.rem(dp + k, D), dp).start()
        agbuf[dp] = tile

    for k in range(1, D):
        frm = lax.rem(dp + D - k, D)

        @pl.when(frm < nred)
        def _():
            ag_copy(k, dp, frm).wait_recv()

    final = agbuf[...].reshape(TILES, 8, 128)
    mg_ref[...] = final[9:12].reshape(24, 128)[:C, :C]
    for tri in range(3):
        block = final[3 * tri : 3 * tri + 3].reshape(24, 128)
        for kk in range(3):
            for ri in range(2):
                off = ri * 60 + kk * 20
                sg_ref[tri * 3 + kk, ri] = block[:C, off : off + C]

    for copy in pending:
        copy.wait_send()
    for k in range(1, D):
        to = lax.rem(dp + k, D)

        @pl.when(to < nred)
        def _():
            rs_copy(k, to).wait_send()

    @pl.when(dp < nred)
    def _():
        for k in range(1, D):
            ag_copy(k, lax.rem(dp + k, D), dp).wait_send()


def local(G, D, fields, cotangent, mix_weight, spectral_weight):
    rows = C * 4 * G
    cells = XL * NY
    t = tables(G)
    tpr = max(1, -(-TILES // D))
    nred = TILES // tpr
    vm = pl.BlockSpec(memory_space=pltpu.VMEM)
    hbm = pl.BlockSpec(memory_space=pl.ANY)
    V = pltpu.VMEM
    scratch = [
        V((rows, cells), BF16),
        V((2, 128, cells), BF16),
        V((2, GY * 6 * G, 32 * G), BF16),
        V((2, 32 * G, GY * 8 * G), BF16),
        V((3 * rows, 128), F32),
        V((rows, cells), F32),
        V((128, 128), F32),
        V((rows, cells), BF16),
        V((G, 32, 256), F32),
        V((G, 32, 256), F32),
        V((G, 32, 256), F32),
        V((G, 32, 256), F32),
        V((GY, 6 * G, 256), F32),
        V((GY, 6 * G, 256), F32),
        V((GY, 6 * G, 256), F32),
        V((GY, 6 * G, 256), F32),
        V((8 * G, 256), BF16),
        V((GY, 8 * G, 256), BF16),
        V((G, 32, 256), BF16),
        V((G, 32, 256), BF16),
        V((32, 640), BF16),
        V((G, 32, 640), BF16),
        V((432, 128), F32),
        V((5, 48 * G, 512), F32),
        V((5, 128, 512), BF16),
        V((G, 8, 256), F32),
        V((G, 8, 256), F32),
        V((G, 8, 256), F32),
        V((G, 8, 256), F32),
        V((3, 256, 128), F32),
        V((24, 128), F32),
        V((G, 24, 128), F32),
        V((24, 128), F32),
        V((GY, 24, 128), F32),
        V((TILES, 8, 128), F32),
        V((D, tpr, 8, 128), F32),
        V((nred, tpr, 8, 128), F32),
        V((tpr, 8, 128), F32),
        pltpu.SemaphoreType.DMA((4,)),
        pltpu.SemaphoreType.DMA((7, G)),
        pltpu.SemaphoreType.DMA((7, G)),
        pltpu.SemaphoreType.DMA((4, GY)),
        pltpu.SemaphoreType.DMA((4, GY)),
        pltpu.SemaphoreType.DMA((2, D)),
        pltpu.SemaphoreType.DMA((2, D)),
    ]
    out, sg, mg = pl.pallas_call(
        functools.partial(kernel, G, D),
        out_shape=(
            jax.ShapeDtypeStruct((rows, cells), BF16),
            jax.ShapeDtypeStruct((9, 2, C, C), F32),
            jax.ShapeDtypeStruct((C, C), F32),
        ),
        in_specs=[vm] * 10 + [hbm] * 4,
        out_specs=(vm, vm, vm),
        scratch_shapes=scratch,
        compiler_params=pltpu.CompilerParams(
            collective_id=0, has_side_effects=True, vmem_limit_bytes=60 * 1024 * 1024
        ),
    )(
        fields.reshape(rows, cells),
        mix_weight,
        spectral_weight,
        t["tyf"],
        t["px"],
        t["pab"],
        t["selw"],
        t["e1"],
        t["e2"],
        t["gmask"],
        cotangent.reshape(rows, cells),
        t["tyi"],
        t["wxp"],
        t["wxi"],
    )
    return out.reshape(fields.shape), sg, mg


def solution(mesh):
    G, D = mesh.shape["gx"], mesh.shape["dp"]
    cells = P("dp", None, None, ("gx", "gy"))
    modes = P(("gx", "gy"), None, None, None)
    return jax.shard_map(
        functools.partial(local, G, D),
        mesh=mesh,
        in_specs=(cells, cells, P(), modes),
        out_specs=(cells, modes, P()),
        check_vma=False,
    )
```

```python
import functools
import math

import jax
import jax.numpy as jnp
import numpy as np
from jax import lax
from jax.experimental import pallas as pl
from jax.experimental.pallas import tpu as pltpu
from jax.sharding import PartitionSpec as P

MESH = pl.DeviceIdType.MESH
F32 = jnp.float32
BF16 = jnp.bfloat16

C = 20
NY = 128
KY = 12
GY = 4
XL = 4
PL_OWN = 4
TILES = 12


def split(table):
    table = np.asarray(table, np.float32)
    hi = table.astype(BF16)
    lo = (table - hi.astype(np.float32)).astype(BF16)
    return np.stack([hi, lo])


@functools.lru_cache(None)
def tables(G):
    nx, kxn = 16 * G, 3 * G
    norm_in = 1.0 / math.sqrt(nx * NY)
    norm_out = 1.0 / math.sqrt(kxn * KY)
    y = np.arange(NY)
    tyf = np.zeros((XL * NY, 128))
    tyi = np.zeros((128, XL * NY))
    for kk in range(3):
        for ks in range(4):
            ang = 2 * np.pi * ((3 * ks + kk) * y % NY) / NY
            for x in range(XL):
                col = kk * 32 + ks * 8 + x * 2
                tyf[x * NY : (x + 1) * NY, col] = np.cos(ang) * norm_in
                tyf[x * NY : (x + 1) * NY, col + 1] = -np.sin(ang) * norm_in
                tyi[col, x * NY : (x + 1) * NY] = np.cos(ang)
                tyi[col + 1, x * NY : (x + 1) * NY] = -np.sin(ang)
    wxp = np.zeros((GY, GY * 6 * G, 32 * G))
    wxi = np.zeros((GY, 32 * G, GY * 8 * G))
    for gy in range(GY):
        for go in range(GY):
            for tri in range(3):
                jj, ks = divmod(3 * go + tri, 4)
                for gq in range(G):
                    j = 3 * gq + jj
                    kx = j if j < kxn // 2 else nx - kxn + j
                    rp = go * 6 * G + gq * 6 + tri * 2
                    ci = go * 8 * G + gq * 8 + tri
                    for gx in range(G):
                        for x in range(XL):
                            ang = 2 * np.pi * (kx * (4 * (gx * GY + gy) + x) % nx) / nx
                            c, s = np.cos(ang), np.sin(ang)
                            k = gx * 32 + ks * 8 + x * 2
                            wxp[gy, rp, k], wxp[gy, rp, k + 1] = c, s
                            wxp[gy, rp + 1, k], wxp[gy, rp + 1, k + 1] = -s, c
                            wxi[gy, k, ci], wxi[gy, k, ci + 4] = c * norm_out, -s * norm_out
                            wxi[gy, k + 1, ci], wxi[gy, k + 1, ci + 4] = s * norm_out, c * norm_out
    px = np.zeros((16 * G, 6 * G))
    pab = np.zeros((3, 16 * G, 32 * G))
    for gq in range(G):
        for ri in range(2):
            for tri in range(3):
                row = gq * 8 + ri * 4 + tri
                px[row, gq * 6 + tri * 2 + ri] = 1
                px[8 * G + row, gq * 6 + tri * 2 + 1 - ri] = 1
                for kk in range(3):
                    src = gq * 32 + kk * 8
                    pab[kk, row, src + tri] = 1
                    pab[kk, 8 * G + row, src + 4 + tri] = -1 if ri == 0 else 1
    selw = np.zeros((32, 18 * 24))
    for kk in range(3):
        for ri in range(2):
            for tri in range(3):
                q = (tri * 3 + kk) * 48 + ri
                selw[kk * 8 + ri * 4 + tri, q : q + 2 * C : 2] = 1
    lane = np.arange(256)
    ok = lane % 128 < 120
    kk, c = lane % 128 // 40, lane // 128 * 10 + lane % 128 % 40 // 4
    e1 = ((np.arange(24)[:, None] == c[None]) & ok[None]).astype(np.float32)
    e2 = np.zeros((512, 128))
    for r in range(2):
        for l in lane[ok]:
            e2[r * 256 + l, r * 60 + kk[l] * 20 + c[l]] = 1
    b = lambda a: np.asarray(a, np.float32).astype(BF16)
    return dict(
        tyf=split(tyf),
        tyi=split(tyi),
        wxp=np.stack([split(w) for w in wxp]),
        wxi=np.stack([split(w) for w in wxi]),
        px=b(px),
        pab=b(pab.reshape(48 * G, 32 * G)),
        selw=b(selw),
        e1=b(e1),
        e2=b(e2),
    )


def mm(a, b):
    return jnp.dot(a, b, preferred_element_type=F32)


def mm_nt(a, b):
    return lax.dot_general(a, b, (((1,), (1,)), ((), ())), preferred_element_type=F32)


def hilo(a):
    hi = a.astype(BF16)
    return hi, (a - hi.astype(F32)).astype(BF16)


def mm_tab(tab, x):
    hi, lo = hilo(x)
    return mm(tab[0], hi) + (mm(tab[0], lo) + mm(tab[1], hi))


def iota(shape, dim):
    return lax.broadcasted_iota(jnp.int32, shape, dim)


def onehot(cond):
    return jnp.where(cond, 1.0, 0.0).astype(BF16)


def key(lane):
    r = lane & 127
    return jnp.where(r >= 80, 8, jnp.where(r >= 40, 4, 0)) + (lane & 3)


def gelu_parts(h):
    k = math.sqrt(2.0 / math.pi)
    hh = h * h
    t = jnp.tanh(k * (h + 0.044715 * (hh * h)))
    value = 0.5 * h * (1.0 + t)
    slope = 0.5 * (1.0 + t) + 0.5 * h * (1.0 - t * t) * (k * (1.0 + 3.0 * 0.044715 * hh))
    return value, slope


def kernel(
    G, D, f_ref, mix_ref, w_ref, tyf_ref, px_ref, pab_ref, selw_ref, e1_ref, e2_ref,
    cot_hbm, tyi_hbm, wxp_hbm, wxi_hbm,
    out_ref, sg_ref, mg_ref,
    cot, tyi, wxp, wxi, a3, mixed, mixpad, backb,
    sx1, rx1, sx3, rx3, sy1, ry1, sy3, ry3, sy2, ry2, sx2, rx2,
    ws, rw, wst, rq, bc, sspec, rspec, sgs, rgs, stt,
    mgx_s, mgx_r, mgy_s, mgy_r, part, rsbuf, agbuf, agsrc,
    lsem, bx_s, bx_r, by_s, by_r, dp_s, dp_r,
):
    rows = C * 4 * G
    planes = 4 * G
    gx = lax.axis_index("gx")
    gy = lax.axis_index("gy")
    dp = lax.axis_index("dp")
    tpr = max(1, -(-TILES // D))
    nred = TILES // tpr

    barrier = pltpu.get_barrier_semaphore()
    for k in range(1, G):
        pl.semaphore_signal(barrier, inc=1, device_id={"gx": lax.rem(gx + k, G)}, device_id_type=MESH)
    for k in range(1, GY):
        pl.semaphore_signal(barrier, inc=1, device_id={"gy": lax.rem(gy + k, GY)}, device_id_type=MESH)
    for k in range(1, D):
        pl.semaphore_signal(barrier, inc=1, device_id={"dp": lax.rem(dp + k, D)}, device_id_type=MESH)

    loads = [
        pltpu.make_async_copy(wxp_hbm.at[gy], wxp, lsem.at[0]),
        pltpu.make_async_copy(cot_hbm, cot, lsem.at[1]),
        pltpu.make_async_copy(tyi_hbm, tyi, lsem.at[2]),
        pltpu.make_async_copy(wxi_hbm.at[gy], wxi, lsem.at[3]),
    ]
    for copy in loads:
        copy.start()

    pending = []

    def exchange(axis, size, me, src_of, dst, sems_s, sems_r, ex):
        def one(k):
            peer = lax.rem(me + k, size)
            return pltpu.make_async_remote_copy(
                src_ref=src_of(peer),
                dst_ref=dst.at[me],
                send_sem=sems_s.at[ex, k],
                recv_sem=sems_r.at[ex, k],
                device_id={axis: peer},
                device_id_type=MESH,
            )

        copies = [one(k) for k in range(1, size)]
        for copy in copies:
            copy.start()
        pending.extend(copies)

        def wait():
            for copy in copies:
                copy.wait_recv()

        return wait

    def ex_x(src_of, dst, ex):
        return exchange("gx", G, gx, src_of, dst, bx_s, bx_r, ex)

    def ex_y(src_of, dst, ex):
        return exchange("gy", GY, gy, src_of, dst, by_s, by_r, ex)

    hrows = rows // 2
    chunk = 160 if hrows % 160 == 0 else hrows
    chunks = [[h * hrows + r for r in range(0, hrows, chunk)] for h in range(2)]
    starts = chunks[0] + chunks[1]
    n = chunk
    rest = jnp.zeros((8, 128), F32)

    def part_of(h, kk, r0):
        return pl.ds((h * 3 + kk) * hrows + r0 - h * hrows, n)

    def y_forward(data, h, r0):
        a = mm(data, tyf_ref[0]) + mm(data, tyf_ref[1])
        a3[part_of(h, 0, r0), :] = a
        a3[part_of(h, 1, r0), :] = pltpu.roll(a, 96, 1)
        a3[part_of(h, 2, r0), :] = pltpu.roll(a, 64, 1)

    def to_groups(h, dst):
        for g in range(G):
            block = a3[pl.ds(h * 3 * hrows + g, 120, stride=G), :]
            dst[h, g] = jnp.concatenate([block, rest], axis=0).T[:32]

    for h in range(2):
        for r0 in chunks[h]:
            y_forward(f_ref[r0 : r0 + n, :], h, r0)
        to_groups(h, sx1)
    pl.semaphore_wait(barrier, G - 1 + GY - 1 + D - 1)
    wait_x1 = [ex_x(lambda peer: sx1.at[h, peer], rx1.at[h], h) for h in range(2)]
    for h in range(2):
        rx1[h, gx] = sx1[h, gx]

    wst[...] = jnp.zeros_like(wst)
    for m in range(9):
        wst[m * 48 : m * 48 + 2 * C, 0:C] = w_ref[m].astype(F32).reshape(2 * C, C)
    ohd = onehot(iota((128, 640), 0) == (iota((128, 640), 1) & 31))
    wexp = mm(wst[...].astype(BF16), ohd)
    wparts = []
    for m in range(9):
        cond = (iota((48, 640), 0) >> 1) == (iota((48, 640), 1) >> 5)
        wparts.append(jnp.where(cond, wexp[m * 48 : m * 48 + 48], 0.0))
    wmasked = jnp.concatenate(wparts, axis=0).astype(BF16)
    ws[...] = mm(selw_ref[...], wmasked).astype(BF16)
    mixpad[...] = jnp.zeros_like(mixpad)
    mixpad[0:C, 0:C] = mix_ref[...].astype(F32)
    mixb = mixpad[...].astype(BF16)
    shift = int(math.log2(planes))
    ecol = onehot((iota((128, rows), 1) >> shift) == iota((128, rows), 0))
    for r0 in starts:
        erow = onehot(((iota((n, 128), 0) + r0) >> shift) == iota((n, 128), 1))
        kron = mm(mm_nt(erow, mixb).astype(BF16), ecol)
        diag = ((iota((n, rows), 0) + r0) & (planes - 1)) == (iota((n, rows), 1) & (planes - 1))
        kron = jnp.where(diag, kron, 0.0).astype(BF16)
        mixed[r0 : r0 + n, :] = mm(kron, f_ref[...])

    for q in range(5):
        lanes = iota((128, 512), 1)
        bc[q] = onehot(iota((128, 512), 0) == ((lanes >> 7) + 4 * q) * 4 + (lanes & 3))
    lanes = iota((128, 512), 1)
    ohr = onehot(iota((128, 512), 0) == (lanes >> 7) * 32 + ((lanes & 127) >> 2))

    def x_forward(recv, send, h):
        hi, lo = hilo(recv[h].reshape(32 * G, 128))
        p = mm(wxp[0], hi) + (mm(wxp[0], lo) + mm(wxp[1], hi))
        send[h] = p.reshape(GY, 6 * G, 128)

    def y_sum(recv):
        halves = [(recv[h, 0] + recv[h, 1]) + (recv[h, 2] + recv[h, 3]) for h in range(2)]
        return jnp.concatenate(halves, axis=1)

    loads[0].wait()
    wait_y1 = []
    for h in range(2):
        wait_x1[h]()
        x_forward(rx1, sy1, h)
        wait_y1.append(ex_y(lambda peer: sy1.at[h, peer], ry1.at[h], h))
        ry1[h, gy] = sy1[h, gy]
    wait_w = ex_x(lambda peer: ws, rw, 2)
    rw[gx] = ws[...]

    wait_w()
    rab = mm(pab_ref[...], rw[...].reshape(32 * G, 640)).astype(BF16)
    for q in range(5):
        rq[q] = mm(rab[:, q * 128 : (q + 1) * 128], ohr)

    for h in range(2):
        wait_y1[h]()
    shi, slo = hilo(y_sum(ry1))
    both = mm(px_ref[...], shi) + mm(px_ref[...], slo)
    sspec[...] = both[: 8 * G].reshape(G, 8, 256)

    low = iota((16 * G, 128), 1) < 40
    turn = lambda a, by: pltpu.roll(a, by % 128, 1) if by % 128 else a
    parts = []
    for kk in range(3):
        h0, h1 = turn(both[:, :128], -40 * kk), turn(both[:, 128:], 40 - 40 * kk)
        parts.append(jnp.where(low, h0, h1))
    stacked = jnp.concatenate(parts, axis=0)
    xhi, xlo = hilo(stacked)
    acc = jnp.zeros((48 * G, 128), F32)
    for q in range(5):
        spread = (mm(xhi, bc[q]) + mm(xlo, bc[q])) * rq[q]
        acc += (spread[:, :128] + spread[:, 128:256]) + (spread[:, 256:384] + spread[:, 384:])
    acc = acc.reshape(3, 2, 8 * G, 128)
    acc = acc[:, 0] + acc[:, 1]
    low = low[: 8 * G]
    wait_y2 = []
    for h in range(2):
        mine = [jnp.where(low if h == 0 else ~low, acc[kk], 0.0) for kk in range(3)]
        vals = sum(turn(mine[kk], 40 * kk - 40 * h) for kk in range(3))
        sy2[h] = vals.astype(BF16)
        wait_y2.append(ex_y(lambda peer: sy2.at[h], ry2.at[h], 2 + h))
        ry2[h, gy] = sy2[h]

    wait_spec = ex_x(lambda peer: sspec.at[peer], rspec, 3)
    rspec[gx] = sspec[gx]

    loads[3].wait()
    wait_x2 = []
    for h in range(2):
        wait_y2[h]()
        v = ry2[h].reshape(32 * G, 128)
        b = mm(wxi[0], v) + mm(wxi[1], v)
        sx2[h] = b.astype(BF16).reshape(G, 32, 128)
        wait_x2.append(ex_x(lambda peer: sx2.at[h, peer], rx2.at[h], 4 + h))
        rx2[h, gx] = sx2[h, gx]

    wait_spec()
    for tri in range(3):
        s0 = rspec[:, tri : tri + 1, :].reshape(G, 256)
        s1 = rspec[:, 4 + tri : 5 + tri, :].reshape(G, 256)
        block = jnp.concatenate([s0, s1, jnp.zeros((128 - 2 * G, 256), F32)], axis=0)
        stt[tri] = block.T

    loads[1].wait()
    loads[2].wait()
    wait_x3 = []
    for h in range(2):
        wait_x2[h]()
        for g in range(G):
            block = jnp.concatenate([rx2[h, g].astype(F32), jnp.zeros((96, 128), F32)], axis=0)
            a3[pl.ds(h * 3 * hrows + g, 120, stride=G), :] = block.T[:120]
        for r0 in chunks[h]:
            bb = a3[part_of(h, 0, r0), :]
            bb += pltpu.roll(a3[part_of(h, 1, r0), :], 32, 1)
            bb += pltpu.roll(a3[part_of(h, 2, r0), :], 64, 1)
            bb = bb.astype(BF16)
            pre = (mm(bb, tyi[0]) + mm(bb, tyi[1])) + mixed[r0 : r0 + n, :]
            value, slope = gelu_parts(pre)
            out_ref[r0 : r0 + n, :] = value.astype(BF16)
            back = (cot[r0 : r0 + n, :].astype(F32) * slope).astype(BF16)
            backb[r0 : r0 + n, :] = back
            y_forward(back, h, r0)
        to_groups(h, sx3)
        wait_x3.append(ex_x(lambda peer: sx3.at[h, peer], rx3.at[h], 6 + h))
        rx3[h, gx] = sx3[h, gx]

    gmix = jnp.zeros((24, 128), F32)
    ecol_t = onehot((iota((rows, 128), 0) >> shift) == iota((rows, 128), 1))
    for r0 in starts:
        full = mm_nt(f_ref[r0 : r0 + n, :], backb[...])
        diag = ((iota((n, rows), 0) + r0) & (planes - 1)) == (iota((n, rows), 1) & (planes - 1))
        hi, lo = hilo(jnp.where(diag, full, 0.0))
        cols = mm(hi, ecol_t) + mm(lo, ecol_t)
        erow_t = onehot(((iota((24, n), 1) + r0) >> shift) == iota((24, n), 0))
        hi, lo = hilo(cols)
        gmix += mm(erow_t, hi) + mm(erow_t, lo)
    mgx_s[...] = gmix
    wait_mgx = ex_x(lambda peer: mgx_s, mgx_r, 8)
    mgx_r[gx] = gmix

    wait_y3 = []
    for h in range(2):
        wait_x3[h]()
        x_forward(rx3, sy3, h)
        wait_y3.append(ex_y(lambda peer: sy3.at[h, peer], ry3.at[h], 4 + h))
        ry3[h, gy] = sy3[h, gy]

    wait_mgx()
    total = mgx_r[0]
    for k in range(1, G):
        total += mgx_r[k]
    mgy_s[...] = total
    wait_mgy = ex_y(lambda peer: mgy_s, mgy_r, 6)
    mgy_r[gy] = total

    for h in range(2):
        wait_y3[h]()
    ghi, glo = hilo(y_sum(ry3))
    half = px_ref[0 : 8 * G, :]
    sgs[...] = (mm(half, ghi) + mm(half, glo)).reshape(G, 8, 256)
    wait_gs = ex_x(lambda peer: sgs.at[peer], rgs, 9)
    rgs[gx] = sgs[gx]

    wait_mgy()
    mix_scale = 1.0 / math.sqrt(D * planes * 16 * G * NY)
    part[9:12] = (((mgy_r[0] + mgy_r[1]) + (mgy_r[2] + mgy_r[3])) * mix_scale).reshape(3, 8, 128)

    norm_in = 1.0 / math.sqrt(16 * G * NY)
    norm_out = 1.0 / math.sqrt(36 * G)
    spec_scale = norm_out / norm_in / math.sqrt(D * planes)
    wait_gs()
    gm = key(iota((256, 512), 0)) == key(iota((256, 512), 1) & 255)
    for tri in range(3):
        g0 = rgs[:, tri : tri + 1, :].reshape(G, 256)
        g1 = rgs[:, 4 + tri : 5 + tri, :].reshape(G, 256)
        top = jnp.concatenate([g0, g1], axis=1)
        bot = jnp.concatenate([g1, -g0], axis=1)
        gg = jnp.concatenate([top, bot, jnp.zeros((128 - 2 * G, 512), F32)], axis=0)
        ahi, alo = hilo(stt[tri])
        bhi, blo = hilo(gg)
        outer = (mm(ahi, bhi) + (mm(ahi, blo) + mm(alo, bhi)))
        outer = jnp.where(gm, outer, 0.0)
        ohi, olo = hilo(outer)
        fold = mm(e1_ref[...], ohi) + mm(e1_ref[...], olo)
        fhi, flo = hilo(fold)
        grad = (mm(fhi, e2_ref[...]) + mm(flo, e2_ref[...])) * spec_scale
        part[3 * tri : 3 * tri + 3] = grad.reshape(3, 8, 128)

    def rs_copy(k, to):
        return pltpu.make_async_remote_copy(
            src_ref=part.at[pl.ds(to * tpr, tpr)],
            dst_ref=rsbuf.at[dp],
            send_sem=dp_s.at[0, k],
            recv_sem=dp_r.at[0, k],
            device_id={"dp": to},
            device_id_type=MESH,
        )

    def ag_copy(k, to, slot):
        return pltpu.make_async_remote_copy(
            src_ref=agsrc,
            dst_ref=agbuf.at[slot],
            send_sem=dp_s.at[1, k],
            recv_sem=dp_r.at[1, k],
            device_id={"dp": to},
            device_id_type=MESH,
        )

    for k in range(1, D):
        to = lax.rem(dp + k, D)

        @pl.when(to < nred)
        def _():
            rs_copy(k, to).start()

    @pl.when(dp < nred)
    def _():
        rsbuf[dp] = part[pl.ds(dp * tpr, tpr)]
        for k in range(1, D):
            rs_copy(k, dp).wait_recv()
        tile = rsbuf[0]
        for k in range(1, D):
            tile += rsbuf[k]
        agsrc[...] = tile
        for k in range(1, D):
            ag_copy(k, lax.rem(dp + k, D), dp).start()
        agbuf[dp] = tile

    for k in range(1, D):
        frm = lax.rem(dp + D - k, D)

        @pl.when(frm < nred)
        def _():
            ag_copy(k, dp, frm).wait_recv()

    final = agbuf[...].reshape(TILES, 8, 128)
    mg_ref[...] = final[9:12].reshape(24, 128)[:C, :C]
    for tri in range(3):
        block = final[3 * tri : 3 * tri + 3].reshape(24, 128)
        for kk in range(3):
            for ri in range(2):
                off = ri * 60 + kk * 20
                sg_ref[tri * 3 + kk, :, ri, :] = block[:C, off : off + C]

    for copy in pending:
        copy.wait_send()
    for k in range(1, D):
        to = lax.rem(dp + k, D)

        @pl.when(to < nred)
        def _():
            rs_copy(k, to).wait_send()

    @pl.when(dp < nred)
    def _():
        for k in range(1, D):
            ag_copy(k, lax.rem(dp + k, D), dp).wait_send()


def local(G, D, fields, cotangent, mix_weight, spectral_weight):
    rows = C * 4 * G
    cells = XL * NY
    t = tables(G)
    tpr = max(1, -(-TILES // D))
    nred = TILES // tpr
    vm = pl.BlockSpec(memory_space=pltpu.VMEM)
    hbm = pl.BlockSpec(memory_space=pl.ANY)
    V = pltpu.VMEM
    scratch = [
        V((rows, cells), BF16),
        V((2, 128, cells), BF16),
        V((2, GY * 6 * G, 32 * G), BF16),
        V((2, 32 * G, GY * 8 * G), BF16),
        V((3 * rows, 128), F32),
        V((rows, cells), F32),
        V((128, 128), F32),
        V((rows, cells), BF16),
        V((2, G, 32, 128), F32),
        V((2, G, 32, 128), F32),
        V((2, G, 32, 128), F32),
        V((2, G, 32, 128), F32),
        V((2, GY, 6 * G, 128), F32),
        V((2, GY, 6 * G, 128), F32),
        V((2, GY, 6 * G, 128), F32),
        V((2, GY, 6 * G, 128), F32),
        V((2, 8 * G, 128), BF16),
        V((2, GY, 8 * G, 128), BF16),
        V((2, G, 32, 128), BF16),
        V((2, G, 32, 128), BF16),
        V((32, 640), BF16),
        V((G, 32, 640), BF16),
        V((432, 128), F32),
        V((5, 48 * G, 512), F32),
        V((5, 128, 512), BF16),
        V((G, 8, 256), F32),
        V((G, 8, 256), F32),
        V((G, 8, 256), F32),
        V((G, 8, 256), F32),
        V((3, 256, 128), F32),
        V((24, 128), F32),
        V((G, 24, 128), F32),
        V((24, 128), F32),
        V((GY, 24, 128), F32),
        V((TILES, 8, 128), F32),
        V((D, tpr, 8, 128), F32),
        V((nred, tpr, 8, 128), F32),
        V((tpr, 8, 128), F32),
        pltpu.SemaphoreType.DMA((4,)),
        pltpu.SemaphoreType.DMA((10, G)),
        pltpu.SemaphoreType.DMA((10, G)),
        pltpu.SemaphoreType.DMA((7, GY)),
        pltpu.SemaphoreType.DMA((7, GY)),
        pltpu.SemaphoreType.DMA((2, D)),
        pltpu.SemaphoreType.DMA((2, D)),
    ]
    out, sg, mg = pl.pallas_call(
        functools.partial(kernel, G, D),
        out_shape=(
            V((rows, cells), BF16),
            V((9, C, 2, C), F32),
            V((C, C), F32),
        ),
        in_specs=[vm] * 9 + [hbm] * 4,
        out_specs=(vm, vm, vm),
        scratch_shapes=scratch,
        compiler_params=pltpu.CompilerParams(
            collective_id=0, has_side_effects=True, vmem_limit_bytes=60 * 1024 * 1024
        ),
    )(
        fields.reshape(rows, cells),
        mix_weight,
        spectral_weight.transpose(0, 2, 1, 3),
        t["tyf"],
        t["px"],
        t["pab"],
        t["selw"],
        t["e1"],
        t["e2"],
        cotangent.reshape(rows, cells),
        t["tyi"],
        t["wxp"],
        t["wxi"],
    )
    return out.reshape(fields.shape), sg.transpose(0, 2, 1, 3), mg


def solution(mesh):
    G, D = mesh.shape["gx"], mesh.shape["dp"]
    cells = P("dp", None, None, ("gx", "gy"))
    modes = P(("gx", "gy"), None, None, None)
    return jax.shard_map(
        functools.partial(local, G, D),
        mesh=mesh,
        in_specs=(cells, cells, P(), modes),
        out_specs=(cells, modes, P()),
        check_vma=False,
    )
```

```python
import functools
import math

import jax
import jax.numpy as jnp
import numpy as np
from jax import lax
from jax.experimental import pallas as pl
from jax.experimental.pallas import tpu as pltpu
from jax.sharding import PartitionSpec as P

MESH = pl.DeviceIdType.MESH
F32 = jnp.float32
BF16 = jnp.bfloat16

C = 20
NY = 128
KY = 12
GY = 4
XL = 4
PL_OWN = 4
TILES = 12


def split(table):
    table = np.asarray(table, np.float32)
    hi = table.astype(BF16)
    lo = (table - hi.astype(np.float32)).astype(BF16)
    return np.stack([hi, lo])


@functools.lru_cache(None)
def tables(G):
    nx, kxn = 16 * G, 3 * G
    norm_in = 1.0 / math.sqrt(nx * NY)
    norm_out = 1.0 / math.sqrt(kxn * KY)
    y = np.arange(NY)
    tyf = np.zeros((XL * NY, 128))
    tyi = np.zeros((128, XL * NY))
    for kk in range(3):
        for ks in range(4):
            ang = 2 * np.pi * ((3 * ks + kk) * y % NY) / NY
            for x in range(XL):
                col = kk * 32 + ks * 8 + x * 2
                tyf[x * NY : (x + 1) * NY, col] = np.cos(ang) * norm_in
                tyf[x * NY : (x + 1) * NY, col + 1] = -np.sin(ang) * norm_in
                tyi[col, x * NY : (x + 1) * NY] = np.cos(ang)
                tyi[col + 1, x * NY : (x + 1) * NY] = -np.sin(ang)
    wxp = np.zeros((GY, GY * 6 * G, 32 * G))
    wxi = np.zeros((GY, 32 * G, GY * 8 * G))
    for gy in range(GY):
        for go in range(GY):
            for tri in range(3):
                jj, ks = divmod(3 * go + tri, 4)
                for gq in range(G):
                    j = 3 * gq + jj
                    kx = j if j < kxn // 2 else nx - kxn + j
                    rp = go * 6 * G + gq * 6 + tri * 2
                    ci = go * 8 * G + gq * 8 + tri
                    for gx in range(G):
                        for x in range(XL):
                            ang = 2 * np.pi * (kx * (4 * (gx * GY + gy) + x) % nx) / nx
                            c, s = np.cos(ang), np.sin(ang)
                            k = gx * 32 + ks * 8 + x * 2
                            wxp[gy, rp, k], wxp[gy, rp, k + 1] = c, s
                            wxp[gy, rp + 1, k], wxp[gy, rp + 1, k + 1] = -s, c
                            wxi[gy, k, ci], wxi[gy, k, ci + 4] = c * norm_out, -s * norm_out
                            wxi[gy, k + 1, ci], wxi[gy, k + 1, ci + 4] = s * norm_out, c * norm_out
    px = np.zeros((8 * G, 6 * G))
    pab = np.zeros((2, 3, 8 * G, 32 * G))
    for gq in range(G):
        for ri in range(2):
            for tri in range(3):
                row = gq * 8 + ri * 4 + tri
                px[row, gq * 6 + tri * 2 + ri] = 1
                for kk in range(3):
                    src = gq * 32 + kk * 8
                    pab[0, kk, row, src + tri] = 1
                    pab[1, kk, row, src + 4 + tri] = 1 if ri == 0 else -1
    selw = np.zeros((32, 18 * 24))
    for kk in range(3):
        for ri in range(2):
            for tri in range(3):
                q = (tri * 3 + kk) * 48 + ri
                selw[kk * 8 + ri * 4 + tri, q : q + 2 * C : 2] = 1
    b = lambda a: np.asarray(a, np.float32).astype(BF16)
    return dict(
        tyf=split(tyf),
        tyi=split(tyi),
        wxp=np.stack([split(w) for w in wxp]),
        wxi=np.stack([split(w) for w in wxi]),
        px=b(px),
        pab=b(pab.reshape(48 * G, 32 * G)),
        selw=b(selw),
    )


def mm(a, b):
    return jnp.dot(a, b, preferred_element_type=F32)


def mm_nt(a, b):
    return lax.dot_general(a, b, (((1,), (1,)), ((), ())), preferred_element_type=F32)


def hilo(a):
    hi = a.astype(BF16)
    return hi, (a - hi.astype(F32)).astype(BF16)


def mm_tab(tab, x):
    hi, lo = hilo(x)
    return mm(tab[0], hi) + (mm(tab[0], lo) + mm(tab[1], hi))


def iota(shape, dim):
    return lax.broadcasted_iota(jnp.int32, shape, dim)


def onehot(cond):
    return jnp.where(cond, 1.0, 0.0).astype(BF16)


def lane_code(shape, stride):
    row = iota(shape, 0)
    q = row & 127
    kk = jnp.where(q >= 80, 2, jnp.where(q >= 40, 1, 0))
    c = (row >> 7) * 10 + ((q - 40 * kk) >> 2)
    return jnp.where(q < 120, (kk * stride + c) * 4 + (q & 3), -1)


def gelu_parts(h):
    k = math.sqrt(2.0 / math.pi)
    hh = h * h
    t = jnp.tanh(k * (h + 0.044715 * (hh * h)))
    value = 0.5 * h * (1.0 + t)
    slope = 0.5 * (1.0 + t) + 0.5 * h * (1.0 - t * t) * (k * (1.0 + 3.0 * 0.044715 * hh))
    return value, slope


def kernel(
    G, D, f_hbm, tyf_hbm, w_hbm, mix_hbm, selw_hbm, wxp_hbm, pab_hbm, px_hbm, wxi_hbm, cot_hbm, tyi_hbm,
    out_ref, sg_ref, mg_ref,
    f_ref, tyf_ref, w_ref, mix_ref, selw_ref, wxp, pab_ref, px_ref, wxi, cot, tyi, a3, mixed, mixpad, backb,
    sx1, rx1, sx3, rx3, sy1, ry1, sy3, ry3, sy2, ry2, sx2, rx2,
    ws, rw, wst, rq, bc, ohg, gi, sspec, rspec, sgs, rgs, stt,
    mgx_s, mgx_r, mgy_s, mgy_r, part, rsbuf, agbuf, agsrc,
    lsem, bx_s, bx_r, by_s, by_r, dp_s, dp_r,
):
    rows = C * 4 * G
    planes = 4 * G
    gx = lax.axis_index("gx")
    gy = lax.axis_index("gy")
    dp = lax.axis_index("dp")
    tpr = max(1, -(-TILES // D))
    nred = TILES // tpr

    hrows = rows // 2
    chunk = 160 if hrows % 160 == 0 else hrows
    chunks = [[h * hrows + r for r in range(0, hrows, chunk)] for h in range(2)]
    starts = chunks[0] + chunks[1]
    n = chunk
    barrier = pltpu.get_barrier_semaphore()
    for k in range(1, G):
        pl.semaphore_signal(barrier, inc=1, device_id={"gx": lax.rem(gx + k, G)}, device_id_type=MESH)
    for k in range(1, GY):
        pl.semaphore_signal(barrier, inc=1, device_id={"gy": lax.rem(gy + k, GY)}, device_id_type=MESH)
    for k in range(1, D):
        pl.semaphore_signal(barrier, inc=1, device_id={"dp": lax.rem(dp + k, D)}, device_id_type=MESH)

    pieces = [(f_hbm.at[pl.ds(r0, n)], f_ref.at[pl.ds(r0, n)]) for r0 in starts]
    pieces.insert(0, (tyf_hbm, tyf_ref))
    pieces += [(w_hbm, w_ref), (selw_hbm, selw_ref), (mix_hbm, mix_ref), (wxp_hbm.at[gy], wxp)]
    pieces += [(pab_hbm, pab_ref), (px_hbm, px_ref), (wxi_hbm.at[gy], wxi), (cot_hbm, cot), (tyi_hbm, tyi)]
    loads = [pltpu.make_async_copy(src, dst, lsem.at[k]) for k, (src, dst) in enumerate(pieces)]
    for copy in loads:
        copy.start()
    late = dict(zip(("w", "selw", "mix", "wxp", "pab", "px", "wxi", "cot", "tyi"), loads[1 + len(starts) :]))

    pending = []

    def exchange(axis, size, me, src_of, dst, sems_s, sems_r, ex):
        def one(k):
            peer = lax.rem(me + k, size)
            return pltpu.make_async_remote_copy(
                src_ref=src_of(peer),
                dst_ref=dst.at[me],
                send_sem=sems_s.at[ex, k],
                recv_sem=sems_r.at[ex, k],
                device_id={axis: peer},
                device_id_type=MESH,
            )

        copies = [one(k) for k in range(1, size)]
        for copy in copies:
            copy.start()
        pending.extend(copies)

        def wait():
            for copy in copies:
                copy.wait_recv()

        return wait

    def ex_x(src_of, dst, ex):
        return exchange("gx", G, gx, src_of, dst, bx_s, bx_r, ex)

    def ex_y(src_of, dst, ex):
        return exchange("gy", GY, gy, src_of, dst, by_s, by_r, ex)

    rest = jnp.zeros((8, 128), F32)

    def part_of(h, kk, r0):
        return pl.ds((h * 3 + kk) * hrows + r0 - h * hrows, n)

    def y_forward(data, h, r0):
        a = mm(data, tyf_ref[0]) + mm(data, tyf_ref[1])
        a3[part_of(h, 0, r0), :] = a
        a3[part_of(h, 1, r0), :] = pltpu.roll(a, 96, 1)
        a3[part_of(h, 2, r0), :] = pltpu.roll(a, 64, 1)

    def to_groups(h, dst):
        for g in range(G):
            block = a3[pl.ds(h * 3 * hrows + g, 120, stride=G), :]
            dst[h, g] = jnp.concatenate([block, rest], axis=0).T[:32]

    def to_planes(value):
        for i in range(4):
            gi[i] = value[:, i * 128 : (i + 1) * 128]

    loads[0].wait()
    for h in range(2):
        for r0 in chunks[h]:
            loads[1 + starts.index(r0)].wait()
            y_forward(f_ref[r0 : r0 + n, :], h, r0)
        to_groups(h, sx1)
    pl.semaphore_wait(barrier, G - 1 + GY - 1 + D - 1)
    wait_x1 = [ex_x(lambda peer: sx1.at[h, peer], rx1.at[h], h) for h in range(2)]
    for h in range(2):
        rx1[h, gx] = sx1[h, gx]

    late["w"].wait()
    late["selw"].wait()
    wst[...] = jnp.zeros_like(wst)
    for m in range(9):
        wst[m * 48 : m * 48 + 2 * C, 0:C] = w_ref[m].astype(F32).reshape(2 * C, C)
    ohd = onehot(iota((128, 640), 0) == (iota((128, 640), 1) & 31))
    wexp = mm(wst[...].astype(BF16), ohd)
    wparts = []
    for m in range(9):
        cond = (iota((48, 640), 0) >> 1) == (iota((48, 640), 1) >> 5)
        wparts.append(jnp.where(cond, wexp[m * 48 : m * 48 + 48], 0.0))
    wmasked = jnp.concatenate(wparts, axis=0).astype(BF16)
    ws[...] = mm(selw_ref[...], wmasked).astype(BF16)
    late["mix"].wait()
    mixpad[...] = jnp.zeros_like(mixpad)
    mixpad[0:C, 0:C] = mix_ref[...].astype(F32)
    mixb = mixpad[...].astype(BF16)
    shift = int(math.log2(planes))
    ecol = onehot((iota((128, rows), 1) >> shift) == iota((128, rows), 0))
    for r0 in starts:
        erow = onehot(((iota((n, 128), 0) + r0) >> shift) == iota((n, 128), 1))
        kron = mm(mm_nt(erow, mixb).astype(BF16), ecol)
        diag = ((iota((n, rows), 0) + r0) & (planes - 1)) == (iota((n, rows), 1) & (planes - 1))
        kron = jnp.where(diag, kron, 0.0).astype(BF16)
        mixed[r0 : r0 + n, :] = mm(kron, f_ref[...])

    for q in range(5):
        lanes = iota((128, 512), 1)
        bc[q] = onehot(iota((128, 512), 0) == ((lanes >> 7) + 4 * q) * 4 + (lanes & 3))
    lanes = iota((128, 512), 1)
    ohr = onehot(iota((128, 512), 0) == (lanes >> 7) * 32 + ((lanes & 127) >> 2))
    col = iota((256, 512), 1)
    ohg[0] = onehot(lane_code((256, 512), 24) == (col & 127) * 4 + (col >> 7))
    ohg[1] = onehot(lane_code((256, 512), 20) == (col & 63) * 4 + (col >> 7))

    def x_forward(recv, send, h):
        hi, lo = hilo(recv[h].reshape(32 * G, 128))
        p = mm(wxp[0], hi) + (mm(wxp[0], lo) + mm(wxp[1], hi))
        send[h] = p.astype(send.dtype).reshape(GY, 6 * G, 128)

    def y_sum(recv):
        halves = []
        for h in range(2):
            p = [recv[h, k].astype(F32) for k in range(GY)]
            halves.append((p[0] + p[1]) + (p[2] + p[3]))
        return jnp.concatenate(halves, axis=1)

    late["wxp"].wait()
    wait_y1 = []
    for h in range(2):
        wait_x1[h]()
        x_forward(rx1, sy1, h)
        wait_y1.append(ex_y(lambda peer: sy1.at[h, peer], ry1.at[h], h))
        ry1[h, gy] = sy1[h, gy]
    wait_w = ex_x(lambda peer: ws, rw, 2)
    rw[gx] = ws[...]

    wait_w()
    late["pab"].wait()
    rab = mm(pab_ref[...], rw[...].reshape(32 * G, 640)).astype(BF16)
    for q in range(5):
        rq[q] = mm(rab[:, q * 128 : (q + 1) * 128], ohr)
    late["px"].wait()

    for h in range(2):
        wait_y1[h]()
    shi, slo = hilo(y_sum(ry1))
    spec = mm(px_ref[...], shi) + mm(px_ref[...], slo)
    sspec[...] = spec.reshape(G, 8, 256)

    low = iota((8 * G, 128), 1) < 40
    turn = lambda a, by: pltpu.roll(a, by % 128, 1) if by % 128 else a
    parts = []
    for kk in range(3):
        h0, h1 = turn(spec[:, :128], -40 * kk), turn(spec[:, 128:], 40 - 40 * kk)
        parts.append(jnp.where(low, h0, h1))
    xhi, xlo = hilo(jnp.concatenate(parts, axis=0))
    acc = [jnp.zeros((24 * G, 128), F32) for _ in range(2)]
    for q in range(5):
        spread = mm(xhi, bc[q]) + mm(xlo, bc[q])
        for ab in range(2):
            prod = spread * rq[q, ab * 24 * G : (ab + 1) * 24 * G]
            acc[ab] += (prod[:, :128] + prod[:, 128:256]) + (prod[:, 256:384] + prod[:, 384:])
    swapped = pltpu.roll(acc[1].reshape(3 * G, 8, 128), 4, 1).reshape(24 * G, 128)
    acc = (acc[0] + swapped).reshape(3, 8 * G, 128)
    wait_y2 = []
    for h in range(2):
        mine = [jnp.where(low if h == 0 else ~low, acc[kk], 0.0) for kk in range(3)]
        vals = sum(turn(mine[kk], 40 * kk - 40 * h) for kk in range(3))
        sy2[h] = vals.astype(BF16)
        wait_y2.append(ex_y(lambda peer: sy2.at[h], ry2.at[h], 2 + h))
        ry2[h, gy] = sy2[h]

    wait_spec = ex_x(lambda peer: sspec.at[peer], rspec, 3)
    rspec[gx] = sspec[gx]

    late["wxi"].wait()
    wait_x2 = []
    for h in range(2):
        wait_y2[h]()
        v = ry2[h].reshape(32 * G, 128)
        b = mm(wxi[0], v) + mm(wxi[1], v)
        sx2[h] = b.astype(BF16).reshape(G, 32, 128)
        wait_x2.append(ex_x(lambda peer: sx2.at[h, peer], rx2.at[h], 4 + h))
        rx2[h, gx] = sx2[h, gx]

    wait_spec()
    hi, lo = hilo(rspec[...].reshape(8 * G, 256))
    to_planes(mm(hi, ohg[0]) + mm(lo, ohg[0]))
    for tri in range(3):
        block = []
        for i in range(4):
            for ri in range(2):
                block.append(gi[i, pl.ds(ri * 4 + tri, G, stride=8), :])
        block.append(jnp.zeros((128 - 8 * G, 128), F32))
        stt[tri] = jnp.concatenate(block, axis=0).T[:72]

    late["cot"].wait()
    late["tyi"].wait()
    wait_x3 = []
    for h in range(2):
        wait_x2[h]()
        for g in range(G):
            block = jnp.concatenate([rx2[h, g].astype(F32), jnp.zeros((96, 128), F32)], axis=0)
            a3[pl.ds(h * 3 * hrows + g, 120, stride=G), :] = block.T[:120]
        for r0 in chunks[h]:
            bb = a3[part_of(h, 0, r0), :]
            bb += pltpu.roll(a3[part_of(h, 1, r0), :], 32, 1)
            bb += pltpu.roll(a3[part_of(h, 2, r0), :], 64, 1)
            bb = bb.astype(BF16)
            pre = (mm(bb, tyi[0]) + mm(bb, tyi[1])) + mixed[r0 : r0 + n, :]
            value, slope = gelu_parts(pre)
            out_ref[r0 : r0 + n, :] = value.astype(BF16)
            back = (cot[r0 : r0 + n, :].astype(F32) * slope).astype(BF16)
            backb[r0 : r0 + n, :] = back
            y_forward(back, h, r0)
        to_groups(h, sx3)
        wait_x3.append(ex_x(lambda peer: sx3.at[h, peer], rx3.at[h], 6 + h))
        rx3[h, gx] = sx3[h, gx]

    gmix = jnp.zeros((24, 128), F32)
    ecol_t = onehot((iota((rows, 128), 0) >> shift) == iota((rows, 128), 1))
    for r0 in starts:
        full = mm_nt(f_ref[r0 : r0 + n, :], backb[...])
        diag = ((iota((n, rows), 0) + r0) & (planes - 1)) == (iota((n, rows), 1) & (planes - 1))
        hi, lo = hilo(jnp.where(diag, full, 0.0))
        cols = mm(hi, ecol_t) + mm(lo, ecol_t)
        erow_t = onehot(((iota((24, n), 1) + r0) >> shift) == iota((24, n), 0))
        hi, lo = hilo(cols)
        gmix += mm(erow_t, hi) + mm(erow_t, lo)
    mgx_s[...] = gmix
    mgx_r[gx] = gmix

    wait_y3 = []
    for h in range(2):
        wait_x3[h]()
        x_forward(rx3, sy3, h)
        wait_y3.append(ex_y(lambda peer: sy3.at[h, peer], ry3.at[h], 4 + h))
        ry3[h, gy] = sy3[h, gy]

    wait_mgx = ex_x(lambda peer: mgx_s, mgx_r, 8)
    wait_mgx()
    total = mgx_r[0]
    for k in range(1, G):
        total += mgx_r[k]
    mgy_s[...] = total
    wait_mgy = ex_y(lambda peer: mgy_s, mgy_r, 6)
    mgy_r[gy] = total

    for h in range(2):
        wait_y3[h]()
    ghi, glo = hilo(y_sum(ry3))
    sgs[...] = (mm(px_ref[...], ghi) + mm(px_ref[...], glo)).reshape(G, 8, 256)
    wait_gs = ex_x(lambda peer: sgs.at[peer], rgs, 9)
    rgs[gx] = sgs[gx]

    wait_mgy()
    mix_scale = 1.0 / math.sqrt(D * planes * 16 * G * NY)
    part[9:12] = (((mgy_r[0] + mgy_r[1]) + (mgy_r[2] + mgy_r[3])) * mix_scale).reshape(3, 8, 128)

    norm_in = 1.0 / math.sqrt(16 * G * NY)
    norm_out = 1.0 / math.sqrt(36 * G)
    spec_scale = norm_out / norm_in / math.sqrt(D * planes)
    wait_gs()
    hi, lo = hilo(rgs[...].reshape(8 * G, 256))
    to_planes(mm(hi, ohg[1]) + mm(lo, ohg[1]))
    lane = iota((G, 128), 1)
    lane24 = iota((24, 128), 1) & 63
    for tri in range(3):
        block = []
        for i in range(4):
            g0 = gi[i, pl.ds(tri, G, stride=8), :]
            g1 = gi[i, pl.ds(4 + tri, G, stride=8), :]
            block += [jnp.where(lane < 64, g0, g1), jnp.where(lane < 64, g1, -g0)]
        block.append(jnp.zeros((128 - 8 * G, 128), F32))
        ahi, alo = hilo(stt[tri])
        bhi, blo = hilo(jnp.concatenate(block, axis=0))
        outer = mm(ahi, bhi) + (mm(ahi, blo) + mm(alo, bhi))
        grad = jnp.zeros((24, 128), F32)
        for kk in range(3):
            mine = (lane24 >= 20 * kk) & (lane24 < 20 * kk + 20)
            grad += jnp.where(mine, outer[24 * kk : 24 * kk + 24], 0.0)
        part[3 * tri : 3 * tri + 3] = (grad * spec_scale).reshape(3, 8, 128)

    def rs_copy(k, to):
        return pltpu.make_async_remote_copy(
            src_ref=part.at[pl.ds(to * tpr, tpr)],
            dst_ref=rsbuf.at[dp],
            send_sem=dp_s.at[0, k],
            recv_sem=dp_r.at[0, k],
            device_id={"dp": to},
            device_id_type=MESH,
        )

    def ag_copy(k, to, slot):
        return pltpu.make_async_remote_copy(
            src_ref=agsrc,
            dst_ref=agbuf.at[slot],
            send_sem=dp_s.at[1, k],
            recv_sem=dp_r.at[1, k],
            device_id={"dp": to},
            device_id_type=MESH,
        )

    for k in range(1, D):
        to = lax.rem(dp + k, D)

        @pl.when(to < nred)
        def _():
            rs_copy(k, to).start()

    @pl.when(dp < nred)
    def _():
        rsbuf[dp] = part[pl.ds(dp * tpr, tpr)]
        for k in range(1, D):
            rs_copy(k, dp).wait_recv()
        tile = rsbuf[0]
        for k in range(1, D):
            tile += rsbuf[k]
        agsrc[...] = tile
        for k in range(1, D):
            ag_copy(k, lax.rem(dp + k, D), dp).start()
        agbuf[dp] = tile

    for k in range(1, D):
        frm = lax.rem(dp + D - k, D)

        @pl.when(frm < nred)
        def _():
            ag_copy(k, dp, frm).wait_recv()

    final = agbuf[...].reshape(TILES, 8, 128)
    mg_ref[...] = final[9:12].reshape(24, 128)[:C, :C]
    for tri in range(3):
        block = final[3 * tri : 3 * tri + 3].reshape(24, 128)
        for kk in range(3):
            for ri in range(2):
                off = ri * 64 + kk * 20
                sg_ref[tri * 3 + kk, :, ri, :] = block[:C, off : off + C]

    for copy in pending:
        copy.wait_send()
    for k in range(1, D):
        to = lax.rem(dp + k, D)

        @pl.when(to < nred)
        def _():
            rs_copy(k, to).wait_send()

    @pl.when(dp < nred)
    def _():
        for k in range(1, D):
            ag_copy(k, lax.rem(dp + k, D), dp).wait_send()


def store_kernel(out, sg, mg, out_hbm, sg_hbm, mg_hbm, sems):
    pairs = ((out, out_hbm), (sg, sg_hbm), (mg, mg_hbm))
    copies = [pltpu.make_async_copy(src, dst, sems.at[k]) for k, (src, dst) in enumerate(pairs)]
    for copy in copies:
        copy.start()
    for copy in copies:
        copy.wait()


def local(G, D, fields, cotangent, mix_weight, spectral_weight):
    rows = C * 4 * G
    cells = XL * NY
    t = tables(G)
    tpr = max(1, -(-TILES // D))
    nred = TILES // tpr
    vm = pl.BlockSpec(memory_space=pltpu.VMEM)
    hbm = pl.BlockSpec(memory_space=pl.ANY)
    V = pltpu.VMEM
    scratch = [
        V((rows, cells), BF16),
        V((2, cells, 128), BF16),
        V((9, C, 2, C), BF16),
        V((C, C), BF16),
        V((32, 432), BF16),
        V((2, GY * 6 * G, 32 * G), BF16),
        V((48 * G, 32 * G), BF16),
        V((8 * G, 6 * G), BF16),
        V((2, 32 * G, GY * 8 * G), BF16),
        V((rows, cells), BF16),
        V((2, 128, cells), BF16),
        V((3 * rows, 128), F32),
        V((rows, cells), F32),
        V((128, 128), F32),
        V((rows, cells), BF16),
        V((2, G, 32, 128), F32),
        V((2, G, 32, 128), F32),
        V((2, G, 32, 128), F32),
        V((2, G, 32, 128), F32),
        V((2, GY, 6 * G, 128), F32),
        V((2, GY, 6 * G, 128), F32),
        V((2, GY, 6 * G, 128), BF16),
        V((2, GY, 6 * G, 128), BF16),
        V((2, 8 * G, 128), BF16),
        V((2, GY, 8 * G, 128), BF16),
        V((2, G, 32, 128), BF16),
        V((2, G, 32, 128), BF16),
        V((32, 640), BF16),
        V((G, 32, 640), BF16),
        V((432, 128), F32),
        V((5, 48 * G, 512), F32),
        V((5, 128, 512), BF16),
        V((2, 256, 512), BF16),
        V((4, 8 * G, 128), F32),
        V((G, 8, 256), F32),
        V((G, 8, 256), F32),
        V((G, 8, 256), F32),
        V((G, 8, 256), F32),
        V((3, 72, 128), F32),
        V((24, 128), F32),
        V((G, 24, 128), F32),
        V((24, 128), F32),
        V((GY, 24, 128), F32),
        V((TILES, 8, 128), F32),
        V((D, tpr, 8, 128), F32),
        V((nred, tpr, 8, 128), F32),
        V((tpr, 8, 128), F32),
        pltpu.SemaphoreType.DMA((18,)),
        pltpu.SemaphoreType.DMA((10, G)),
        pltpu.SemaphoreType.DMA((10, G)),
        pltpu.SemaphoreType.DMA((7, GY)),
        pltpu.SemaphoreType.DMA((7, GY)),
        pltpu.SemaphoreType.DMA((2, D)),
        pltpu.SemaphoreType.DMA((2, D)),
    ]
    out, sg, mg = pl.pallas_call(
        functools.partial(kernel, G, D),
        out_shape=(
            V((rows, cells), BF16),
            V((9, C, 2, C), F32),
            V((C, C), F32),
        ),
        in_specs=[hbm] * 11,
        out_specs=(vm, vm, vm),
        scratch_shapes=scratch,
        compiler_params=pltpu.CompilerParams(
            collective_id=0, has_side_effects=True, vmem_limit_bytes=60 * 1024 * 1024
        ),
    )(
        fields.reshape(rows, cells),
        t["tyf"],
        spectral_weight.transpose(0, 2, 1, 3),
        mix_weight,
        t["selw"],
        t["wxp"],
        t["pab"],
        t["px"],
        t["wxi"],
        cotangent.reshape(rows, cells),
        t["tyi"],
    )
    out, sg, mg = pl.pallas_call(
        store_kernel,
        out_shape=tuple(jax.ShapeDtypeStruct(a.shape, a.dtype) for a in (out, sg, mg)),
        in_specs=[hbm] * 3,
        out_specs=(hbm,) * 3,
        scratch_shapes=[pltpu.SemaphoreType.DMA((3,))],
        compiler_params=pltpu.CompilerParams(vmem_limit_bytes=1 << 20),
    )(out, sg, mg)
    return out.reshape(fields.shape), sg.transpose(0, 2, 1, 3), mg


def solution(mesh):
    G, D = mesh.shape["gx"], mesh.shape["dp"]
    cells = P("dp", None, None, ("gx", "gy"))
    modes = P(("gx", "gy"), None, None, None)
    return jax.shard_map(
        functools.partial(local, G, D),
        mesh=mesh,
        in_specs=(cells, cells, P(), modes),
        out_specs=(cells, modes, P()),
        check_vma=False,
    )
```

```python
import functools
import math

import jax
import jax.numpy as jnp
import numpy as np
from jax import lax
from jax.experimental import pallas as pl
from jax.experimental.pallas import tpu as pltpu
from jax.sharding import PartitionSpec as P

MESH = pl.DeviceIdType.MESH
F32 = jnp.float32
BF16 = jnp.bfloat16

C = 20
NY = 128
KY = 12
GY = 4
XL = 4
PL_OWN = 4
TILES = 12


def split(table):
    table = np.asarray(table, np.float32)
    hi = table.astype(BF16)
    lo = (table - hi.astype(np.float32)).astype(BF16)
    return np.stack([hi, lo])


@functools.lru_cache(None)
def tables(G):
    nx, kxn = 16 * G, 3 * G
    norm_in = 1.0 / math.sqrt(nx * NY)
    norm_out = 1.0 / math.sqrt(kxn * KY)
    y = np.arange(NY)
    tyf = np.zeros((XL * NY, 128))
    tyi = np.zeros((128, XL * NY))
    for kk in range(3):
        for ks in range(4):
            ang = 2 * np.pi * ((3 * ks + kk) * y % NY) / NY
            for x in range(XL):
                col = kk * 32 + ks * 8 + x * 2
                tyf[x * NY : (x + 1) * NY, col] = np.cos(ang) * norm_in
                tyf[x * NY : (x + 1) * NY, col + 1] = -np.sin(ang) * norm_in
                tyi[col, x * NY : (x + 1) * NY] = np.cos(ang)
                tyi[col + 1, x * NY : (x + 1) * NY] = -np.sin(ang)
    wxp = np.zeros((GY, GY * 6 * G, 32 * G))
    wxi = np.zeros((GY, 32 * G, GY * 8 * G))
    for gy in range(GY):
        for go in range(GY):
            for tri in range(3):
                jj, ks = divmod(3 * go + tri, 4)
                for gq in range(G):
                    j = 3 * gq + jj
                    kx = j if j < kxn // 2 else nx - kxn + j
                    rp = go * 6 * G + gq * 6 + tri * 2
                    ci = go * 8 * G + gq * 8 + tri
                    for gx in range(G):
                        for x in range(XL):
                            ang = 2 * np.pi * (kx * (4 * (gx * GY + gy) + x) % nx) / nx
                            c, s = np.cos(ang), np.sin(ang)
                            k = gx * 32 + ks * 8 + x * 2
                            wxp[gy, rp, k], wxp[gy, rp, k + 1] = c, s
                            wxp[gy, rp + 1, k], wxp[gy, rp + 1, k + 1] = -s, c
                            wxi[gy, k, ci], wxi[gy, k, ci + 4] = c * norm_out, -s * norm_out
                            wxi[gy, k + 1, ci], wxi[gy, k + 1, ci + 4] = s * norm_out, c * norm_out
    px = np.zeros((8 * G, 6 * G))
    pab = np.zeros((2, 3, 8 * G, 32 * G))
    for gq in range(G):
        for ri in range(2):
            for tri in range(3):
                row = gq * 8 + ri * 4 + tri
                px[row, gq * 6 + tri * 2 + ri] = 1
                for kk in range(3):
                    src = gq * 32 + kk * 8
                    pab[0, kk, row, src + tri] = 1
                    pab[1, kk, row, src + 4 + tri] = 1 if ri == 0 else -1
    selw = np.zeros((32, 18 * 24))
    for kk in range(3):
        for ri in range(2):
            for tri in range(3):
                q = (tri * 3 + kk) * 48 + ri
                selw[kk * 8 + ri * 4 + tri, q : q + 2 * C : 2] = 1
    b = lambda a: np.asarray(a, np.float32).astype(BF16)
    return dict(
        tyf=np.concatenate(split(tyf)),
        tyi=np.concatenate(split(tyi)),
        wxp=np.stack([split(w) for w in wxp]),
        wxi=np.stack([split(w) for w in wxi]),
        px=b(px),
        pab=b(pab.reshape(48 * G, 32 * G)),
        selw=b(selw),
    )


def mm(a, b):
    return jnp.dot(a, b, preferred_element_type=F32)


def mm_nt(a, b):
    return lax.dot_general(a, b, (((1,), (1,)), ((), ())), preferred_element_type=F32)


def hilo(a):
    hi = a.astype(BF16)
    return hi, (a - hi.astype(F32)).astype(BF16)


def mm_tab(tab, x):
    hi, lo = hilo(x)
    return mm(tab[0], hi) + (mm(tab[0], lo) + mm(tab[1], hi))


def iota(shape, dim):
    return lax.broadcasted_iota(jnp.int32, shape, dim)


def onehot(cond):
    return jnp.where(cond, 1.0, 0.0).astype(BF16)


def lane_code(shape, stride):
    row = iota(shape, 0)
    q = row & 127
    kk = jnp.where(q >= 80, 2, jnp.where(q >= 40, 1, 0))
    c = (row >> 7) * 10 + ((q - 40 * kk) >> 2)
    return jnp.where(q < 120, (kk * stride + c) * 4 + (q & 3), -1)


def gelu_parts(h):
    k = math.sqrt(2.0 / math.pi)
    hh = h * h
    u = 0.5 * jnp.tanh(h * (k + (0.044715 * k) * hh)) + 0.5
    value = h * u
    slope = u + (value * (1.0 - u)) * (2.0 * k + (6.0 * 0.044715 * k) * hh)
    return value, slope


def kernel(
    G, D, f_hbm, tyf_hbm, w_hbm, mix_hbm, selw_hbm, wxp_hbm, pab_hbm, px_hbm, wxi_hbm, cot_hbm, tyi_hbm,
    out_ref, sg_ref, mg_ref,
    f_ref, tyf_ref, w_ref, mix_ref, selw_ref, wxp, pab_ref, px_ref, wxi, cot, tyi, a3, mixed, mixpad, backb,
    sx1, rx1, sx3, rx3, sy1, ry1, sy3, ry3, sy2, ry2, sx2, rx2,
    ws, rw, wst, rq, bc, ohg, gi, sspec, rspec, sgs, rgs, stt,
    mgx_s, mgx_r, mgy_s, mgy_r, part, rsbuf, agbuf, agsrc,
    ready, go, lsem, bx_s, bx_r, by_s, by_r, dp_s, dp_r,
):
    rows = C * 4 * G
    planes = 4 * G
    gx = lax.axis_index("gx")
    gy = lax.axis_index("gy")
    dp = lax.axis_index("dp")
    tpr = max(1, -(-TILES // D))
    nred = TILES // tpr

    hrows = rows // 2
    chunk = 160 if hrows % 160 == 0 else hrows
    chunks = [[h * hrows + r for r in range(0, hrows, chunk)] for h in range(2)]
    starts = chunks[0] + chunks[1]
    n = chunk
    barrier = pltpu.get_barrier_semaphore()
    for k in range(1, G):
        pl.semaphore_signal(barrier, inc=1, device_id={"gx": lax.rem(gx + k, G)}, device_id_type=MESH)
    for k in range(1, GY):
        pl.semaphore_signal(barrier, inc=1, device_id={"gy": lax.rem(gy + k, GY)}, device_id_type=MESH)

    @pl.when(dp == 0)
    def _():
        for k in range(1, D):
            pl.semaphore_signal(barrier, inc=1, device_id={"dp": k}, device_id_type=MESH)


    pieces = [(f_hbm.at[pl.ds(r0, n)], f_ref.at[pl.ds(r0, n)]) for r0 in starts]
    pieces.insert(0, (tyf_hbm, tyf_ref))
    pieces += [(w_hbm, w_ref), (selw_hbm, selw_ref), (mix_hbm, mix_ref), (wxp_hbm.at[gy], wxp)]
    pieces += [(pab_hbm, pab_ref), (px_hbm, px_ref), (wxi_hbm.at[gy], wxi), (cot_hbm, cot), (tyi_hbm, tyi)]
    loads = [pltpu.make_async_copy(src, dst, lsem.at[k]) for k, (src, dst) in enumerate(pieces)]
    for copy in loads:
        copy.start()
    late = dict(zip(("w", "selw", "mix", "wxp", "pab", "px", "wxi", "cot", "tyi"), loads[1 + len(starts) :]))

    pending = []

    def exchange(axis, size, me, src_of, dst, sems_s, sems_r, ex):
        def one(k):
            peer = lax.rem(me + k, size)
            return pltpu.make_async_remote_copy(
                src_ref=src_of(peer),
                dst_ref=dst.at[me],
                send_sem=sems_s.at[ex, k],
                recv_sem=sems_r.at[ex, k],
                device_id={axis: peer},
                device_id_type=MESH,
            )

        copies = [one(k) for k in range(1, size)]
        for copy in copies:
            copy.start()
        pending.extend(copies)

        def wait():
            for copy in copies:
                copy.wait_recv()

        return wait

    def ex_x(src_of, dst, ex):
        return exchange("gx", G, gx, src_of, dst, bx_s, bx_r, ex)

    def ex_y(src_of, dst, ex):
        return exchange("gy", GY, gy, src_of, dst, by_s, by_r, ex)

    rest = jnp.zeros((8, 128), F32)

    def part_of(h, kk, r0):
        return pl.ds((h * 3 + kk) * hrows + r0 - h * hrows, n)

    def y_forward(data, h, r0):
        a = mm(jnp.concatenate([data, data], axis=1), tyf_ref[...])
        a3[part_of(h, 0, r0), :] = a
        a3[part_of(h, 1, r0), :] = pltpu.roll(a, 96, 1)
        a3[part_of(h, 2, r0), :] = pltpu.roll(a, 64, 1)

    def to_groups(h, dst):
        for g in range(G):
            block = a3[pl.ds(h * 3 * hrows + g, 120, stride=G), :]
            dst[h, g] = jnp.concatenate([block, rest], axis=0).T[:32]

    def to_planes(value):
        for i in range(4):
            gi[i] = value[:, i * 128 : (i + 1) * 128]

    loads[0].wait()
    wait_x1 = []
    for h in range(2):
        for r0 in chunks[h]:
            loads[1 + starts.index(r0)].wait()
            y_forward(f_ref[r0 : r0 + n, :], h, r0)
        to_groups(h, sx1)
        if h == 0:


            @pl.when(dp == 0)
            def _():
                pl.semaphore_wait(barrier, G - 1 + GY - 1)

            @pl.when(dp != 0)
            def _():
                pl.semaphore_wait(barrier, G - 1 + GY - 1 + 1)
                pl.semaphore_signal(ready, inc=1, device_id={"dp": 0}, device_id_type=MESH)

        wait_x1.append(ex_x(lambda peer: sx1.at[h, peer], rx1.at[h], h))
        rx1[h, gx] = sx1[h, gx]

    late["w"].wait()
    late["selw"].wait()
    wst[...] = jnp.zeros_like(wst)
    for m in range(9):
        wst[m * 48 : m * 48 + 2 * C, 0:C] = w_ref[m].astype(F32).reshape(2 * C, C)
    r = iota((128, 512), 1) & 127
    fifth = lambda r: sum(jnp.where(r >= 20 * k, 1, 0) for k in range(1, 5))
    ohd = onehot((iota((128, 512), 0) == r - 20 * fifth(r)) & (r < 100))
    wexp = mm(wst[...].astype(BF16), ohd)
    lane = iota((48, 512), 1)
    cond = (iota((48, 512), 0) >> 1) == (lane >> 7) * 5 + fifth(lane & 127)
    wparts = [jnp.where(cond, wexp[m * 48 : m * 48 + 48], 0.0) for m in range(9)]
    wmasked = jnp.concatenate(wparts, axis=0).astype(BF16)
    ws[...] = mm(selw_ref[...], wmasked).astype(BF16)
    late["mix"].wait()
    mixpad[...] = jnp.zeros_like(mixpad)
    mixpad[0:C, 0:C] = mix_ref[...].astype(F32)
    mixb = mixpad[...].astype(BF16)
    shift = int(math.log2(planes))
    ecol = onehot((iota((128, rows), 1) >> shift) == iota((128, rows), 0))
    for r0 in starts:
        erow = onehot(((iota((n, 128), 0) + r0) >> shift) == iota((n, 128), 1))
        kron = mm(mm_nt(erow, mixb).astype(BF16), ecol)
        diag = ((iota((n, rows), 0) + r0) & (planes - 1)) == (iota((n, rows), 1) & (planes - 1))
        kron = jnp.where(diag, kron, 0.0).astype(BF16)
        mixed[r0 : r0 + n, :] = mm(kron, f_ref[...])

    lanes = iota((128, 640), 1)
    for q in range(4):
        bc[q] = onehot(iota((128, 640), 0) == ((lanes >> 7) + 5 * q) * 4 + (lanes & 3))
    row = (lanes >> 7) * 20 + ((lanes & 127) >> 2)
    ohr = onehot((iota((128, 640), 0) == row) & ((lanes & 127) < 80))
    col = iota((256, 512), 1)
    ohg[0] = onehot(lane_code((256, 512), 24) == (col & 127) * 4 + (col >> 7))
    ohg[1] = onehot(lane_code((256, 512), 20) == (col & 63) * 4 + (col >> 7))

    def x_forward(recv, send, h):
        hi, lo = hilo(recv[h].reshape(32 * G, 128))
        p = mm(wxp[0], hi) + (mm(wxp[0], lo) + mm(wxp[1], hi))
        send[h] = p.astype(send.dtype).reshape(GY, 6 * G, 128)

    def y_sum(recv):
        halves = []
        for h in range(2):
            p = [recv[h, k].astype(F32) for k in range(GY)]
            halves.append((p[0] + p[1]) + (p[2] + p[3]))
        return jnp.concatenate(halves, axis=1)

    late["wxp"].wait()
    wait_y1 = []
    for h in range(2):
        wait_x1[h]()
        x_forward(rx1, sy1, h)
        wait_y1.append(ex_y(lambda peer: sy1.at[h, peer], ry1.at[h], h))
        ry1[h, gy] = sy1[h, gy]
        if h == 0:
            wait_w = ex_x(lambda peer: ws, rw, 2)
            rw[gx] = ws[...]

    wait_w()
    late["pab"].wait()
    rab = mm(pab_ref[...], rw[...].reshape(32 * G, 512)).astype(BF16)
    for q in range(4):
        rq[q] = mm(rab[:, q * 128 : (q + 1) * 128], ohr)
    late["px"].wait()

    for h in range(2):
        wait_y1[h]()
    shi, slo = hilo(y_sum(ry1))
    spec = mm(px_ref[...], shi) + mm(px_ref[...], slo)
    sspec[...] = spec.reshape(G, 8, 256)

    low = iota((8 * G, 128), 1) < 40
    turn = lambda a, by: pltpu.roll(a, by % 128, 1) if by % 128 else a
    parts = []
    for kk in range(3):
        h0, h1 = turn(spec[:, :128], -40 * kk), turn(spec[:, 128:], 40 - 40 * kk)
        parts.append(jnp.where(low, h0, h1))
    xhi, xlo = hilo(jnp.concatenate(parts, axis=0))
    acc = [jnp.zeros((24 * G, 128), F32) for _ in range(2)]
    for q in range(4):
        spread = mm(xhi, bc[q]) + mm(xlo, bc[q])
        for ab in range(2):
            prod = spread * rq[q, ab * 24 * G : (ab + 1) * 24 * G]
            acc[ab] += sum(prod[:, k * 128 : k * 128 + 128] for k in range(5))
    swapped = pltpu.roll(acc[1].reshape(3 * G, 8, 128), 4, 1).reshape(24 * G, 128)
    acc = (acc[0] + swapped).reshape(3, 8 * G, 128)
    wait_y2 = []
    for h in range(2):
        mine = [jnp.where(low if h == 0 else ~low, acc[kk], 0.0) for kk in range(3)]
        vals = sum(turn(mine[kk], 40 * kk - 40 * h) for kk in range(3))
        sy2[h] = vals.astype(BF16)
        wait_y2.append(ex_y(lambda peer: sy2.at[h], ry2.at[h], 2 + h))
        ry2[h, gy] = sy2[h]

    @pl.when(dp == 0)
    def _():
        pl.semaphore_wait(ready, D - 1)
        for k in range(1, D):
            pl.semaphore_signal(go, inc=1, device_id={"dp": k}, device_id_type=MESH)

    wait_spec = ex_x(lambda peer: sspec.at[peer], rspec, 3)
    rspec[gx] = sspec[gx]

    late["wxi"].wait()
    wait_x2 = []
    for h in range(2):
        wait_y2[h]()
        v = ry2[h].reshape(32 * G, 128)
        b = mm(wxi[0], v) + mm(wxi[1], v)
        sx2[h] = b.astype(BF16).reshape(G, 32, 128)
        wait_x2.append(ex_x(lambda peer: sx2.at[h, peer], rx2.at[h], 4 + h))
        rx2[h, gx] = sx2[h, gx]

    wait_spec()
    hi, lo = hilo(rspec[...].reshape(8 * G, 256))
    to_planes(mm(hi, ohg[0]) + mm(lo, ohg[0]))
    for tri in range(3):
        block = []
        for i in range(4):
            for ri in range(2):
                block.append(gi[i, pl.ds(ri * 4 + tri, G, stride=8), :])
        block.append(jnp.zeros((128 - 8 * G, 128), F32))
        stt[tri] = jnp.concatenate(block, axis=0).T[:72]

    late["cot"].wait()
    late["tyi"].wait()
    wait_x3 = []
    for h in range(2):
        wait_x2[h]()
        for g in range(G):
            block = jnp.concatenate([rx2[h, g].astype(F32), jnp.zeros((96, 128), F32)], axis=0)
            a3[pl.ds(h * 3 * hrows + g, 120, stride=G), :] = block.T[:120]
        for r0 in chunks[h]:
            bb = a3[part_of(h, 0, r0), :]
            bb += pltpu.roll(a3[part_of(h, 1, r0), :], 32, 1)
            bb += pltpu.roll(a3[part_of(h, 2, r0), :], 64, 1)
            bb = bb.astype(BF16)
            pre = mm(jnp.concatenate([bb, bb], axis=1), tyi[...]) + mixed[r0 : r0 + n, :]
            value, slope = gelu_parts(pre)
            out_ref[r0 : r0 + n, :] = value.astype(BF16)
            back = (cot[r0 : r0 + n, :].astype(F32) * slope).astype(BF16)
            backb[r0 : r0 + n, :] = back
            y_forward(back, h, r0)
        to_groups(h, sx3)
        wait_x3.append(ex_x(lambda peer: sx3.at[h, peer], rx3.at[h], 6 + h))
        rx3[h, gx] = sx3[h, gx]

    gmix = jnp.zeros((24, 128), F32)
    ecol_t = onehot((iota((rows, 128), 0) >> shift) == iota((rows, 128), 1))
    for r0 in starts:
        full = mm_nt(f_ref[r0 : r0 + n, :], backb[...])
        diag = ((iota((n, rows), 0) + r0) & (planes - 1)) == (iota((n, rows), 1) & (planes - 1))
        hi, lo = hilo(jnp.where(diag, full, 0.0))
        cols = mm(hi, ecol_t) + mm(lo, ecol_t)
        erow_t = onehot(((iota((24, n), 1) + r0) >> shift) == iota((24, n), 0))
        hi, lo = hilo(cols)
        gmix += mm(erow_t, hi) + mm(erow_t, lo)
    mgx_s[...] = gmix
    mgx_r[gx] = gmix

    wait_y3 = []
    for h in range(2):
        wait_x3[h]()
        x_forward(rx3, sy3, h)
        wait_y3.append(ex_y(lambda peer: sy3.at[h, peer], ry3.at[h], 4 + h))
        ry3[h, gy] = sy3[h, gy]

    wait_mgx = ex_x(lambda peer: mgx_s, mgx_r, 8)
    wait_mgx()
    total = mgx_r[0]
    for k in range(1, G):
        total += mgx_r[k]
    mgy_s[...] = total
    wait_mgy = ex_y(lambda peer: mgy_s, mgy_r, 6)
    mgy_r[gy] = total

    for h in range(2):
        wait_y3[h]()
    ghi, glo = hilo(y_sum(ry3))
    sgs[...] = (mm(px_ref[...], ghi) + mm(px_ref[...], glo)).reshape(G, 8, 256)
    wait_gs = ex_x(lambda peer: sgs.at[peer], rgs, 9)
    rgs[gx] = sgs[gx]

    wait_mgy()
    mix_scale = 1.0 / math.sqrt(D * planes * 16 * G * NY)
    part[9:12] = (((mgy_r[0] + mgy_r[1]) + (mgy_r[2] + mgy_r[3])) * mix_scale).reshape(3, 8, 128)

    norm_in = 1.0 / math.sqrt(16 * G * NY)
    norm_out = 1.0 / math.sqrt(36 * G)
    spec_scale = norm_out / norm_in / math.sqrt(D * planes)
    wait_gs()
    hi, lo = hilo(rgs[...].reshape(8 * G, 256))
    to_planes(mm(hi, ohg[1]) + mm(lo, ohg[1]))
    lane = iota((G, 128), 1)
    lane24 = iota((24, 128), 1) & 63
    for tri in range(3):
        block = []
        for i in range(4):
            g0 = gi[i, pl.ds(tri, G, stride=8), :]
            g1 = gi[i, pl.ds(4 + tri, G, stride=8), :]
            block += [jnp.where(lane < 64, g0, g1), jnp.where(lane < 64, g1, -g0)]
        block.append(jnp.zeros((128 - 8 * G, 128), F32))
        ahi, alo = hilo(stt[tri])
        bhi, blo = hilo(jnp.concatenate(block, axis=0))
        outer = mm(ahi, bhi) + (mm(ahi, blo) + mm(alo, bhi))
        grad = jnp.zeros((24, 128), F32)
        for kk in range(3):
            mine = (lane24 >= 20 * kk) & (lane24 < 20 * kk + 20)
            grad += jnp.where(mine, outer[24 * kk : 24 * kk + 24], 0.0)
        part[3 * tri : 3 * tri + 3] = (grad * spec_scale).reshape(3, 8, 128)

    def rs_copy(k, to):
        return pltpu.make_async_remote_copy(
            src_ref=part.at[pl.ds(to * tpr, tpr)],
            dst_ref=rsbuf.at[dp],
            send_sem=dp_s.at[0, k],
            recv_sem=dp_r.at[0, k],
            device_id={"dp": to},
            device_id_type=MESH,
        )

    def ag_copy(k, to, slot):
        return pltpu.make_async_remote_copy(
            src_ref=agsrc,
            dst_ref=agbuf.at[slot],
            send_sem=dp_s.at[1, k],
            recv_sem=dp_r.at[1, k],
            device_id={"dp": to},
            device_id_type=MESH,
        )

    @pl.when(dp != 0)
    def _():
        pl.semaphore_wait(go, 1)

    for k in range(1, D):
        to = lax.rem(dp + k, D)

        @pl.when(to < nred)
        def _():
            rs_copy(k, to).start()

    @pl.when(dp < nred)
    def _():
        rsbuf[dp] = part[pl.ds(dp * tpr, tpr)]
        for k in range(1, D):
            rs_copy(k, dp).wait_recv()
        tile = rsbuf[0]
        for k in range(1, D):
            tile += rsbuf[k]
        agsrc[...] = tile
        for k in range(1, D):
            ag_copy(k, lax.rem(dp + k, D), dp).start()
        agbuf[dp] = tile

    for k in range(1, D):
        frm = lax.rem(dp + D - k, D)

        @pl.when(frm < nred)
        def _():
            ag_copy(k, dp, frm).wait_recv()

    final = agbuf[...].reshape(TILES, 8, 128)
    mg_ref[...] = final[9:12].reshape(24, 128)[:C, :C]
    for tri in range(3):
        block = final[3 * tri : 3 * tri + 3].reshape(24, 128)
        for kk in range(3):
            for ri in range(2):
                off = ri * 64 + kk * 20
                sg_ref[tri * 3 + kk, :, ri, :] = block[:C, off : off + C]

    for copy in pending:
        copy.wait_send()
    for k in range(1, D):
        to = lax.rem(dp + k, D)

        @pl.when(to < nred)
        def _():
            rs_copy(k, to).wait_send()

    @pl.when(dp < nred)
    def _():
        for k in range(1, D):
            ag_copy(k, lax.rem(dp + k, D), dp).wait_send()


def store_kernel(out, sg, mg, out_hbm, sg_hbm, mg_hbm, sems):
    pairs = ((out, out_hbm), (sg, sg_hbm), (mg, mg_hbm))
    copies = [pltpu.make_async_copy(src, dst, sems.at[k]) for k, (src, dst) in enumerate(pairs)]
    for copy in copies:
        copy.start()
    for copy in copies:
        copy.wait()


def local(G, D, fields, cotangent, mix_weight, spectral_weight):
    rows = C * 4 * G
    cells = XL * NY
    t = tables(G)
    tpr = max(1, -(-TILES // D))
    nred = TILES // tpr
    vm = pl.BlockSpec(memory_space=pltpu.VMEM)
    hbm = pl.BlockSpec(memory_space=pl.ANY)
    V = pltpu.VMEM
    scratch = [
        V((rows, cells), BF16),
        V((2 * cells, 128), BF16),
        V((9, C, 2, C), BF16),
        V((C, C), BF16),
        V((32, 432), BF16),
        V((2, GY * 6 * G, 32 * G), BF16),
        V((48 * G, 32 * G), BF16),
        V((8 * G, 6 * G), BF16),
        V((2, 32 * G, GY * 8 * G), BF16),
        V((rows, cells), BF16),
        V((256, cells), BF16),
        V((3 * rows, 128), F32),
        V((rows, cells), F32),
        V((128, 128), F32),
        V((rows, cells), BF16),
        V((2, G, 32, 128), F32),
        V((2, G, 32, 128), F32),
        V((2, G, 32, 128), F32),
        V((2, G, 32, 128), F32),
        V((2, GY, 6 * G, 128), F32),
        V((2, GY, 6 * G, 128), F32),
        V((2, GY, 6 * G, 128), BF16),
        V((2, GY, 6 * G, 128), BF16),
        V((2, 8 * G, 128), BF16),
        V((2, GY, 8 * G, 128), BF16),
        V((2, G, 32, 128), BF16),
        V((2, G, 32, 128), BF16),
        V((32, 512), BF16),
        V((G, 32, 512), BF16),
        V((432, 128), F32),
        V((4, 48 * G, 640), F32),
        V((4, 128, 640), BF16),
        V((2, 256, 512), BF16),
        V((4, 8 * G, 128), F32),
        V((G, 8, 256), F32),
        V((G, 8, 256), F32),
        V((G, 8, 256), F32),
        V((G, 8, 256), F32),
        V((3, 72, 128), F32),
        V((24, 128), F32),
        V((G, 24, 128), F32),
        V((24, 128), F32),
        V((GY, 24, 128), F32),
        V((TILES, 8, 128), F32),
        V((D, tpr, 8, 128), F32),
        V((nred, tpr, 8, 128), F32),
        V((tpr, 8, 128), F32),
        pltpu.SemaphoreType.REGULAR,
        pltpu.SemaphoreType.REGULAR,
        pltpu.SemaphoreType.DMA((18,)),
        pltpu.SemaphoreType.DMA((10, G)),
        pltpu.SemaphoreType.DMA((10, G)),
        pltpu.SemaphoreType.DMA((7, GY)),
        pltpu.SemaphoreType.DMA((7, GY)),
        pltpu.SemaphoreType.DMA((2, D)),
        pltpu.SemaphoreType.DMA((2, D)),
    ]
    out, sg, mg = pl.pallas_call(
        functools.partial(kernel, G, D),
        out_shape=(
            V((rows, cells), BF16),
            V((9, C, 2, C), F32),
            V((C, C), F32),
        ),
        in_specs=[hbm] * 11,
        out_specs=(vm, vm, vm),
        scratch_shapes=scratch,
        compiler_params=pltpu.CompilerParams(
            collective_id=0, has_side_effects=True, vmem_limit_bytes=60 * 1024 * 1024
        ),
    )(
        fields.reshape(rows, cells),
        t["tyf"],
        spectral_weight.transpose(0, 2, 1, 3),
        mix_weight,
        t["selw"],
        t["wxp"],
        t["pab"],
        t["px"],
        t["wxi"],
        cotangent.reshape(rows, cells),
        t["tyi"],
    )
    out, sg, mg = pl.pallas_call(
        store_kernel,
        out_shape=tuple(jax.ShapeDtypeStruct(a.shape, a.dtype) for a in (out, sg, mg)),
        in_specs=[hbm] * 3,
        out_specs=(hbm,) * 3,
        scratch_shapes=[pltpu.SemaphoreType.DMA((3,))],
        compiler_params=pltpu.CompilerParams(vmem_limit_bytes=1 << 20),
    )(out, sg, mg)
    return out.reshape(fields.shape), sg.transpose(0, 2, 1, 3), mg


def solution(mesh):
    G, D = mesh.shape["gx"], mesh.shape["dp"]
    cells = P("dp", None, None, ("gx", "gy"))
    modes = P(("gx", "gy"), None, None, None)
    return jax.shard_map(
        functools.partial(local, G, D),
        mesh=mesh,
        in_specs=(cells, cells, P(), modes),
        out_specs=(cells, modes, P()),
        check_vma=False,
    )
```

```python
import functools
import math

import jax
import jax.numpy as jnp
import numpy as np
from jax import lax
from jax.experimental import pallas as pl
from jax.experimental.pallas import tpu as pltpu
from jax.sharding import PartitionSpec as P

MESH = pl.DeviceIdType.MESH
F32 = jnp.float32
BF16 = jnp.bfloat16

C = 20
NY = 128
KY = 12
GY = 4
XL = 4
PL_OWN = 4
TILES = 12


def split(table):
    table = np.asarray(table, np.float32)
    hi = table.astype(BF16)
    lo = (table - hi.astype(np.float32)).astype(BF16)
    return np.stack([hi, lo])


@functools.lru_cache(None)
def tables(G):
    nx, kxn = 16 * G, 3 * G
    norm_in = 1.0 / math.sqrt(nx * NY)
    norm_out = 1.0 / math.sqrt(kxn * KY)
    y = np.arange(NY)
    tyf = np.zeros((XL * NY, 128))
    tyi = np.zeros((128, XL * NY))
    for kk in range(3):
        for ks in range(4):
            ang = 2 * np.pi * ((3 * ks + kk) * y % NY) / NY
            for x in range(XL):
                col = kk * 32 + ks * 8 + x * 2
                tyf[x * NY : (x + 1) * NY, col] = np.cos(ang) * norm_in
                tyf[x * NY : (x + 1) * NY, col + 1] = -np.sin(ang) * norm_in
                tyi[col, x * NY : (x + 1) * NY] = np.cos(ang)
                tyi[col + 1, x * NY : (x + 1) * NY] = -np.sin(ang)
    wxp = np.zeros((GY, GY * 6 * G, 32 * G))
    wxi = np.zeros((GY, 32 * G, GY * 8 * G))
    for gy in range(GY):
        for go in range(GY):
            for tri in range(3):
                jj, ks = divmod(3 * go + tri, 4)
                for gq in range(G):
                    j = 3 * gq + jj
                    kx = j if j < kxn // 2 else nx - kxn + j
                    rp = go * 6 * G + gq * 6 + tri * 2
                    ci = go * 8 * G + gq * 8 + tri
                    for gx in range(G):
                        for x in range(XL):
                            ang = 2 * np.pi * (kx * (4 * (gx * GY + gy) + x) % nx) / nx
                            c, s = np.cos(ang), np.sin(ang)
                            k = gx * 32 + ks * 8 + x * 2
                            wxp[gy, rp, k], wxp[gy, rp, k + 1] = c, s
                            wxp[gy, rp + 1, k], wxp[gy, rp + 1, k + 1] = -s, c
                            wxi[gy, k, ci], wxi[gy, k, ci + 4] = c * norm_out, -s * norm_out
                            wxi[gy, k + 1, ci], wxi[gy, k + 1, ci + 4] = s * norm_out, c * norm_out
    px = np.zeros((8 * G, 6 * G))
    pab = np.zeros((2, 3, 8 * G, 32 * G))
    for gq in range(G):
        for ri in range(2):
            for tri in range(3):
                row = gq * 8 + ri * 4 + tri
                px[row, gq * 6 + tri * 2 + ri] = 1
                for kk in range(3):
                    src = gq * 32 + kk * 8
                    pab[0, kk, row, src + tri] = 1
                    pab[1, kk, row, src + 4 + tri] = 1 if ri == 0 else -1
    selw = np.zeros((32, 18 * 24))
    for kk in range(3):
        for ri in range(2):
            for tri in range(3):
                q = (tri * 3 + kk) * 48 + ri
                selw[kk * 8 + ri * 4 + tri, q : q + 2 * C : 2] = 1
    b = lambda a: np.asarray(a, np.float32).astype(BF16)
    return dict(
        tyf=np.concatenate(split(tyf)),
        tyi=np.concatenate(split(tyi)),
        wxp=np.stack([split(w) for w in wxp]),
        wxi=np.stack([split(w) for w in wxi]),
        px=b(px),
        pab=b(pab.reshape(48 * G, 32 * G)),
        selw=b(selw),
    )


def mm(a, b):
    return jnp.dot(a, b, preferred_element_type=F32)


def mm_nt(a, b):
    return lax.dot_general(a, b, (((1,), (1,)), ((), ())), preferred_element_type=F32)


def hilo(a):
    hi = a.astype(BF16)
    return hi, (a - hi.astype(F32)).astype(BF16)


def mm_tab(tab, x):
    hi, lo = hilo(x)
    return mm(tab[0], hi) + (mm(tab[0], lo) + mm(tab[1], hi))


def iota(shape, dim):
    return lax.broadcasted_iota(jnp.int32, shape, dim)


def onehot(cond):
    return jnp.where(cond, 1.0, 0.0).astype(BF16)


def lane_code(shape, stride):
    row = iota(shape, 0)
    q = row & 127
    kk = jnp.where(q >= 80, 2, jnp.where(q >= 40, 1, 0))
    c = (row >> 7) * 10 + ((q - 40 * kk) >> 2)
    return jnp.where(q < 120, (kk * stride + c) * 4 + (q & 3), -1)


def gelu_parts(h):
    k = math.sqrt(2.0 / math.pi)
    hh = h * h
    u = 0.5 * jnp.tanh(h * (k + (0.044715 * k) * hh)) + 0.5
    value = h * u
    slope = u + (value * (1.0 - u)) * (2.0 * k + (6.0 * 0.044715 * k) * hh)
    return value, slope


def kernel(
    G, D, f_hbm, tyf_hbm, w_hbm, mix_hbm, selw_hbm, wxp_hbm, pab_hbm, px_hbm, wxi_hbm, cot_hbm, tyi_hbm,
    out_ref, sg_ref, mg_ref,
    f_ref, tyf_ref, w_ref, mix_ref, selw_ref, wxp, pab_ref, px_ref, wxi, cot, tyi, a3, b3, mixed, mixpad, backb,
    sx1, rx1, sx3, rx3, sy1, ry1, sy3, ry3, sy2, ry2, sx2, rx2,
    ws, rw, wst, rq, bc, ohg, gi, sspec, rspec, sgs, rgs, stt,
    mgx_s, mgx_r, mgy_s, mgy_r, part, rsbuf, agbuf, agsrc,
    ready, go, lsem, bx_s, bx_r, by_s, by_r, dp_s, dp_r,
):
    rows = C * 4 * G
    planes = 4 * G
    gx = lax.axis_index("gx")
    gy = lax.axis_index("gy")
    dp = lax.axis_index("dp")
    tpr = max(1, -(-TILES // D))
    nred = TILES // tpr

    hrows = rows // 2
    chunk = 160 if hrows % 160 == 0 else hrows
    chunks = [[h * hrows + r for r in range(0, hrows, chunk)] for h in range(2)]
    starts = chunks[0] + chunks[1]
    n = chunk
    barrier = pltpu.get_barrier_semaphore()
    for k in range(1, G):
        pl.semaphore_signal(barrier, inc=1, device_id={"gx": lax.rem(gx + k, G)}, device_id_type=MESH)
    for k in range(1, GY):
        pl.semaphore_signal(barrier, inc=1, device_id={"gy": lax.rem(gy + k, GY)}, device_id_type=MESH)

    @pl.when(dp == 0)
    def _():
        for k in range(1, D):
            pl.semaphore_signal(barrier, inc=1, device_id={"dp": k}, device_id_type=MESH)


    pieces = [(f_hbm.at[pl.ds(r0, n)], f_ref.at[pl.ds(r0, n)]) for r0 in starts]
    pieces.insert(0, (tyf_hbm, tyf_ref))
    pieces += [(w_hbm, w_ref), (selw_hbm, selw_ref), (mix_hbm, mix_ref), (wxp_hbm.at[gy], wxp)]
    pieces += [(pab_hbm, pab_ref), (px_hbm, px_ref), (wxi_hbm.at[gy], wxi), (cot_hbm, cot), (tyi_hbm, tyi)]
    loads = [pltpu.make_async_copy(src, dst, lsem.at[k]) for k, (src, dst) in enumerate(pieces)]
    for copy in loads:
        copy.start()
    late = dict(zip(("w", "selw", "mix", "wxp", "pab", "px", "wxi", "cot", "tyi"), loads[1 + len(starts) :]))

    pending = []

    def exchange(axis, size, me, src_of, dst, sems_s, sems_r, ex):
        def one(k):
            peer = lax.rem(me + k, size)
            return pltpu.make_async_remote_copy(
                src_ref=src_of(peer),
                dst_ref=dst.at[me],
                send_sem=sems_s.at[ex, k],
                recv_sem=sems_r.at[ex, k],
                device_id={axis: peer},
                device_id_type=MESH,
            )

        copies = [one(k) for k in sorted(range(1, size), key=lambda k: abs(2 * k - size))]
        for copy in copies:
            copy.start()
        pending.extend(copies)

        def wait():
            for copy in copies:
                copy.wait_recv()

        return wait

    def ex_x(src_of, dst, ex):
        return exchange("gx", G, gx, src_of, dst, bx_s, bx_r, ex)

    def ex_y(src_of, dst, ex):
        return exchange("gy", GY, gy, src_of, dst, by_s, by_r, ex)

    rest = jnp.zeros((8, 128), F32)

    def part_of(h, kk, r0):
        return pl.ds((h * 3 + kk) * hrows + r0 - h * hrows, n)

    def y_forward(data, h, r0):
        a = mm(jnp.concatenate([data, data], axis=1), tyf_ref[...])
        a3[part_of(h, 0, r0), :] = a
        a3[part_of(h, 1, r0), :] = pltpu.roll(a, 96, 1)
        a3[part_of(h, 2, r0), :] = pltpu.roll(a, 64, 1)

    def to_groups(h, dst):
        for g in range(G):
            block = a3[pl.ds(h * 3 * hrows + g, 120, stride=G), :]
            dst[h, g] = jnp.concatenate([block, rest], axis=0).T[:32]

    def to_planes(value):
        for i in range(4):
            gi[i] = value[:, i * 128 : (i + 1) * 128]

    loads[0].wait()
    wait_x1 = []
    for h in range(2):
        for r0 in chunks[h]:
            loads[1 + starts.index(r0)].wait()
            y_forward(f_ref[r0 : r0 + n, :], h, r0)
        to_groups(h, sx1)
        if h == 0:


            @pl.when(dp == 0)
            def _():
                pl.semaphore_wait(barrier, G - 1 + GY - 1)

            @pl.when(dp != 0)
            def _():
                pl.semaphore_wait(barrier, G - 1 + GY - 1 + 1)
                pl.semaphore_signal(ready, inc=1, device_id={"dp": 0}, device_id_type=MESH)

        wait_x1.append(ex_x(lambda peer: sx1.at[h, peer], rx1.at[h], h))
        rx1[h, gx] = sx1[h, gx]

    late["w"].wait()
    late["selw"].wait()
    wst[...] = jnp.zeros_like(wst)
    for m in range(9):
        wst[m * 48 : m * 48 + 2 * C, 0:C] = w_ref[m].astype(F32).reshape(2 * C, C)
    r = iota((128, 512), 1) & 127
    fifth = lambda r: sum(jnp.where(r >= 20 * k, 1, 0) for k in range(1, 5))
    ohd = onehot((iota((128, 512), 0) == r - 20 * fifth(r)) & (r < 100))
    wexp = mm(wst[...].astype(BF16), ohd)
    lane = iota((48, 512), 1)
    cond = (iota((48, 512), 0) >> 1) == (lane >> 7) * 5 + fifth(lane & 127)
    wparts = [jnp.where(cond, wexp[m * 48 : m * 48 + 48], 0.0) for m in range(9)]
    wmasked = jnp.concatenate(wparts, axis=0).astype(BF16)
    ws[...] = mm(selw_ref[...], wmasked).astype(BF16)
    late["mix"].wait()
    mixpad[...] = jnp.zeros_like(mixpad)
    mixpad[0:C, 0:C] = mix_ref[...].astype(F32)
    mixb = mixpad[...].astype(BF16)
    shift = int(math.log2(planes))
    ecol = onehot((iota((128, rows), 1) >> shift) == iota((128, rows), 0))
    for r0 in starts:
        erow = onehot(((iota((n, 128), 0) + r0) >> shift) == iota((n, 128), 1))
        kron = mm(mm_nt(erow, mixb).astype(BF16), ecol)
        diag = ((iota((n, rows), 0) + r0) & (planes - 1)) == (iota((n, rows), 1) & (planes - 1))
        kron = jnp.where(diag, kron, 0.0).astype(BF16)
        mixed[r0 : r0 + n, :] = mm(kron, f_ref[...])

    lanes = iota((256, 640), 1)
    for q in range(4):
        spot = ((lanes >> 7) + 5 * q) * 4 + (lanes & 3)
        bc[q] = onehot((iota((256, 640), 0) & 127) == spot)
    lanes = iota((128, 640), 1)
    row = (lanes >> 7) * 20 + ((lanes & 127) >> 2)
    ohr = onehot((iota((128, 640), 0) == row) & ((lanes & 127) < 80))
    col = iota((256, 512), 1)
    ohg[0] = onehot(lane_code((256, 512), 24) == (col & 127) * 4 + (col >> 7))
    ohg[1] = onehot(lane_code((256, 512), 20) == (col & 63) * 4 + (col >> 7))

    def x_forward(recv, send, h):
        hi, lo = hilo(recv[h].reshape(32 * G, 128))
        p = mm(wxp[0], hi) + (mm(wxp[0], lo) + mm(wxp[1], hi))
        send[h] = p.astype(send.dtype).reshape(GY, 6 * G, 128)

    def y_sum(recv, h):
        p = [recv[h, k].astype(F32) for k in range(GY)]
        return (p[0] + p[1]) + (p[2] + p[3])

    late["wxp"].wait()
    wait_y1 = []
    for h in range(2):
        wait_x1[h]()
        x_forward(rx1, sy1, h)
        wait_y1.append(ex_y(lambda peer: sy1.at[h, peer], ry1.at[h], h))
        ry1[h, gy] = sy1[h, gy]
        if h == 0:
            wait_w = ex_x(lambda peer: ws, rw, 2)
            rw[gx] = ws[...]

    wait_w()
    late["pab"].wait()
    rab = mm(pab_ref[...], rw[...].reshape(32 * G, 512)).astype(BF16)
    for q in range(4):
        rq[q] = mm(rab[:, q * 128 : (q + 1) * 128], ohr)
    late["px"].wait()

    for h in range(2):
        wait_y1[h]()
    shi, slo = hilo(jnp.concatenate([y_sum(ry1, h) for h in range(2)], axis=1))
    spec = mm(px_ref[...], shi) + mm(px_ref[...], slo)
    sspec[...] = spec.reshape(G, 8, 256)

    low = iota((8 * G, 128), 1) < 40
    turn = lambda a, by: pltpu.roll(a, by % 128, 1) if by % 128 else a
    parts = []
    for kk in range(3):
        h0, h1 = turn(spec[:, :128], -40 * kk), turn(spec[:, 128:], 40 - 40 * kk)
        parts.append(jnp.where(low, h0, h1))
    xx = jnp.concatenate(hilo(jnp.concatenate(parts, axis=0)), axis=1)
    acc = [jnp.zeros((24 * G, 128), F32) for _ in range(2)]
    for q in range(4):
        spread = mm(xx, bc[q])
        for ab in range(2):
            prod = spread * rq[q, ab * 24 * G : (ab + 1) * 24 * G]
            acc[ab] += sum(prod[:, k * 128 : k * 128 + 128] for k in range(5))
    swapped = pltpu.roll(acc[1].reshape(3 * G, 8, 128), 4, 1).reshape(24 * G, 128)
    acc = (acc[0] + swapped).reshape(3, 8 * G, 128)
    wait_y2 = []
    for h in range(2):
        mine = [jnp.where(low if h == 0 else ~low, acc[kk], 0.0) for kk in range(3)]
        vals = sum(turn(mine[kk], 40 * kk - 40 * h) for kk in range(3))
        sy2[h] = vals.astype(BF16)
        wait_y2.append(ex_y(lambda peer: sy2.at[h], ry2.at[h], 2 + h))
        ry2[h, gy] = sy2[h]

    @pl.when(dp == 0)
    def _():
        pl.semaphore_wait(ready, D - 1)
        for k in range(1, D):
            pl.semaphore_signal(go, inc=1, device_id={"dp": k}, device_id_type=MESH)

    wait_spec = ex_x(lambda peer: sspec.at[peer], rspec, 3)
    rspec[gx] = sspec[gx]

    late["wxi"].wait()
    wait_x2 = []
    for h in range(2):
        wait_y2[h]()
        v = ry2[h].reshape(32 * G, 128)
        b = mm(wxi[0], v) + mm(wxi[1], v)
        sx2[h] = b.astype(BF16).reshape(G, 32, 128)
        wait_x2.append(ex_x(lambda peer: sx2.at[h, peer], rx2.at[h], 4 + h))
        rx2[h, gx] = sx2[h, gx]

    wait_spec()
    hi, lo = hilo(rspec[...].reshape(8 * G, 256))
    to_planes(mm(hi, ohg[0]) + mm(lo, ohg[0]))
    for tri in range(3):
        block = []
        for i in range(4):
            for ri in range(2):
                block.append(gi[i, pl.ds(ri * 4 + tri, G, stride=8), :])
        block.append(jnp.zeros((128 - 8 * G, 128), F32))
        stt[tri] = jnp.concatenate(block, axis=0).T[:72]

    late["cot"].wait()
    late["tyi"].wait()
    def planes_back(h):
        wait_x2[h]()
        for g in range(G):
            block = jnp.concatenate([rx2[h, g].astype(F32), jnp.zeros((96, 128), F32)], axis=0)
            b3[pl.ds(h * 3 * hrows + g, 120, stride=G), :] = block.T[:120]

    def pointwise(h, r0):
        bb = b3[part_of(h, 0, r0), :]
        bb += pltpu.roll(b3[part_of(h, 1, r0), :], 32, 1)
        bb += pltpu.roll(b3[part_of(h, 2, r0), :], 64, 1)
        bb = bb.astype(BF16)
        pre = mm(jnp.concatenate([bb, bb], axis=1), tyi[...]) + mixed[r0 : r0 + n, :]
        value, slope = gelu_parts(pre)
        out_ref[r0 : r0 + n, :] = value.astype(BF16)
        back = (cot[r0 : r0 + n, :].astype(F32) * slope).astype(BF16)
        backb[r0 : r0 + n, :] = back
        y_forward(back, h, r0)

    wait_x3 = []
    for h in range(2):
        planes_back(h)
        for r0 in chunks[h]:
            pointwise(h, r0)
        to_groups(h, sx3)
        wait_x3.append(ex_x(lambda peer: sx3.at[h, peer], rx3.at[h], 6 + h))
        rx3[h, gx] = sx3[h, gx]

    gmix = jnp.zeros((24, 128), F32)
    ecol_t = onehot((iota((rows, 128), 0) >> shift) == iota((rows, 128), 1))
    for r0 in starts:
        full = mm_nt(f_ref[r0 : r0 + n, :], backb[...])
        diag = ((iota((n, rows), 0) + r0) & (planes - 1)) == (iota((n, rows), 1) & (planes - 1))
        hi, lo = hilo(jnp.where(diag, full, 0.0))
        cols = mm(hi, ecol_t) + mm(lo, ecol_t)
        erow_t = onehot(((iota((24, n), 1) + r0) >> shift) == iota((24, n), 0))
        hi, lo = hilo(cols)
        gmix += mm(erow_t, hi) + mm(erow_t, lo)
    mgx_s[...] = gmix
    mgx_r[gx] = gmix

    wait_y3 = []
    for h in range(2):
        wait_x3[h]()
        x_forward(rx3, sy3, h)
        wait_y3.append(ex_y(lambda peer: sy3.at[h, peer], ry3.at[h], 4 + h))
        ry3[h, gy] = sy3[h, gy]

    wait_mgx = ex_x(lambda peer: mgx_s, mgx_r, 8)
    wait_mgx()
    total = mgx_r[0]
    for k in range(1, G):
        total += mgx_r[k]
    mgy_s[...] = total
    wait_mgy = ex_y(lambda peer: mgy_s, mgy_r, 6)
    mgy_r[gy] = total

    wait_gs = []
    for h in range(2):
        wait_y3[h]()
        ghi, glo = hilo(y_sum(ry3, h))
        sgs[h] = (mm(px_ref[...], ghi) + mm(px_ref[...], glo)).reshape(G, 8, 128)
        wait_gs.append(ex_x(lambda peer: sgs.at[h, peer], rgs.at[h], 9 + h))
        rgs[h, gx] = sgs[h, gx]

    wait_mgy()
    mix_scale = 1.0 / math.sqrt(D * planes * 16 * G * NY)
    part[9:12] = (((mgy_r[0] + mgy_r[1]) + (mgy_r[2] + mgy_r[3])) * mix_scale).reshape(3, 8, 128)

    norm_in = 1.0 / math.sqrt(16 * G * NY)
    norm_out = 1.0 / math.sqrt(36 * G)
    spec_scale = norm_out / norm_in / math.sqrt(D * planes)
    for h in range(2):
        wait_gs[h]()
    hi, lo = hilo(jnp.concatenate([rgs[h].reshape(8 * G, 128) for h in range(2)], axis=1))
    to_planes(mm(hi, ohg[1]) + mm(lo, ohg[1]))
    lane = iota((G, 128), 1)
    lane24 = iota((24, 128), 1) & 63
    for tri in range(3):
        block = []
        for i in range(4):
            g0 = gi[i, pl.ds(tri, G, stride=8), :]
            g1 = gi[i, pl.ds(4 + tri, G, stride=8), :]
            block += [jnp.where(lane < 64, g0, g1), jnp.where(lane < 64, g1, -g0)]
        block.append(jnp.zeros((128 - 8 * G, 128), F32))
        ahi, alo = hilo(stt[tri])
        bhi, blo = hilo(jnp.concatenate(block, axis=0))
        outer = mm(ahi, bhi) + (mm(ahi, blo) + mm(alo, bhi))
        grad = jnp.zeros((24, 128), F32)
        for kk in range(3):
            mine = (lane24 >= 20 * kk) & (lane24 < 20 * kk + 20)
            grad += jnp.where(mine, outer[24 * kk : 24 * kk + 24], 0.0)
        part[3 * tri : 3 * tri + 3] = (grad * spec_scale).reshape(3, 8, 128)

    def rs_copy(k, to):
        return pltpu.make_async_remote_copy(
            src_ref=part.at[pl.ds(to * tpr, tpr)],
            dst_ref=rsbuf.at[dp],
            send_sem=dp_s.at[0, k],
            recv_sem=dp_r.at[0, k],
            device_id={"dp": to},
            device_id_type=MESH,
        )

    def ag_copy(k, to, slot):
        return pltpu.make_async_remote_copy(
            src_ref=agsrc,
            dst_ref=agbuf.at[slot],
            send_sem=dp_s.at[1, k],
            recv_sem=dp_r.at[1, k],
            device_id={"dp": to},
            device_id_type=MESH,
        )

    @pl.when(dp != 0)
    def _():
        pl.semaphore_wait(go, 1)

    for k in range(1, D):
        to = lax.rem(dp + k, D)

        @pl.when(to < nred)
        def _():
            rs_copy(k, to).start()

    @pl.when(dp < nred)
    def _():
        rsbuf[dp] = part[pl.ds(dp * tpr, tpr)]
        for k in range(1, D):
            rs_copy(k, dp).wait_recv()
        tile = rsbuf[0]
        for k in range(1, D):
            tile += rsbuf[k]
        agsrc[...] = tile
        for k in range(1, D):
            ag_copy(k, lax.rem(dp + k, D), dp).start()
        agbuf[dp] = tile

    for copy in pending:
        copy.wait_send()
    for k in range(1, D):
        to = lax.rem(dp + k, D)

        @pl.when(to < nred)
        def _():
            rs_copy(k, to).wait_send()

    for k in range(1, D):
        frm = lax.rem(dp + D - k, D)

        @pl.when(frm < nred)
        def _():
            ag_copy(k, dp, frm).wait_recv()

    final = agbuf[...].reshape(TILES, 8, 128)
    mg_ref[...] = final[9:12].reshape(24, 128)[:C, :C]
    pairs = iota((40, 64), 0) == (iota((40, 64), 1) & 31) * 2 + (iota((40, 64), 1) >> 5)
    pairs = onehot(pairs)
    gap = jnp.zeros((8, 128), F32)
    for tri in range(3):
        block = final[3 * tri : 3 * tri + 3].reshape(24, 128)
        both = jnp.concatenate([block, gap, pltpu.roll(block, 64, 1), gap], axis=0)
        hi, lo = hilo(both)
        both = mm(pairs, hi) + mm(pairs, lo)
        for kk in range(3):
            piece = both if kk == 0 else pltpu.roll(both, 128 - 20 * kk, 1)
            sg_ref[tri * 3 + kk] = piece[:, :C].reshape(C, 2, C)

    @pl.when(dp < nred)
    def _():
        for k in range(1, D):
            ag_copy(k, lax.rem(dp + k, D), dp).wait_send()


def store_kernel(out, sg, mg, out_hbm, sg_hbm, mg_hbm, sems):
    pairs = ((out, out_hbm), (sg, sg_hbm), (mg, mg_hbm))
    copies = [pltpu.make_async_copy(src, dst, sems.at[k]) for k, (src, dst) in enumerate(pairs)]
    for copy in copies:
        copy.start()
    for copy in copies:
        copy.wait()


def local(G, D, fields, cotangent, mix_weight, spectral_weight):
    rows = C * 4 * G
    cells = XL * NY
    t = tables(G)
    tpr = max(1, -(-TILES // D))
    nred = TILES // tpr
    vm = pl.BlockSpec(memory_space=pltpu.VMEM)
    hbm = pl.BlockSpec(memory_space=pl.ANY)
    V = pltpu.VMEM
    scratch = [
        V((rows, cells), BF16),
        V((2 * cells, 128), BF16),
        V((9, C, 2, C), BF16),
        V((C, C), BF16),
        V((32, 432), BF16),
        V((2, GY * 6 * G, 32 * G), BF16),
        V((48 * G, 32 * G), BF16),
        V((8 * G, 6 * G), BF16),
        V((2, 32 * G, GY * 8 * G), BF16),
        V((rows, cells), BF16),
        V((256, cells), BF16),
        V((3 * rows, 128), F32),
        V((3 * rows, 128), F32),
        V((rows, cells), F32),
        V((128, 128), F32),
        V((rows, cells), BF16),
        V((2, G, 32, 128), F32),
        V((2, G, 32, 128), F32),
        V((2, G, 32, 128), F32),
        V((2, G, 32, 128), F32),
        V((2, GY, 6 * G, 128), F32),
        V((2, GY, 6 * G, 128), F32),
        V((2, GY, 6 * G, 128), BF16),
        V((2, GY, 6 * G, 128), BF16),
        V((2, 8 * G, 128), BF16),
        V((2, GY, 8 * G, 128), BF16),
        V((2, G, 32, 128), BF16),
        V((2, G, 32, 128), BF16),
        V((32, 512), BF16),
        V((G, 32, 512), BF16),
        V((432, 128), F32),
        V((4, 48 * G, 640), F32),
        V((4, 256, 640), BF16),
        V((2, 256, 512), BF16),
        V((4, 8 * G, 128), F32),
        V((G, 8, 256), F32),
        V((G, 8, 256), F32),
        V((2, G, 8, 128), F32),
        V((2, G, 8, 128), F32),
        V((3, 72, 128), F32),
        V((24, 128), F32),
        V((G, 24, 128), F32),
        V((24, 128), F32),
        V((GY, 24, 128), F32),
        V((TILES, 8, 128), F32),
        V((D, tpr, 8, 128), F32),
        V((nred, tpr, 8, 128), F32),
        V((tpr, 8, 128), F32),
        pltpu.SemaphoreType.REGULAR,
        pltpu.SemaphoreType.REGULAR,
        pltpu.SemaphoreType.DMA((32,)),
        pltpu.SemaphoreType.DMA((11, G)),
        pltpu.SemaphoreType.DMA((11, G)),
        pltpu.SemaphoreType.DMA((7, GY)),
        pltpu.SemaphoreType.DMA((7, GY)),
        pltpu.SemaphoreType.DMA((2, D)),
        pltpu.SemaphoreType.DMA((2, D)),
    ]
    out, sg, mg = pl.pallas_call(
        functools.partial(kernel, G, D),
        out_shape=(
            V((rows, cells), BF16),
            V((9, C, 2, C), F32),
            V((C, C), F32),
        ),
        in_specs=[hbm] * 11,
        out_specs=(vm, vm, vm),
        scratch_shapes=scratch,
        compiler_params=pltpu.CompilerParams(
            collective_id=0, has_side_effects=True, vmem_limit_bytes=60 * 1024 * 1024
        ),
    )(
        fields.reshape(rows, cells),
        t["tyf"],
        spectral_weight.transpose(0, 2, 1, 3),
        mix_weight,
        t["selw"],
        t["wxp"],
        t["pab"],
        t["px"],
        t["wxi"],
        cotangent.reshape(rows, cells),
        t["tyi"],
    )
    out, sg, mg = pl.pallas_call(
        store_kernel,
        out_shape=tuple(jax.ShapeDtypeStruct(a.shape, a.dtype) for a in (out, sg, mg)),
        in_specs=[hbm] * 3,
        out_specs=(hbm,) * 3,
        scratch_shapes=[pltpu.SemaphoreType.DMA((3,))],
        compiler_params=pltpu.CompilerParams(vmem_limit_bytes=1 << 20),
    )(out, sg, mg)
    return out.reshape(fields.shape), sg.transpose(0, 2, 1, 3), mg


def solution(mesh):
    G, D = mesh.shape["gx"], mesh.shape["dp"]
    cells = P("dp", None, None, ("gx", "gy"))
    modes = P(("gx", "gy"), None, None, None)
    return jax.shard_map(
        functools.partial(local, G, D),
        mesh=mesh,
        in_specs=(cells, cells, P(), modes),
        out_specs=(cells, modes, P()),
        check_vma=False,
    )
```

```python
import functools
import math

import jax
import jax.numpy as jnp
import numpy as np
from jax import lax
from jax.experimental import pallas as pl
from jax.experimental.pallas import tpu as pltpu
from jax.sharding import PartitionSpec as P

MESH = pl.DeviceIdType.MESH
F32 = jnp.float32
BF16 = jnp.bfloat16

C = 20
NY = 128
KY = 12
GY = 4
XL = 4
PL_OWN = 4
TILES = 12


def split(table):
    table = np.asarray(table, np.float32)
    hi = table.astype(BF16)
    lo = (table - hi.astype(np.float32)).astype(BF16)
    return np.stack([hi, lo])


@functools.lru_cache(None)
def tables(G):
    nx, kxn = 16 * G, 3 * G
    norm_in = 1.0 / math.sqrt(nx * NY)
    norm_out = 1.0 / math.sqrt(kxn * KY)
    y = np.arange(NY)
    tyf = np.zeros((XL * NY, 128))
    tyi = np.zeros((128, XL * NY))
    for kk in range(3):
        for ks in range(4):
            ang = 2 * np.pi * ((3 * ks + kk) * y % NY) / NY
            for x in range(XL):
                col = kk * 32 + ks * 8 + x * 2
                tyf[x * NY : (x + 1) * NY, col] = np.cos(ang) * norm_in
                tyf[x * NY : (x + 1) * NY, col + 1] = -np.sin(ang) * norm_in
                tyi[col, x * NY : (x + 1) * NY] = np.cos(ang)
                tyi[col + 1, x * NY : (x + 1) * NY] = -np.sin(ang)
    wxp = np.zeros((GY, GY * 6 * G, 32 * G))
    wxi = np.zeros((GY, 32 * G, GY * 6 * G))
    for gy in range(GY):
        for go in range(GY):
            for tri in range(3):
                jj, ks = divmod(3 * go + tri, 4)
                for gq in range(G):
                    j = 3 * gq + jj
                    kx = j if j < kxn // 2 else nx - kxn + j
                    rp = go * 6 * G + gq * 6 + tri * 2
                    for gx in range(G):
                        for x in range(XL):
                            ang = 2 * np.pi * (kx * (4 * (gx * GY + gy) + x) % nx) / nx
                            c, s = np.cos(ang), np.sin(ang)
                            k = gx * 32 + ks * 8 + x * 2
                            wxp[gy, rp, k], wxp[gy, rp, k + 1] = c, s
                            wxp[gy, rp + 1, k], wxp[gy, rp + 1, k + 1] = -s, c
                            wxi[gy, k, rp], wxi[gy, k, rp + 1] = c * norm_out, -s * norm_out
                            wxi[gy, k + 1, rp], wxi[gy, k + 1, rp + 1] = s * norm_out, c * norm_out
    px = np.zeros((8 * G, 6 * G))
    pab = np.zeros((2, 3, 8 * G, 32 * G))
    for gq in range(G):
        for ri in range(2):
            for tri in range(3):
                row = gq * 8 + ri * 4 + tri
                px[row, gq * 6 + tri * 2 + ri] = 1
                for kk in range(3):
                    src = gq * 32 + kk * 8
                    pab[0, kk, row, src + tri] = 1
                    pab[1, kk, row, src + 4 + tri] = 1 if ri == 0 else -1
    selw = np.zeros((32, 18 * 24))
    for kk in range(3):
        for ri in range(2):
            for tri in range(3):
                q = (tri * 3 + kk) * 48 + ri
                selw[kk * 8 + ri * 4 + tri, q : q + 2 * C : 2] = 1
    b = lambda a: np.asarray(a, np.float32).astype(BF16)
    return dict(
        tyf=np.concatenate(split(tyf)),
        tyi=np.concatenate(split(tyi)),
        wxp=np.stack([split(w) for w in wxp]),
        wxi=np.stack([split(w) for w in wxi]),
        px=b(px),
        pxt=b(px.T),
        pab=b(pab.reshape(48 * G, 32 * G)),
        selw=b(selw),
    )


def mm(a, b):
    return jnp.dot(a, b, preferred_element_type=F32)


def mm_nt(a, b):
    return lax.dot_general(a, b, (((1,), (1,)), ((), ())), preferred_element_type=F32)


def hilo(a):
    hi = a.astype(BF16)
    return hi, (a - hi.astype(F32)).astype(BF16)


def mm_tab(tab, x):
    hi, lo = hilo(x)
    return mm(tab[0], hi) + (mm(tab[0], lo) + mm(tab[1], hi))


def iota(shape, dim):
    return lax.broadcasted_iota(jnp.int32, shape, dim)


def onehot(cond):
    return jnp.where(cond, 1.0, 0.0).astype(BF16)


def lane_code(shape, stride):
    row = iota(shape, 0)
    q = row & 127
    kk = jnp.where(q >= 80, 2, jnp.where(q >= 40, 1, 0))
    c = (row >> 7) * 10 + ((q - 40 * kk) >> 2)
    return jnp.where(q < 120, (kk * stride + c) * 4 + (q & 3), -1)


def gelu_parts(h):
    k = math.sqrt(2.0 / math.pi)
    hh = h * h
    u = 0.5 * jnp.tanh(h * (k + (0.044715 * k) * hh)) + 0.5
    value = h * u
    slope = u + (value * (1.0 - u)) * (2.0 * k + (6.0 * 0.044715 * k) * hh)
    return value, slope


def kernel(
    G, D, f_hbm, tyf_hbm, w_hbm, mix_hbm, selw_hbm, wxp_hbm, pab_hbm, px_hbm, pxt_hbm, wxi_hbm, cot_hbm, tyi_hbm,
    out_ref, sg_ref, mg_ref,
    f_ref, tyf_ref, w_ref, mix_ref, selw_ref, wxp, pab_ref, px_ref, pxt_ref, wxi, cot, tyi, a3, b3, mixed, mixpad, backb,
    sx1, rx1, sx3, rx3, sy1, ry1, sy3, ry3, sy2, ry2, sx2, rx2,
    ws, rw, wst, rq, bc, ohg, gi, sspec, rspec, sgs, rgs, stt,
    mgx_s, mgx_r, mgy_s, mgy_r, part, rsbuf, agbuf, agsrc,
    ready, go, lsem, bx_s, bx_r, by_s, by_r, dp_s, dp_r,
):
    rows = C * 4 * G
    planes = 4 * G
    gx = lax.axis_index("gx")
    gy = lax.axis_index("gy")
    dp = lax.axis_index("dp")
    tpr = max(1, -(-TILES // D))
    nred = TILES // tpr

    hrows = rows // 2
    chunk = 160 if hrows % 160 == 0 else hrows
    chunks = [[h * hrows + r for r in range(0, hrows, chunk)] for h in range(2)]
    starts = chunks[0] + chunks[1]
    n = chunk
    pieces = [(f_hbm.at[pl.ds(r0, n)], f_ref.at[pl.ds(r0, n)]) for r0 in starts]
    pieces.insert(0, (tyf_hbm, tyf_ref))
    pieces += [(w_hbm, w_ref), (selw_hbm, selw_ref), (mix_hbm, mix_ref), (wxp_hbm.at[gy], wxp)]
    pieces += [(pab_hbm, pab_ref), (px_hbm, px_ref), (pxt_hbm, pxt_ref), (wxi_hbm.at[gy], wxi), (cot_hbm, cot), (tyi_hbm, tyi)]
    loads = [pltpu.make_async_copy(src, dst, lsem.at[k]) for k, (src, dst) in enumerate(pieces)]
    for copy in loads[: 1 + len(starts)]:
        copy.start()

    barrier = pltpu.get_barrier_semaphore()
    for k in range(1, G):
        pl.semaphore_signal(barrier, inc=1, device_id={"gx": lax.rem(gx + k, G)}, device_id_type=MESH)
    for k in range(1, GY):
        pl.semaphore_signal(barrier, inc=1, device_id={"gy": lax.rem(gy + k, GY)}, device_id_type=MESH)

    @pl.when(dp == 0)
    def _():
        for k in range(1, D):
            pl.semaphore_signal(barrier, inc=1, device_id={"dp": k}, device_id_type=MESH)


    for copy in loads[1 + len(starts) :]:
        copy.start()
    late = dict(zip(("w", "selw", "mix", "wxp", "pab", "px", "pxt", "wxi", "cot", "tyi"), loads[1 + len(starts) :]))

    pending = []

    def exchange(axis, size, me, src_of, dst, sems_s, sems_r, ex):
        def one(k):
            peer = lax.rem(me + k, size)
            return pltpu.make_async_remote_copy(
                src_ref=src_of(peer),
                dst_ref=dst.at[me],
                send_sem=sems_s.at[ex, k],
                recv_sem=sems_r.at[ex, k],
                device_id={axis: peer},
                device_id_type=MESH,
            )

        copies = [one(k) for k in sorted(range(1, size), key=lambda k: abs(2 * k - size))]
        for copy in copies:
            copy.start()
        pending.extend(copies)

        def wait():
            for copy in copies:
                copy.wait_recv()

        return wait

    def ex_x(src_of, dst, ex):
        return exchange("gx", G, gx, src_of, dst, bx_s, bx_r, ex)

    def ex_y(src_of, dst, ex):
        return exchange("gy", GY, gy, src_of, dst, by_s, by_r, ex)

    rest = jnp.zeros((8, 128), F32)

    def part_of(h, kk, r0):
        return pl.ds((h * 3 + kk) * hrows + r0 - h * hrows, n)

    def y_forward(data, h, r0):
        a = mm(jnp.concatenate([data, data], axis=1), tyf_ref[...])
        a3[part_of(h, 0, r0), :] = a
        a3[part_of(h, 1, r0), :] = pltpu.roll(a, 96, 1)
        a3[part_of(h, 2, r0), :] = pltpu.roll(a, 64, 1)

    def to_groups(h, dst):
        for g in range(G):
            block = a3[pl.ds(h * 3 * hrows + g, 120, stride=G), :]
            dst[h, g] = jnp.concatenate([block, rest], axis=0).T[:32]

    def to_planes(value):
        for i in range(4):
            gi[i] = value[:, i * 128 : (i + 1) * 128]

    loads[0].wait()
    wait_x1 = []
    for h in range(2):
        for r0 in chunks[h]:
            loads[1 + starts.index(r0)].wait()
            y_forward(f_ref[r0 : r0 + n, :], h, r0)
        to_groups(h, sx1)
        if h == 0:


            @pl.when(dp == 0)
            def _():
                pl.semaphore_wait(barrier, G - 1 + GY - 1)

            @pl.when(dp != 0)
            def _():
                pl.semaphore_wait(barrier, G - 1 + GY - 1 + 1)
                pl.semaphore_signal(ready, inc=1, device_id={"dp": 0}, device_id_type=MESH)

        wait_x1.append(ex_x(lambda peer: sx1.at[h, peer], rx1.at[h], h))
        rx1[h, gx] = sx1[h, gx]

    late["w"].wait()
    late["selw"].wait()
    wst[...] = jnp.zeros_like(wst)
    for m in range(9):
        wst[m * 48 : m * 48 + 2 * C, 0:C] = w_ref[m].astype(F32).reshape(2 * C, C)
    r = iota((128, 512), 1) & 127
    fifth = lambda r: sum(jnp.where(r >= 20 * k, 1, 0) for k in range(1, 5))
    ohd = onehot((iota((128, 512), 0) == r - 20 * fifth(r)) & (r < 100))
    wexp = mm(wst[...].astype(BF16), ohd)
    lane = iota((48, 512), 1)
    cond = (iota((48, 512), 0) >> 1) == (lane >> 7) * 5 + fifth(lane & 127)
    wparts = [jnp.where(cond, wexp[m * 48 : m * 48 + 48], 0.0) for m in range(9)]
    wmasked = jnp.concatenate(wparts, axis=0).astype(BF16)
    ws[...] = mm(selw_ref[...], wmasked).astype(BF16)
    late["mix"].wait()
    mixpad[...] = jnp.zeros_like(mixpad)
    mixpad[0:C, 0:C] = mix_ref[...].astype(F32)
    mixb = mixpad[...].astype(BF16)
    shift = int(math.log2(planes))
    ecol = onehot((iota((128, rows), 1) >> shift) == iota((128, rows), 0))
    for r0 in starts:
        erow = onehot(((iota((n, 128), 0) + r0) >> shift) == iota((n, 128), 1))
        kron = mm(mm_nt(erow, mixb).astype(BF16), ecol)
        diag = ((iota((n, rows), 0) + r0) & (planes - 1)) == (iota((n, rows), 1) & (planes - 1))
        kron = jnp.where(diag, kron, 0.0).astype(BF16)
        mixed[r0 : r0 + n, :] = mm(kron, f_ref[...])

    lanes = iota((256, 640), 1)
    for q in range(4):
        spot = ((lanes >> 7) + 5 * q) * 4 + (lanes & 3)
        bc[q] = onehot((iota((256, 640), 0) & 127) == spot)
    lanes = iota((128, 640), 1)
    row = (lanes >> 7) * 20 + ((lanes & 127) >> 2)
    ohr = onehot((iota((128, 640), 0) == row) & ((lanes & 127) < 80))
    col = iota((256, 512), 1)
    ohg[0] = onehot(lane_code((256, 512), 24) == (col & 127) * 4 + (col >> 7))
    ohg[1] = onehot(lane_code((256, 512), 20) == (col & 63) * 4 + (col >> 7))

    def x_forward(recv, send, h):
        hi, lo = hilo(recv[h].reshape(32 * G, 128))
        p = mm(wxp[0], hi) + (mm(wxp[0], lo) + mm(wxp[1], hi))
        send[h] = p.astype(send.dtype).reshape(GY, 6 * G, 128)

    def y_sum(recv, h):
        p = [recv[h, k].astype(F32) for k in range(GY)]
        return (p[0] + p[1]) + (p[2] + p[3])

    late["wxp"].wait()
    wait_y1 = []
    for h in range(2):
        wait_x1[h]()
        x_forward(rx1, sy1, h)
        wait_y1.append(ex_y(lambda peer: sy1.at[h, peer], ry1.at[h], h))
        ry1[h, gy] = sy1[h, gy]
        if h == 0:
            wait_w = ex_x(lambda peer: ws, rw, 2)
            rw[gx] = ws[...]

    wait_w()
    late["pab"].wait()
    rab = mm(pab_ref[...], rw[...].reshape(32 * G, 512)).astype(BF16)
    for q in range(4):
        rq[q] = mm(rab[:, q * 128 : (q + 1) * 128], ohr)
    late["px"].wait()
    late["pxt"].wait()

    for h in range(2):
        wait_y1[h]()
    shi, slo = hilo(jnp.concatenate([y_sum(ry1, h) for h in range(2)], axis=1))
    spec = mm(px_ref[...], shi) + mm(px_ref[...], slo)
    sspec[...] = spec.reshape(G, 8, 256)

    low = iota((8 * G, 128), 1) < 40
    turn = lambda a, by: pltpu.roll(a, by % 128, 1) if by % 128 else a
    parts = []
    for kk in range(3):
        h0, h1 = turn(spec[:, :128], -40 * kk), turn(spec[:, 128:], 40 - 40 * kk)
        parts.append(jnp.where(low, h0, h1))
    xx = jnp.concatenate(hilo(jnp.concatenate(parts, axis=0)), axis=1)
    acc = [jnp.zeros((24 * G, 128), F32) for _ in range(2)]
    for q in range(4):
        spread = mm(xx, bc[q])
        for ab in range(2):
            prod = spread * rq[q, ab * 24 * G : (ab + 1) * 24 * G]
            acc[ab] += sum(prod[:, k * 128 : k * 128 + 128] for k in range(5))
    swapped = pltpu.roll(acc[1].reshape(3 * G, 8, 128), 4, 1).reshape(24 * G, 128)
    acc = (acc[0] + swapped).reshape(3, 8 * G, 128)
    wait_y2 = []
    for h in range(2):
        mine = [jnp.where(low if h == 0 else ~low, acc[kk], 0.0) for kk in range(3)]
        vals = sum(turn(mine[kk], 40 * kk - 40 * h) for kk in range(3))
        sy2[h] = mm(pxt_ref[...], vals.astype(BF16)).astype(BF16)
        wait_y2.append(ex_y(lambda peer: sy2.at[h], ry2.at[h], 2 + h))
        ry2[h, gy] = sy2[h]

    @pl.when(dp == 0)
    def _():
        pl.semaphore_wait(ready, D - 1)
        for k in range(1, D):
            pl.semaphore_signal(go, inc=1, device_id={"dp": k}, device_id_type=MESH)

    wait_spec = ex_x(lambda peer: sspec.at[peer], rspec, 3)
    rspec[gx] = sspec[gx]

    late["wxi"].wait()
    wait_x2 = []
    for h in range(2):
        wait_y2[h]()
        v = ry2[h].reshape(24 * G, 128)
        b = mm(wxi[0], v) + mm(wxi[1], v)
        sx2[h] = b.astype(BF16).reshape(G, 32, 128)
        wait_x2.append(ex_x(lambda peer: sx2.at[h, peer], rx2.at[h], 4 + h))
        rx2[h, gx] = sx2[h, gx]

    wait_spec()
    hi, lo = hilo(rspec[...].reshape(8 * G, 256))
    to_planes(mm(hi, ohg[0]) + mm(lo, ohg[0]))
    for tri in range(3):
        block = []
        for i in range(4):
            for ri in range(2):
                block.append(gi[i, pl.ds(ri * 4 + tri, G, stride=8), :])
        block.append(jnp.zeros((128 - 8 * G, 128), F32))
        stt[tri] = jnp.concatenate(block, axis=0).T[:72]

    late["cot"].wait()
    late["tyi"].wait()
    def planes_back(h):
        wait_x2[h]()
        for g in range(G):
            block = jnp.concatenate([rx2[h, g].astype(F32), jnp.zeros((96, 128), F32)], axis=0)
            b3[pl.ds(h * 3 * hrows + g, 120, stride=G), :] = block.T[:120]

    def pointwise(h, r0):
        bb = b3[part_of(h, 0, r0), :]
        bb += pltpu.roll(b3[part_of(h, 1, r0), :], 32, 1)
        bb += pltpu.roll(b3[part_of(h, 2, r0), :], 64, 1)
        bb = bb.astype(BF16)
        pre = mm(jnp.concatenate([bb, bb], axis=1), tyi[...]) + mixed[r0 : r0 + n, :]
        value, slope = gelu_parts(pre)
        out_ref[r0 : r0 + n, :] = value.astype(BF16)
        back = (cot[r0 : r0 + n, :].astype(F32) * slope).astype(BF16)
        backb[r0 : r0 + n, :] = back
        y_forward(back, h, r0)

    wait_x3 = []
    for h in range(2):
        planes_back(h)
        for r0 in chunks[h]:
            pointwise(h, r0)
        to_groups(h, sx3)
        wait_x3.append(ex_x(lambda peer: sx3.at[h, peer], rx3.at[h], 6 + h))
        rx3[h, gx] = sx3[h, gx]

    gmix = jnp.zeros((24, 128), F32)
    ecol_t = onehot((iota((rows, 128), 0) >> shift) == iota((rows, 128), 1))
    for r0 in starts:
        full = mm_nt(f_ref[r0 : r0 + n, :], backb[...])
        diag = ((iota((n, rows), 0) + r0) & (planes - 1)) == (iota((n, rows), 1) & (planes - 1))
        hi, lo = hilo(jnp.where(diag, full, 0.0))
        cols = mm(hi, ecol_t) + mm(lo, ecol_t)
        erow_t = onehot(((iota((24, n), 1) + r0) >> shift) == iota((24, n), 0))
        hi, lo = hilo(cols)
        gmix += mm(erow_t, hi) + mm(erow_t, lo)
    mgx_s[...] = gmix
    mgx_r[gx] = gmix

    wait_y3 = []
    for h in range(2):
        wait_x3[h]()
        x_forward(rx3, sy3, h)
        wait_y3.append(ex_y(lambda peer: sy3.at[h, peer], ry3.at[h], 4 + h))
        ry3[h, gy] = sy3[h, gy]

    wait_mgx = ex_x(lambda peer: mgx_s, mgx_r, 8)
    wait_mgx()
    total = mgx_r[0]
    for k in range(1, G):
        total += mgx_r[k]
    mgy_s[...] = total
    wait_mgy = ex_y(lambda peer: mgy_s, mgy_r, 6)
    mgy_r[gy] = total

    wait_gs = []
    for h in range(2):
        wait_y3[h]()
        ghi, glo = hilo(y_sum(ry3, h))
        sgs[h] = (mm(px_ref[...], ghi) + mm(px_ref[...], glo)).reshape(G, 8, 128)
        wait_gs.append(ex_x(lambda peer: sgs.at[h, peer], rgs.at[h], 9 + h))
        rgs[h, gx] = sgs[h, gx]

    wait_mgy()
    mix_scale = 1.0 / math.sqrt(D * planes * 16 * G * NY)
    part[9:12] = (((mgy_r[0] + mgy_r[1]) + (mgy_r[2] + mgy_r[3])) * mix_scale).reshape(3, 8, 128)

    norm_in = 1.0 / math.sqrt(16 * G * NY)
    norm_out = 1.0 / math.sqrt(36 * G)
    spec_scale = norm_out / norm_in / math.sqrt(D * planes)
    for h in range(2):
        wait_gs[h]()
    hi, lo = hilo(jnp.concatenate([rgs[h].reshape(8 * G, 128) for h in range(2)], axis=1))
    to_planes(mm(hi, ohg[1]) + mm(lo, ohg[1]))
    lane = iota((G, 128), 1)
    lane24 = iota((24, 128), 1) & 63
    for tri in range(3):
        block = []
        for i in range(4):
            g0 = gi[i, pl.ds(tri, G, stride=8), :]
            g1 = gi[i, pl.ds(4 + tri, G, stride=8), :]
            block += [jnp.where(lane < 64, g0, g1), jnp.where(lane < 64, g1, -g0)]
        block.append(jnp.zeros((128 - 8 * G, 128), F32))
        ahi, alo = hilo(stt[tri])
        bhi, blo = hilo(jnp.concatenate(block, axis=0))
        outer = mm(ahi, bhi) + (mm(ahi, blo) + mm(alo, bhi))
        grad = jnp.zeros((24, 128), F32)
        for kk in range(3):
            mine = (lane24 >= 20 * kk) & (lane24 < 20 * kk + 20)
            grad += jnp.where(mine, outer[24 * kk : 24 * kk + 24], 0.0)
        part[3 * tri : 3 * tri + 3] = (grad * spec_scale).reshape(3, 8, 128)

    def rs_copy(k, to):
        return pltpu.make_async_remote_copy(
            src_ref=part.at[pl.ds(to * tpr, tpr)],
            dst_ref=rsbuf.at[dp],
            send_sem=dp_s.at[0, k],
            recv_sem=dp_r.at[0, k],
            device_id={"dp": to},
            device_id_type=MESH,
        )

    def ag_copy(k, to, slot):
        return pltpu.make_async_remote_copy(
            src_ref=agsrc,
            dst_ref=agbuf.at[slot],
            send_sem=dp_s.at[1, k],
            recv_sem=dp_r.at[1, k],
            device_id={"dp": to},
            device_id_type=MESH,
        )

    @pl.when(dp != 0)
    def _():
        pl.semaphore_wait(go, 1)

    far = sorted(range(1, D), key=lambda k: -min(k % 8, 8 - k % 8))
    for k in far:
        to = lax.rem(dp + k, D)

        @pl.when(to < nred)
        def _():
            rs_copy(k, to).start()

    @pl.when(dp < nred)
    def _():
        rsbuf[dp] = part[pl.ds(dp * tpr, tpr)]
        for k in range(1, D):
            rs_copy(k, dp).wait_recv()
        tile = rsbuf[0]
        for k in range(1, D):
            tile += rsbuf[k]
        agsrc[...] = tile
        for k in far:
            ag_copy(k, lax.rem(dp + k, D), dp).start()
        agbuf[dp] = tile

    for copy in pending:
        copy.wait_send()
    for k in range(1, D):
        to = lax.rem(dp + k, D)

        @pl.when(to < nred)
        def _():
            rs_copy(k, to).wait_send()

    for k in range(1, D):
        frm = lax.rem(dp + D - k, D)

        @pl.when(frm < nred)
        def _():
            ag_copy(k, dp, frm).wait_recv()

    final = agbuf[...].reshape(TILES, 8, 128)
    mg_ref[...] = final[9:12].reshape(24, 128)[:C, :C]
    pairs = iota((40, 64), 0) == (iota((40, 64), 1) & 31) * 2 + (iota((40, 64), 1) >> 5)
    pairs = onehot(pairs)
    gap = jnp.zeros((8, 128), F32)
    for tri in range(3):
        block = final[3 * tri : 3 * tri + 3].reshape(24, 128)
        both = jnp.concatenate([block, gap, pltpu.roll(block, 64, 1), gap], axis=0)
        hi, lo = hilo(both)
        both = mm(pairs, hi) + mm(pairs, lo)
        for kk in range(3):
            piece = both if kk == 0 else pltpu.roll(both, 128 - 20 * kk, 1)
            sg_ref[tri * 3 + kk] = piece[:, :C].reshape(C, 2, C)

    @pl.when(dp < nred)
    def _():
        for k in range(1, D):
            ag_copy(k, lax.rem(dp + k, D), dp).wait_send()


def store_kernel(out, sg, mg, out_hbm, sg_hbm, mg_hbm, sems):
    step = out.shape[0] // 4
    pairs = [(sg, sg_hbm), (mg, mg_hbm)]
    pairs += [(out.at[pl.ds(k * step, step)], out_hbm.at[pl.ds(k * step, step)]) for k in range(4)]
    copies = [pltpu.make_async_copy(src, dst, sems.at[k]) for k, (src, dst) in enumerate(pairs)]
    for copy in copies:
        copy.start()
    for copy in copies:
        copy.wait()


def local(G, D, fields, cotangent, mix_weight, spectral_weight):
    rows = C * 4 * G
    cells = XL * NY
    t = tables(G)
    tpr = max(1, -(-TILES // D))
    nred = TILES // tpr
    vm = pl.BlockSpec(memory_space=pltpu.VMEM)
    hbm = pl.BlockSpec(memory_space=pl.ANY)
    V = pltpu.VMEM
    scratch = [
        V((rows, cells), BF16),
        V((2 * cells, 128), BF16),
        V((9, C, 2, C), BF16),
        V((C, C), BF16),
        V((32, 432), BF16),
        V((2, GY * 6 * G, 32 * G), BF16),
        V((48 * G, 32 * G), BF16),
        V((8 * G, 6 * G), BF16),
        V((6 * G, 8 * G), BF16),
        V((2, 32 * G, GY * 6 * G), BF16),
        V((rows, cells), BF16),
        V((256, cells), BF16),
        V((3 * rows, 128), F32),
        V((3 * rows, 128), F32),
        V((rows, cells), F32),
        V((128, 128), F32),
        V((rows, cells), BF16),
        V((2, G, 32, 128), F32),
        V((2, G, 32, 128), F32),
        V((2, G, 32, 128), F32),
        V((2, G, 32, 128), F32),
        V((2, GY, 6 * G, 128), F32),
        V((2, GY, 6 * G, 128), F32),
        V((2, GY, 6 * G, 128), BF16),
        V((2, GY, 6 * G, 128), BF16),
        V((2, 6 * G, 128), BF16),
        V((2, GY, 6 * G, 128), BF16),
        V((2, G, 32, 128), BF16),
        V((2, G, 32, 128), BF16),
        V((32, 512), BF16),
        V((G, 32, 512), BF16),
        V((432, 128), F32),
        V((4, 48 * G, 640), F32),
        V((4, 256, 640), BF16),
        V((2, 256, 512), BF16),
        V((4, 8 * G, 128), F32),
        V((G, 8, 256), F32),
        V((G, 8, 256), F32),
        V((2, G, 8, 128), F32),
        V((2, G, 8, 128), F32),
        V((3, 72, 128), F32),
        V((24, 128), F32),
        V((G, 24, 128), F32),
        V((24, 128), F32),
        V((GY, 24, 128), F32),
        V((TILES, 8, 128), F32),
        V((D, tpr, 8, 128), F32),
        V((nred, tpr, 8, 128), F32),
        V((tpr, 8, 128), F32),
        pltpu.SemaphoreType.REGULAR,
        pltpu.SemaphoreType.REGULAR,
        pltpu.SemaphoreType.DMA((32,)),
        pltpu.SemaphoreType.DMA((11, G)),
        pltpu.SemaphoreType.DMA((11, G)),
        pltpu.SemaphoreType.DMA((7, GY)),
        pltpu.SemaphoreType.DMA((7, GY)),
        pltpu.SemaphoreType.DMA((2, D)),
        pltpu.SemaphoreType.DMA((2, D)),
    ]
    out, sg, mg = pl.pallas_call(
        functools.partial(kernel, G, D),
        out_shape=(
            V((rows, cells), BF16),
            V((9, C, 2, C), F32),
            V((C, C), F32),
        ),
        in_specs=[hbm] * 12,
        out_specs=(vm, vm, vm),
        scratch_shapes=scratch,
        compiler_params=pltpu.CompilerParams(
            collective_id=0, has_side_effects=True, vmem_limit_bytes=60 * 1024 * 1024
        ),
    )(
        fields.reshape(rows, cells),
        t["tyf"],
        spectral_weight.transpose(0, 2, 1, 3),
        mix_weight,
        t["selw"],
        t["wxp"],
        t["pab"],
        t["px"],
        t["pxt"],
        t["wxi"],
        cotangent.reshape(rows, cells),
        t["tyi"],
    )
    out, sg, mg = pl.pallas_call(
        store_kernel,
        out_shape=tuple(jax.ShapeDtypeStruct(a.shape, a.dtype) for a in (out, sg, mg)),
        in_specs=[hbm] * 3,
        out_specs=(hbm,) * 3,
        scratch_shapes=[pltpu.SemaphoreType.DMA((6,))],
        compiler_params=pltpu.CompilerParams(vmem_limit_bytes=1 << 20),
    )(out, sg, mg)
    return out.reshape(fields.shape), sg.transpose(0, 2, 1, 3), mg


def solution(mesh):
    G, D = mesh.shape["gx"], mesh.shape["dp"]
    cells = P("dp", None, None, ("gx", "gy"))
    modes = P(("gx", "gy"), None, None, None)
    return jax.shard_map(
        functools.partial(local, G, D),
        mesh=mesh,
        in_specs=(cells, cells, P(), modes),
        out_specs=(cells, modes, P()),
        check_vma=False,
    )
```

```python
import functools
import math

import jax
import jax.numpy as jnp
import numpy as np
from jax import lax
from jax.experimental import pallas as pl
from jax.experimental.pallas import tpu as pltpu
from jax.sharding import PartitionSpec as P

MESH = pl.DeviceIdType.MESH
F32 = jnp.float32
BF16 = jnp.bfloat16

C = 20
NY = 128
KY = 12
GY = 4
XL = 4
PL_OWN = 4
TILES = 12


def split(table):
    table = np.asarray(table, np.float32)
    hi = table.astype(BF16)
    lo = (table - hi.astype(np.float32)).astype(BF16)
    return np.stack([hi, lo])


@functools.lru_cache(None)
def tables(G):
    nx, kxn = 16 * G, 3 * G
    norm_in = 1.0 / math.sqrt(nx * NY)
    norm_out = 1.0 / math.sqrt(kxn * KY)
    y = np.arange(NY)
    tyf = np.zeros((XL * NY, 128))
    tyi = np.zeros((128, XL * NY))
    for kk in range(3):
        for ks in range(4):
            ang = 2 * np.pi * ((3 * ks + kk) * y % NY) / NY
            for x in range(XL):
                col = kk * 32 + ks * 8 + x * 2
                tyf[x * NY : (x + 1) * NY, col] = np.cos(ang) * norm_in
                tyf[x * NY : (x + 1) * NY, col + 1] = -np.sin(ang) * norm_in
                tyi[col, x * NY : (x + 1) * NY] = np.cos(ang)
                tyi[col + 1, x * NY : (x + 1) * NY] = -np.sin(ang)
    wxp = np.zeros((GY, GY * 6 * G, 32 * G))
    wxi = np.zeros((GY, 32 * G, GY * 6 * G))
    for gy in range(GY):
        for go in range(GY):
            for tri in range(3):
                jj, ks = divmod(3 * go + tri, 4)
                for gq in range(G):
                    j = 3 * gq + jj
                    kx = j if j < kxn // 2 else nx - kxn + j
                    rp = go * 6 * G + gq * 6 + tri * 2
                    for gx in range(G):
                        for x in range(XL):
                            ang = 2 * np.pi * (kx * (4 * (gx * GY + gy) + x) % nx) / nx
                            c, s = np.cos(ang), np.sin(ang)
                            k = gx * 32 + ks * 8 + x * 2
                            wxp[gy, rp, k], wxp[gy, rp, k + 1] = c, s
                            wxp[gy, rp + 1, k], wxp[gy, rp + 1, k + 1] = -s, c
                            wxi[gy, k, rp], wxi[gy, k, rp + 1] = c * norm_out, -s * norm_out
                            wxi[gy, k + 1, rp], wxi[gy, k + 1, rp + 1] = s * norm_out, c * norm_out
    px = np.zeros((8 * G, 6 * G))
    pab = np.zeros((2, 3, 8 * G, 32 * G))
    for gq in range(G):
        for ri in range(2):
            for tri in range(3):
                row = gq * 8 + ri * 4 + tri
                px[row, gq * 6 + tri * 2 + ri] = 1
                for kk in range(3):
                    src = gq * 32 + kk * 8
                    pab[0, kk, row, src + tri] = 1
                    pab[1, kk, row, src + 4 + tri] = 1 if ri == 0 else -1
    selw = np.zeros((32, 18 * 24))
    for kk in range(3):
        for ri in range(2):
            for tri in range(3):
                q = (tri * 3 + kk) * 48 + ri
                selw[kk * 8 + ri * 4 + tri, q : q + 2 * C : 2] = 1
    b = lambda a: np.asarray(a, np.float32).astype(BF16)
    return dict(
        tyf=np.concatenate(split(tyf)),
        tyi=np.concatenate(split(tyi)),
        wxp=np.stack([split(w) for w in wxp]),
        wxi=np.stack([split(w) for w in wxi]),
        px=b(px),
        pxt=b(px.T),
        pab=b(pab.reshape(48 * G, 32 * G)),
        selw=b(selw),
    )


def mm(a, b):
    return jnp.dot(a, b, preferred_element_type=F32)


def mm_nt(a, b):
    return lax.dot_general(a, b, (((1,), (1,)), ((), ())), preferred_element_type=F32)


def hilo(a):
    hi = a.astype(BF16)
    return hi, (a - hi.astype(F32)).astype(BF16)


def mm_tab(tab, x):
    hi, lo = hilo(x)
    return mm(tab[0], hi) + (mm(tab[0], lo) + mm(tab[1], hi))


def iota(shape, dim):
    return lax.broadcasted_iota(jnp.int32, shape, dim)


def onehot(cond):
    return jnp.where(cond, 1.0, 0.0).astype(BF16)


def lane_code(shape, stride):
    row = iota(shape, 0)
    q = row & 127
    kk = jnp.where(q >= 80, 2, jnp.where(q >= 40, 1, 0))
    c = (row >> 7) * 10 + ((q - 40 * kk) >> 2)
    return jnp.where(q < 120, (kk * stride + c) * 4 + (q & 3), -1)


def gelu_parts(h):
    k = math.sqrt(2.0 / math.pi)
    hh = h * h
    u = 0.5 * jnp.tanh(h * (k + (0.044715 * k) * hh)) + 0.5
    value = h * u
    slope = u + (value * (1.0 - u)) * (2.0 * k + (6.0 * 0.044715 * k) * hh)
    return value, slope


def kernel(
    G, D, f_hbm, tyf_hbm, w_hbm, mix_hbm, selw_hbm, wxp_hbm, pab_hbm, px_hbm, pxt_hbm, wxi_hbm, cot_hbm, tyi_hbm,
    out_ref, sg_ref, mg_ref,
    f_ref, tyf_ref, w_ref, mix_ref, selw_ref, wxp, pab_ref, px_ref, pxt_ref, wxi, cot, tyi, a3, b3, mixed, mixpad, backb,
    sx1, rx1, sx3, rx3, sy1, ry1, sy3, ry3, sy2, ry2, sx2, rx2,
    ws, rw, wst, rq, bc, ohg, gi, sspec, rspec, sgs, rgs, stt,
    mgx_s, mgx_r, mgy_s, mgy_r, part, rsbuf, agbuf, agsrc,
    ready, go, lsem, bx_s, bx_r, by_s, by_r, dp_s, dp_r,
):
    rows = C * 4 * G
    planes = 4 * G
    gx = lax.axis_index("gx")
    gy = lax.axis_index("gy")
    dp = lax.axis_index("dp")
    tpr = max(1, -(-TILES // D))
    nred = TILES // tpr

    hrows = rows // 2
    chunk = hrows
    chunks = [[h * hrows + r for r in range(0, hrows, chunk)] for h in range(2)]
    starts = chunks[0] + chunks[1]
    n = chunk
    pieces = [(f_hbm.at[pl.ds(r0, n)], f_ref.at[pl.ds(r0, n)]) for r0 in starts]
    pieces.insert(0, (tyf_hbm, tyf_ref))
    pieces += [(w_hbm, w_ref), (selw_hbm, selw_ref), (mix_hbm, mix_ref), (wxp_hbm.at[gy], wxp)]
    pieces += [(pab_hbm, pab_ref), (px_hbm, px_ref), (pxt_hbm, pxt_ref), (wxi_hbm.at[gy], wxi), (cot_hbm, cot), (tyi_hbm, tyi)]
    loads = [pltpu.make_async_copy(src, dst, lsem.at[k]) for k, (src, dst) in enumerate(pieces)]
    for copy in loads[: 1 + len(starts)]:
        copy.start()

    barrier = pltpu.get_barrier_semaphore()
    for k in range(1, G):
        pl.semaphore_signal(barrier, inc=1, device_id={"gx": lax.rem(gx + k, G)}, device_id_type=MESH)
    for k in range(1, GY):
        pl.semaphore_signal(barrier, inc=1, device_id={"gy": lax.rem(gy + k, GY)}, device_id_type=MESH)

    @pl.when(dp == 0)
    def _():
        for k in range(1, D):
            pl.semaphore_signal(barrier, inc=1, device_id={"dp": k}, device_id_type=MESH)


    for copy in loads[1 + len(starts) :]:
        copy.start()
    late = dict(zip(("w", "selw", "mix", "wxp", "pab", "px", "pxt", "wxi", "cot", "tyi"), loads[1 + len(starts) :]))

    pending = []

    def exchange(axis, size, me, src_of, dst, sems_s, sems_r, ex):
        def one(k):
            peer = lax.rem(me + k, size)
            return pltpu.make_async_remote_copy(
                src_ref=src_of(peer),
                dst_ref=dst.at[me],
                send_sem=sems_s.at[ex, k],
                recv_sem=sems_r.at[ex, k],
                device_id={axis: peer},
                device_id_type=MESH,
            )

        copies = [one(k) for k in sorted(range(1, size), key=lambda k: abs(2 * k - size))]
        for copy in copies:
            copy.start()
        pending.extend(copies)

        def wait():
            for copy in copies:
                copy.wait_recv()

        return wait

    def ex_x(src_of, dst, ex):
        return exchange("gx", G, gx, src_of, dst, bx_s, bx_r, ex)

    def ex_y(src_of, dst, ex):
        return exchange("gy", GY, gy, src_of, dst, by_s, by_r, ex)

    rest = jnp.zeros((8, 128), F32)

    def part_of(h, kk, r0):
        return pl.ds((h * 3 + kk) * hrows + r0 - h * hrows, n)

    def y_forward(data, h, r0):
        a = mm(jnp.concatenate([data, data], axis=1), tyf_ref[...])
        a3[part_of(h, 0, r0), :] = a
        a3[part_of(h, 1, r0), :] = pltpu.roll(a, 96, 1)
        a3[part_of(h, 2, r0), :] = pltpu.roll(a, 64, 1)

    def to_groups(h, dst):
        for g in range(G):
            block = a3[pl.ds(h * 3 * hrows + g, 120, stride=G), :]
            dst[h, g] = jnp.concatenate([block, rest], axis=0).T[:32]

    def to_planes(value):
        for i in range(4):
            gi[i] = value[:, i * 128 : (i + 1) * 128]

    loads[0].wait()
    wait_x1 = []
    for h in range(2):
        for r0 in chunks[h]:
            loads[1 + starts.index(r0)].wait()
            y_forward(f_ref[r0 : r0 + n, :], h, r0)
        to_groups(h, sx1)
        if h == 0:


            @pl.when(dp == 0)
            def _():
                pl.semaphore_wait(barrier, G - 1 + GY - 1)

            @pl.when(dp != 0)
            def _():
                pl.semaphore_wait(barrier, G - 1 + GY - 1 + 1)
                pl.semaphore_signal(ready, inc=1, device_id={"dp": 0}, device_id_type=MESH)

        wait_x1.append(ex_x(lambda peer: sx1.at[h, peer], rx1.at[h], h))
        rx1[h, gx] = sx1[h, gx]

    late["w"].wait()
    late["selw"].wait()
    wst[...] = jnp.zeros_like(wst)
    for m in range(9):
        wst[m * 48 : m * 48 + 2 * C, 0:C] = w_ref[m].astype(F32).reshape(2 * C, C)
    r = iota((128, 512), 1) & 127
    fifth = lambda r: sum(jnp.where(r >= 20 * k, 1, 0) for k in range(1, 5))
    ohd = onehot((iota((128, 512), 0) == r - 20 * fifth(r)) & (r < 100))
    wexp = mm(wst[...].astype(BF16), ohd)
    lane = iota((48, 512), 1)
    cond = (iota((48, 512), 0) >> 1) == (lane >> 7) * 5 + fifth(lane & 127)
    wparts = [jnp.where(cond, wexp[m * 48 : m * 48 + 48], 0.0) for m in range(9)]
    wmasked = jnp.concatenate(wparts, axis=0).astype(BF16)
    ws[...] = mm(selw_ref[...], wmasked).astype(BF16)
    late["mix"].wait()
    mixpad[...] = jnp.zeros_like(mixpad)
    mixpad[0:C, 0:C] = mix_ref[...].astype(F32)
    mixb = mixpad[...].astype(BF16)
    shift = int(math.log2(planes))
    ecol = onehot((iota((128, rows), 1) >> shift) == iota((128, rows), 0))
    for r0 in starts:
        erow = onehot(((iota((n, 128), 0) + r0) >> shift) == iota((n, 128), 1))
        kron = mm(mm_nt(erow, mixb).astype(BF16), ecol)
        diag = ((iota((n, rows), 0) + r0) & (planes - 1)) == (iota((n, rows), 1) & (planes - 1))
        kron = jnp.where(diag, kron, 0.0).astype(BF16)
        mixed[r0 : r0 + n, :] = mm(kron, f_ref[...])

    lanes = iota((256, 640), 1)
    for q in range(4):
        spot = ((lanes >> 7) + 5 * q) * 4 + (lanes & 3)
        bc[q] = onehot((iota((256, 640), 0) & 127) == spot)
    lanes = iota((128, 640), 1)
    row = (lanes >> 7) * 20 + ((lanes & 127) >> 2)
    ohr = onehot((iota((128, 640), 0) == row) & ((lanes & 127) < 80))
    col = iota((256, 512), 1)
    ohg[0] = onehot(lane_code((256, 512), 24) == (col & 127) * 4 + (col >> 7))
    ohg[1] = onehot(lane_code((256, 512), 20) == (col & 63) * 4 + (col >> 7))

    def x_forward(recv, send, h):
        hi, lo = hilo(recv[h].reshape(32 * G, 128))
        p = mm(wxp[0], hi) + (mm(wxp[0], lo) + mm(wxp[1], hi))
        send[h] = p.astype(send.dtype).reshape(GY, 6 * G, 128)

    def y_sum(recv, h):
        p = [recv[h, k].astype(F32) for k in range(GY)]
        return (p[0] + p[1]) + (p[2] + p[3])

    late["wxp"].wait()
    wait_y1 = []
    for h in range(2):
        wait_x1[h]()
        x_forward(rx1, sy1, h)
        wait_y1.append(ex_y(lambda peer: sy1.at[h, peer], ry1.at[h], h))
        ry1[h, gy] = sy1[h, gy]
        if h == 0:
            wait_w = ex_x(lambda peer: ws, rw, 2)
            rw[gx] = ws[...]

    wait_w()
    late["pab"].wait()
    rab = mm(pab_ref[...], rw[...].reshape(32 * G, 512)).astype(BF16)
    for q in range(4):
        rq[q] = mm(rab[:, q * 128 : (q + 1) * 128], ohr)
    late["px"].wait()
    late["pxt"].wait()

    for h in range(2):
        wait_y1[h]()
    shi, slo = hilo(jnp.concatenate([y_sum(ry1, h) for h in range(2)], axis=1))
    spec = mm(px_ref[...], shi) + mm(px_ref[...], slo)
    sspec[...] = spec.reshape(G, 8, 256)

    low = iota((8 * G, 128), 1) < 40
    turn = lambda a, by: pltpu.roll(a, by % 128, 1) if by % 128 else a
    parts = []
    for kk in range(3):
        h0, h1 = turn(spec[:, :128], -40 * kk), turn(spec[:, 128:], 40 - 40 * kk)
        parts.append(jnp.where(low, h0, h1))
    xx = jnp.concatenate(hilo(jnp.concatenate(parts, axis=0)), axis=1)
    acc = [jnp.zeros((24 * G, 128), F32) for _ in range(2)]
    for q in range(4):
        spread = mm(xx, bc[q])
        for ab in range(2):
            prod = spread * rq[q, ab * 24 * G : (ab + 1) * 24 * G]
            acc[ab] += sum(prod[:, k * 128 : k * 128 + 128] for k in range(5))
    swapped = pltpu.roll(acc[1].reshape(3 * G, 8, 128), 4, 1).reshape(24 * G, 128)
    acc = (acc[0] + swapped).reshape(3, 8 * G, 128)
    wait_y2 = []
    for h in range(2):
        mine = [jnp.where(low if h == 0 else ~low, acc[kk], 0.0) for kk in range(3)]
        vals = sum(turn(mine[kk], 40 * kk - 40 * h) for kk in range(3))
        sy2[h] = mm(pxt_ref[...], vals.astype(BF16)).astype(BF16)
        wait_y2.append(ex_y(lambda peer: sy2.at[h], ry2.at[h], 2 + h))
        ry2[h, gy] = sy2[h]

    @pl.when(dp == 0)
    def _():
        pl.semaphore_wait(ready, D - 1)
        for k in range(1, D):
            pl.semaphore_signal(go, inc=1, device_id={"dp": k}, device_id_type=MESH)

    wait_spec = ex_x(lambda peer: sspec.at[peer], rspec, 3)
    rspec[gx] = sspec[gx]

    late["wxi"].wait()
    wait_x2 = []
    for h in range(2):
        wait_y2[h]()
        v = ry2[h].reshape(24 * G, 128)
        b = mm(wxi[0], v) + mm(wxi[1], v)
        sx2[h] = b.astype(BF16).reshape(G, 32, 128)
        wait_x2.append(ex_x(lambda peer: sx2.at[h, peer], rx2.at[h], 4 + h))
        rx2[h, gx] = sx2[h, gx]

    wait_spec()
    hi, lo = hilo(rspec[...].reshape(8 * G, 256))
    to_planes(mm(hi, ohg[0]) + mm(lo, ohg[0]))
    for tri in range(3):
        block = []
        for i in range(4):
            for ri in range(2):
                block.append(gi[i, pl.ds(ri * 4 + tri, G, stride=8), :])
        block.append(jnp.zeros((128 - 8 * G, 128), F32))
        stt[tri] = jnp.concatenate(block, axis=0).T[:72]

    late["cot"].wait()
    late["tyi"].wait()
    def planes_back(h):
        wait_x2[h]()
        for g in range(G):
            block = jnp.concatenate([rx2[h, g].astype(F32), jnp.zeros((96, 128), F32)], axis=0)
            b3[pl.ds(h * 3 * hrows + g, 120, stride=G), :] = block.T[:120]

    def pointwise(h, r0):
        bb = b3[part_of(h, 0, r0), :]
        bb += pltpu.roll(b3[part_of(h, 1, r0), :], 32, 1)
        bb += pltpu.roll(b3[part_of(h, 2, r0), :], 64, 1)
        bb = bb.astype(BF16)
        pre = mm(jnp.concatenate([bb, bb], axis=1), tyi[...]) + mixed[r0 : r0 + n, :]
        value, slope = gelu_parts(pre)
        out_ref[r0 : r0 + n, :] = value.astype(BF16)
        back = (cot[r0 : r0 + n, :].astype(F32) * slope).astype(BF16)
        backb[r0 : r0 + n, :] = back
        y_forward(back, h, r0)

    wait_x3 = []
    for h in range(2):
        planes_back(h)
        for r0 in chunks[h]:
            pointwise(h, r0)
        to_groups(h, sx3)
        wait_x3.append(ex_x(lambda peer: sx3.at[h, peer], rx3.at[h], 6 + h))
        rx3[h, gx] = sx3[h, gx]

    gmix = jnp.zeros((24, 128), F32)
    ecol_t = onehot((iota((rows, 128), 0) >> shift) == iota((rows, 128), 1))
    for r0 in starts:
        full = mm_nt(f_ref[r0 : r0 + n, :], backb[...])
        diag = ((iota((n, rows), 0) + r0) & (planes - 1)) == (iota((n, rows), 1) & (planes - 1))
        hi, lo = hilo(jnp.where(diag, full, 0.0))
        cols = mm(hi, ecol_t) + mm(lo, ecol_t)
        erow_t = onehot(((iota((24, n), 1) + r0) >> shift) == iota((24, n), 0))
        hi, lo = hilo(cols)
        gmix += mm(erow_t, hi) + mm(erow_t, lo)
    mgx_s[...] = gmix
    mgx_r[gx] = gmix

    wait_y3 = []
    for h in range(2):
        wait_x3[h]()
        x_forward(rx3, sy3, h)
        wait_y3.append(ex_y(lambda peer: sy3.at[h, peer], ry3.at[h], 4 + h))
        ry3[h, gy] = sy3[h, gy]

    wait_mgx = ex_x(lambda peer: mgx_s, mgx_r, 8)
    wait_mgx()
    total = mgx_r[0]
    for k in range(1, G):
        total += mgx_r[k]
    mgy_s[...] = total
    wait_mgy = ex_y(lambda peer: mgy_s, mgy_r, 6)
    mgy_r[gy] = total

    wait_gs = []
    for h in range(2):
        wait_y3[h]()
        ghi, glo = hilo(y_sum(ry3, h))
        sgs[h] = (mm(px_ref[...], ghi) + mm(px_ref[...], glo)).reshape(G, 8, 128)
        wait_gs.append(ex_x(lambda peer: sgs.at[h, peer], rgs.at[h], 9 + h))
        rgs[h, gx] = sgs[h, gx]

    wait_mgy()
    mix_scale = 1.0 / math.sqrt(D * planes * 16 * G * NY)
    part[9:12] = (((mgy_r[0] + mgy_r[1]) + (mgy_r[2] + mgy_r[3])) * mix_scale).reshape(3, 8, 128)

    norm_in = 1.0 / math.sqrt(16 * G * NY)
    norm_out = 1.0 / math.sqrt(36 * G)
    spec_scale = norm_out / norm_in / math.sqrt(D * planes)
    for h in range(2):
        wait_gs[h]()
    hi, lo = hilo(jnp.concatenate([rgs[h].reshape(8 * G, 128) for h in range(2)], axis=1))
    to_planes(mm(hi, ohg[1]) + mm(lo, ohg[1]))
    lane = iota((G, 128), 1)
    lane24 = iota((24, 128), 1) & 63
    for tri in range(3):
        block = []
        for i in range(4):
            g0 = gi[i, pl.ds(tri, G, stride=8), :]
            g1 = gi[i, pl.ds(4 + tri, G, stride=8), :]
            block += [jnp.where(lane < 64, g0, g1), jnp.where(lane < 64, g1, -g0)]
        block.append(jnp.zeros((128 - 8 * G, 128), F32))
        ahi, alo = hilo(stt[tri])
        bhi, blo = hilo(jnp.concatenate(block, axis=0))
        outer = mm(ahi, bhi) + (mm(ahi, blo) + mm(alo, bhi))
        grad = jnp.zeros((24, 128), F32)
        for kk in range(3):
            mine = (lane24 >= 20 * kk) & (lane24 < 20 * kk + 20)
            grad += jnp.where(mine, outer[24 * kk : 24 * kk + 24], 0.0)
        part[3 * tri : 3 * tri + 3] = (grad * spec_scale).reshape(3, 8, 128)

    def rs_copy(k, to):
        return pltpu.make_async_remote_copy(
            src_ref=part.at[pl.ds(to * tpr, tpr)],
            dst_ref=rsbuf.at[dp],
            send_sem=dp_s.at[0, k],
            recv_sem=dp_r.at[0, k],
            device_id={"dp": to},
            device_id_type=MESH,
        )

    def ag_copy(k, to, slot):
        return pltpu.make_async_remote_copy(
            src_ref=agsrc,
            dst_ref=agbuf.at[slot],
            send_sem=dp_s.at[1, k],
            recv_sem=dp_r.at[1, k],
            device_id={"dp": to},
            device_id_type=MESH,
        )

    @pl.when(dp != 0)
    def _():
        pl.semaphore_wait(go, 1)

    far = sorted(range(1, D), key=lambda k: -min(k % 8, 8 - k % 8))
    for k in far:
        to = lax.rem(dp + k, D)

        @pl.when(to < nred)
        def _():
            rs_copy(k, to).start()

    @pl.when(dp < nred)
    def _():
        rsbuf[dp] = part[pl.ds(dp * tpr, tpr)]
        for k in range(1, D):
            rs_copy(k, dp).wait_recv()
        tile = rsbuf[0]
        for k in range(1, D):
            tile += rsbuf[k]
        agsrc[...] = tile
        for k in far:
            ag_copy(k, lax.rem(dp + k, D), dp).start()
        agbuf[dp] = tile

    for copy in pending:
        copy.wait_send()
    for k in range(1, D):
        to = lax.rem(dp + k, D)

        @pl.when(to < nred)
        def _():
            rs_copy(k, to).wait_send()

    for k in range(1, D):
        frm = lax.rem(dp + D - k, D)

        @pl.when(frm < nred)
        def _():
            ag_copy(k, dp, frm).wait_recv()

    final = agbuf[...].reshape(TILES, 8, 128)
    mg_ref[...] = final[9:12].reshape(24, 128)[:C, :C]
    pairs = iota((40, 64), 0) == (iota((40, 64), 1) & 31) * 2 + (iota((40, 64), 1) >> 5)
    pairs = onehot(pairs)
    gap = jnp.zeros((8, 128), F32)
    for tri in range(3):
        block = final[3 * tri : 3 * tri + 3].reshape(24, 128)
        both = jnp.concatenate([block, gap, pltpu.roll(block, 64, 1), gap], axis=0)
        hi, lo = hilo(both)
        both = mm(pairs, hi) + mm(pairs, lo)
        for kk in range(3):
            piece = both if kk == 0 else pltpu.roll(both, 128 - 20 * kk, 1)
            sg_ref[tri * 3 + kk] = piece[:, :C].reshape(C, 2, C)

    @pl.when(dp < nred)
    def _():
        for k in range(1, D):
            ag_copy(k, lax.rem(dp + k, D), dp).wait_send()


def store_kernel(out, sg, mg, out_hbm, sg_hbm, mg_hbm, sems):
    step = out.shape[0] // 4
    pairs = [(sg, sg_hbm), (mg, mg_hbm)]
    pairs += [(out.at[pl.ds(k * step, step)], out_hbm.at[pl.ds(k * step, step)]) for k in range(4)]
    copies = [pltpu.make_async_copy(src, dst, sems.at[k]) for k, (src, dst) in enumerate(pairs)]
    for copy in copies:
        copy.start()
    for copy in copies:
        copy.wait()


def local(G, D, fields, cotangent, mix_weight, spectral_weight):
    rows = C * 4 * G
    cells = XL * NY
    t = tables(G)
    tpr = max(1, -(-TILES // D))
    nred = TILES // tpr
    vm = pl.BlockSpec(memory_space=pltpu.VMEM)
    hbm = pl.BlockSpec(memory_space=pl.ANY)
    V = pltpu.VMEM
    scratch = [
        V((rows, cells), BF16),
        V((2 * cells, 128), BF16),
        V((9, C, 2, C), BF16),
        V((C, C), BF16),
        V((32, 432), BF16),
        V((2, GY * 6 * G, 32 * G), BF16),
        V((48 * G, 32 * G), BF16),
        V((8 * G, 6 * G), BF16),
        V((6 * G, 8 * G), BF16),
        V((2, 32 * G, GY * 6 * G), BF16),
        V((rows, cells), BF16),
        V((256, cells), BF16),
        V((3 * rows, 128), F32),
        V((3 * rows, 128), F32),
        V((rows, cells), F32),
        V((128, 128), F32),
        V((rows, cells), BF16),
        V((2, G, 32, 128), F32),
        V((2, G, 32, 128), F32),
        V((2, G, 32, 128), F32),
        V((2, G, 32, 128), F32),
        V((2, GY, 6 * G, 128), F32),
        V((2, GY, 6 * G, 128), F32),
        V((2, GY, 6 * G, 128), BF16),
        V((2, GY, 6 * G, 128), BF16),
        V((2, 6 * G, 128), BF16),
        V((2, GY, 6 * G, 128), BF16),
        V((2, G, 32, 128), BF16),
        V((2, G, 32, 128), BF16),
        V((32, 512), BF16),
        V((G, 32, 512), BF16),
        V((432, 128), F32),
        V((4, 48 * G, 640), F32),
        V((4, 256, 640), BF16),
        V((2, 256, 512), BF16),
        V((4, 8 * G, 128), F32),
        V((G, 8, 256), F32),
        V((G, 8, 256), F32),
        V((2, G, 8, 128), F32),
        V((2, G, 8, 128), F32),
        V((3, 72, 128), F32),
        V((24, 128), F32),
        V((G, 24, 128), F32),
        V((24, 128), F32),
        V((GY, 24, 128), F32),
        V((TILES, 8, 128), F32),
        V((D, tpr, 8, 128), F32),
        V((nred, tpr, 8, 128), F32),
        V((tpr, 8, 128), F32),
        pltpu.SemaphoreType.REGULAR,
        pltpu.SemaphoreType.REGULAR,
        pltpu.SemaphoreType.DMA((32,)),
        pltpu.SemaphoreType.DMA((11, G)),
        pltpu.SemaphoreType.DMA((11, G)),
        pltpu.SemaphoreType.DMA((7, GY)),
        pltpu.SemaphoreType.DMA((7, GY)),
        pltpu.SemaphoreType.DMA((2, D)),
        pltpu.SemaphoreType.DMA((2, D)),
    ]
    out, sg, mg = pl.pallas_call(
        functools.partial(kernel, G, D),
        out_shape=(
            V((rows, cells), BF16),
            V((9, C, 2, C), F32),
            V((C, C), F32),
        ),
        in_specs=[hbm] * 12,
        out_specs=(vm, vm, vm),
        scratch_shapes=scratch,
        compiler_params=pltpu.CompilerParams(
            collective_id=0, has_side_effects=True, vmem_limit_bytes=60 * 1024 * 1024
        ),
    )(
        fields.reshape(rows, cells),
        t["tyf"],
        spectral_weight.transpose(0, 2, 1, 3),
        mix_weight,
        t["selw"],
        t["wxp"],
        t["pab"],
        t["px"],
        t["pxt"],
        t["wxi"],
        cotangent.reshape(rows, cells),
        t["tyi"],
    )
    out, sg, mg = pl.pallas_call(
        store_kernel,
        out_shape=tuple(jax.ShapeDtypeStruct(a.shape, a.dtype) for a in (out, sg, mg)),
        in_specs=[hbm] * 3,
        out_specs=(hbm,) * 3,
        scratch_shapes=[pltpu.SemaphoreType.DMA((6,))],
        compiler_params=pltpu.CompilerParams(vmem_limit_bytes=1 << 20),
    )(out, sg, mg)
    return out.reshape(fields.shape), sg.transpose(0, 2, 1, 3), mg


def solution(mesh):
    G, D = mesh.shape["gx"], mesh.shape["dp"]
    cells = P("dp", None, None, ("gx", "gy"))
    modes = P(("gx", "gy"), None, None, None)
    return jax.shard_map(
        functools.partial(local, G, D),
        mesh=mesh,
        in_specs=(cells, cells, P(), modes),
        out_specs=(cells, modes, P()),
        check_vma=False,
    )
```

```python
import functools
import math

import jax
import jax.numpy as jnp
import numpy as np
from jax import lax
from jax.experimental import pallas as pl
from jax.experimental.pallas import tpu as pltpu
from jax.sharding import PartitionSpec as P

MESH = pl.DeviceIdType.MESH
F32 = jnp.float32
BF16 = jnp.bfloat16

C = 20
NY = 128
KY = 12
GY = 4
XL = 4
PL_OWN = 4
TILES = 12


def split(table):
    table = np.asarray(table, np.float32)
    hi = table.astype(BF16)
    lo = (table - hi.astype(np.float32)).astype(BF16)
    return np.stack([hi, lo])


@functools.lru_cache(None)
def tables(G):
    nx, kxn = 16 * G, 3 * G
    norm_in = 1.0 / math.sqrt(nx * NY)
    norm_out = 1.0 / math.sqrt(kxn * KY)
    y = np.arange(NY)
    tyf = np.zeros((XL * NY, 128))
    tyi = np.zeros((128, XL * NY))
    for kk in range(3):
        for ks in range(4):
            ang = 2 * np.pi * ((3 * ks + kk) * y % NY) / NY
            for x in range(XL):
                col = kk * 32 + ks * 8 + x * 2
                tyf[x * NY : (x + 1) * NY, col] = np.cos(ang) * norm_in
                tyf[x * NY : (x + 1) * NY, col + 1] = -np.sin(ang) * norm_in
                tyi[col, x * NY : (x + 1) * NY] = np.cos(ang)
                tyi[col + 1, x * NY : (x + 1) * NY] = -np.sin(ang)
    wxp = np.zeros((GY, GY * 6 * G, 32 * G))
    wxi = np.zeros((GY, 32 * G, GY * 6 * G))
    for gy in range(GY):
        for go in range(GY):
            for tri in range(3):
                jj, ks = divmod(3 * go + tri, 4)
                for gq in range(G):
                    j = 3 * gq + jj
                    kx = j if j < kxn // 2 else nx - kxn + j
                    rp = go * 6 * G + gq * 6 + tri * 2
                    for gx in range(G):
                        for x in range(XL):
                            ang = 2 * np.pi * (kx * (4 * (gx * GY + gy) + x) % nx) / nx
                            c, s = np.cos(ang), np.sin(ang)
                            k = gx * 32 + ks * 8 + x * 2
                            wxp[gy, rp, k], wxp[gy, rp, k + 1] = c, s
                            wxp[gy, rp + 1, k], wxp[gy, rp + 1, k + 1] = -s, c
                            wxi[gy, k, rp], wxi[gy, k, rp + 1] = c * norm_out, -s * norm_out
                            wxi[gy, k + 1, rp], wxi[gy, k + 1, rp + 1] = s * norm_out, c * norm_out
    px = np.zeros((8 * G, 6 * G))
    pab = np.zeros((2, 3, 8 * G, 32 * G))
    for gq in range(G):
        for ri in range(2):
            for tri in range(3):
                row = gq * 8 + ri * 4 + tri
                px[row, gq * 6 + tri * 2 + ri] = 1
                for kk in range(3):
                    src = gq * 32 + kk * 8
                    pab[0, kk, row, src + tri] = 1
                    pab[1, kk, row, src + 4 + tri] = 1 if ri == 0 else -1
    selw = np.zeros((32, 18 * 24))
    for kk in range(3):
        for ri in range(2):
            for tri in range(3):
                q = (tri * 3 + kk) * 48 + ri
                selw[kk * 8 + ri * 4 + tri, q : q + 2 * C : 2] = 1
    b = lambda a: np.asarray(a, np.float32).astype(BF16)
    return dict(
        tyf=np.concatenate(split(tyf)),
        tyi=np.concatenate(split(tyi)),
        wxp=np.stack([split(w) for w in wxp]),
        wxi=np.stack([split(w) for w in wxi]),
        px=b(px),
        pxt=b(px.T),
        pab=b(pab.reshape(48 * G, 32 * G)),
        selw=b(selw),
    )


def mm(a, b):
    return jnp.dot(a, b, preferred_element_type=F32)


def mm_nt(a, b):
    return lax.dot_general(a, b, (((1,), (1,)), ((), ())), preferred_element_type=F32)


def hilo(a):
    hi = a.astype(BF16)
    return hi, (a - hi.astype(F32)).astype(BF16)


def mm_tab(tab, x):
    hi, lo = hilo(x)
    return mm(tab[0], hi) + (mm(tab[0], lo) + mm(tab[1], hi))


def iota(shape, dim):
    return lax.broadcasted_iota(jnp.int32, shape, dim)


def onehot(cond):
    return jnp.where(cond, 1.0, 0.0).astype(BF16)


def lane_code(shape, stride):
    row = iota(shape, 0)
    q = row & 127
    kk = jnp.where(q >= 80, 2, jnp.where(q >= 40, 1, 0))
    c = (row >> 7) * 10 + ((q - 40 * kk) >> 2)
    return jnp.where(q < 120, (kk * stride + c) * 4 + (q & 3), -1)


def gelu_parts(h):
    k = math.sqrt(2.0 / math.pi)
    hh = h * h
    u = 0.5 * jnp.tanh(h * (k + (0.044715 * k) * hh)) + 0.5
    value = h * u
    slope = u + (value * (1.0 - u)) * (2.0 * k + (6.0 * 0.044715 * k) * hh)
    return value, slope


def kernel(
    G, D, f_hbm, tyf_hbm, w_hbm, mix_hbm, selw_hbm, wxp_hbm, pab_hbm, px_hbm, pxt_hbm, wxi_hbm, cot_hbm, tyi_hbm,
    out_ref, sg_ref, mg_ref,
    f_ref, tyf_ref, w_ref, mix_ref, selw_ref, wxp, pab_ref, px_ref, pxt_ref, wxi, cot, tyi, a3, b3, mixed, mixpad, backb,
    sx1, rx1, sx3, rx3, sy1, ry1, sy3, ry3, sy2, ry2, sx2, rx2,
    ws, rw, wst, rq, bc, ohg, gi, sspec, rspec, sgs, rgs, stt,
    mgx_s, mgx_r, mgy_s, mgy_r, part, rsbuf, agbuf, agsrc,
    ready, go, lsem, bx_s, bx_r, by_s, by_r, dp_s, dp_r,
):
    rows = C * 4 * G
    planes = 4 * G
    gx = lax.axis_index("gx")
    gy = lax.axis_index("gy")
    dp = lax.axis_index("dp")
    tpr = max(1, -(-TILES // D))
    nred = TILES // tpr

    hrows = rows // 2
    chunk = 160 if hrows % 160 == 0 else hrows
    chunks = [[h * hrows + r for r in range(0, hrows, chunk)] for h in range(2)]
    starts = chunks[0] + chunks[1]
    n = chunk
    pieces = [(f_hbm.at[pl.ds(r0, n)], f_ref.at[pl.ds(r0, n)]) for r0 in starts]
    pieces.insert(0, (tyf_hbm, tyf_ref))
    pieces += [(w_hbm, w_ref), (selw_hbm, selw_ref), (mix_hbm, mix_ref), (wxp_hbm.at[gy], wxp)]
    pieces += [(pab_hbm, pab_ref), (px_hbm, px_ref), (pxt_hbm, pxt_ref), (wxi_hbm.at[gy], wxi), (cot_hbm, cot), (tyi_hbm, tyi)]
    loads = [pltpu.make_async_copy(src, dst, lsem.at[k]) for k, (src, dst) in enumerate(pieces)]
    for copy in loads[: 1 + len(starts)]:
        copy.start()

    barrier = pltpu.get_barrier_semaphore()
    for k in range(1, G):
        pl.semaphore_signal(barrier, inc=1, device_id={"gx": lax.rem(gx + k, G)}, device_id_type=MESH)
    for k in range(1, GY):
        pl.semaphore_signal(barrier, inc=1, device_id={"gy": lax.rem(gy + k, GY)}, device_id_type=MESH)

    @pl.when(dp == 0)
    def _():
        for k in range(1, D):
            pl.semaphore_signal(barrier, inc=1, device_id={"dp": k}, device_id_type=MESH)


    for copy in loads[1 + len(starts) :]:
        copy.start()
    late = dict(zip(("w", "selw", "mix", "wxp", "pab", "px", "pxt", "wxi", "cot", "tyi"), loads[1 + len(starts) :]))

    pending = []

    def exchange(axis, size, me, src_of, dst, sems_s, sems_r, ex):
        def one(k):
            peer = lax.rem(me + k, size)
            return pltpu.make_async_remote_copy(
                src_ref=src_of(peer),
                dst_ref=dst.at[me],
                send_sem=sems_s.at[ex, k],
                recv_sem=sems_r.at[ex, k],
                device_id={axis: peer},
                device_id_type=MESH,
            )

        copies = [one(k) for k in sorted(range(1, size), key=lambda k: abs(2 * k - size))]
        for copy in copies:
            copy.start()
        pending.extend(copies)

        def wait():
            for copy in copies:
                copy.wait_recv()

        return wait

    def ex_x(src_of, dst, ex):
        return exchange("gx", G, gx, src_of, dst, bx_s, bx_r, ex)

    def ex_y(src_of, dst, ex):
        return exchange("gy", GY, gy, src_of, dst, by_s, by_r, ex)

    rest = jnp.zeros((8, 128), F32)

    def part_of(h, kk, r0):
        return pl.ds((h * 3 + kk) * hrows + r0 - h * hrows, n)

    def y_forward(data, h, r0):
        a = mm(jnp.concatenate([data, data], axis=1), tyf_ref[...])
        a3[part_of(h, 0, r0), :] = a
        a3[part_of(h, 1, r0), :] = pltpu.roll(a, 96, 1)
        a3[part_of(h, 2, r0), :] = pltpu.roll(a, 64, 1)

    def to_groups(h, dst):
        for g in range(G):
            block = a3[pl.ds(h * 3 * hrows + g, 120, stride=G), :]
            dst[h, g] = jnp.concatenate([block, rest], axis=0).T[:32]

    def to_planes(value):
        for i in range(4):
            gi[i] = value[:, i * 128 : (i + 1) * 128]

    loads[0].wait()
    wait_x1 = []
    for h in range(2):
        for r0 in chunks[h]:
            loads[1 + starts.index(r0)].wait()
            y_forward(f_ref[r0 : r0 + n, :], h, r0)
        to_groups(h, sx1)
        if h == 0:


            @pl.when(dp == 0)
            def _():
                pl.semaphore_wait(barrier, G - 1 + GY - 1)

            @pl.when(dp != 0)
            def _():
                pl.semaphore_wait(barrier, G - 1 + GY - 1 + 1)
                pl.semaphore_signal(ready, inc=1, device_id={"dp": 0}, device_id_type=MESH)

        wait_x1.append(ex_x(lambda peer: sx1.at[h, peer], rx1.at[h], h))
        rx1[h, gx] = sx1[h, gx]

    late["w"].wait()
    late["selw"].wait()
    wst[...] = jnp.zeros_like(wst)
    for m in range(9):
        wst[m * 48 : m * 48 + 2 * C, 0:C] = w_ref[m].astype(F32).reshape(2 * C, C)
    r = iota((128, 512), 1) & 127
    fifth = lambda r: sum(jnp.where(r >= 20 * k, 1, 0) for k in range(1, 5))
    ohd = onehot((iota((128, 512), 0) == r - 20 * fifth(r)) & (r < 100))
    wexp = mm(wst[...].astype(BF16), ohd)
    lane = iota((48, 512), 1)
    cond = (iota((48, 512), 0) >> 1) == (lane >> 7) * 5 + fifth(lane & 127)
    wparts = [jnp.where(cond, wexp[m * 48 : m * 48 + 48], 0.0) for m in range(9)]
    wmasked = jnp.concatenate(wparts, axis=0).astype(BF16)
    ws[...] = mm(selw_ref[...], wmasked).astype(BF16)
    late["mix"].wait()
    mixpad[...] = jnp.zeros_like(mixpad)
    mixpad[0:C, 0:C] = mix_ref[...].astype(F32)
    mixb = mixpad[...].astype(BF16)
    shift = int(math.log2(planes))
    ecol = onehot((iota((128, rows), 1) >> shift) == iota((128, rows), 0))
    for r0 in starts:
        erow = onehot(((iota((n, 128), 0) + r0) >> shift) == iota((n, 128), 1))
        kron = mm(mm_nt(erow, mixb).astype(BF16), ecol)
        diag = ((iota((n, rows), 0) + r0) & (planes - 1)) == (iota((n, rows), 1) & (planes - 1))
        kron = jnp.where(diag, kron, 0.0).astype(BF16)
        mixed[r0 : r0 + n, :] = mm(kron, f_ref[...])

    lanes = iota((256, 640), 1)
    for q in range(4):
        spot = ((lanes >> 7) + 5 * q) * 4 + (lanes & 3)
        bc[q] = onehot((iota((256, 640), 0) & 127) == spot)
    lanes = iota((128, 640), 1)
    row = (lanes >> 7) * 20 + ((lanes & 127) >> 2)
    ohr = onehot((iota((128, 640), 0) == row) & ((lanes & 127) < 80))
    col = iota((256, 512), 1)
    ohg[0] = onehot(lane_code((256, 512), 24) == (col & 127) * 4 + (col >> 7))
    ohg[1] = onehot(lane_code((256, 512), 20) == (col & 63) * 4 + (col >> 7))

    def x_forward(recv, send, h):
        hi, lo = hilo(recv[h].reshape(32 * G, 128))
        p = mm(wxp[0], hi) + (mm(wxp[0], lo) + mm(wxp[1], hi))
        send[h] = p.astype(send.dtype).reshape(GY, 6 * G, 128)

    def y_sum(recv, h):
        p = [recv[h, k].astype(F32) for k in range(GY)]
        return (p[0] + p[1]) + (p[2] + p[3])

    late["wxp"].wait()
    wait_y1 = []
    for h in range(2):
        wait_x1[h]()
        if h == 0:
            wait_w = ex_x(lambda peer: ws, rw, 2)
            rw[gx] = ws[...]
        x_forward(rx1, sy1, h)
        wait_y1.append(ex_y(lambda peer: sy1.at[h, peer], ry1.at[h], h))
        ry1[h, gy] = sy1[h, gy]

    wait_w()
    late["pab"].wait()
    rab = mm(pab_ref[...], rw[...].reshape(32 * G, 512)).astype(BF16)
    for q in range(4):
        rq[q] = mm(rab[:, q * 128 : (q + 1) * 128], ohr)
    late["px"].wait()
    late["pxt"].wait()

    for h in range(2):
        wait_y1[h]()
    shi, slo = hilo(jnp.concatenate([y_sum(ry1, h) for h in range(2)], axis=1))
    spec = mm(px_ref[...], shi) + mm(px_ref[...], slo)
    sspec[...] = spec.reshape(G, 8, 256)

    low = iota((8 * G, 128), 1) < 40
    turn = lambda a, by: pltpu.roll(a, by % 128, 1) if by % 128 else a
    parts = []
    for kk in range(3):
        h0, h1 = turn(spec[:, :128], -40 * kk), turn(spec[:, 128:], 40 - 40 * kk)
        parts.append(jnp.where(low, h0, h1))
    xx = jnp.concatenate(hilo(jnp.concatenate(parts, axis=0)), axis=1)
    acc = [jnp.zeros((24 * G, 128), F32) for _ in range(2)]
    for q in range(4):
        spread = mm(xx, bc[q])
        for ab in range(2):
            prod = spread * rq[q, ab * 24 * G : (ab + 1) * 24 * G]
            acc[ab] += sum(prod[:, k * 128 : k * 128 + 128] for k in range(5))
    swapped = pltpu.roll(acc[1].reshape(3 * G, 8, 128), 4, 1).reshape(24 * G, 128)
    acc = (acc[0] + swapped).reshape(3, 8 * G, 128)
    wait_y2 = []
    for h in range(2):
        mine = [jnp.where(low if h == 0 else ~low, acc[kk], 0.0) for kk in range(3)]
        vals = sum(turn(mine[kk], 40 * kk - 40 * h) for kk in range(3))
        sy2[h] = mm(pxt_ref[...], vals.astype(BF16)).astype(BF16)
        wait_y2.append(ex_y(lambda peer: sy2.at[h], ry2.at[h], 2 + h))
        ry2[h, gy] = sy2[h]

    @pl.when(dp == 0)
    def _():
        pl.semaphore_wait(ready, D - 1)
        for k in range(1, D):
            pl.semaphore_signal(go, inc=1, device_id={"dp": k}, device_id_type=MESH)

    wait_spec = ex_x(lambda peer: sspec.at[peer], rspec, 3)
    rspec[gx] = sspec[gx]

    late["wxi"].wait()
    wait_x2 = []
    for h in range(2):
        wait_y2[h]()
        v = ry2[h].reshape(24 * G, 128)
        b = mm(wxi[0], v) + mm(wxi[1], v)
        sx2[h] = b.astype(BF16).reshape(G, 32, 128)
        wait_x2.append(ex_x(lambda peer: sx2.at[h, peer], rx2.at[h], 4 + h))
        rx2[h, gx] = sx2[h, gx]

    wait_spec()
    hi, lo = hilo(rspec[...].reshape(8 * G, 256))
    to_planes(mm(hi, ohg[0]) + mm(lo, ohg[0]))
    for tri in range(3):
        block = []
        for i in range(4):
            for ri in range(2):
                block.append(gi[i, pl.ds(ri * 4 + tri, G, stride=8), :])
        block.append(jnp.zeros((128 - 8 * G, 128), F32))
        stt[tri] = jnp.concatenate(block, axis=0).T[:72]

    late["cot"].wait()
    late["tyi"].wait()
    def planes_back(h):
        wait_x2[h]()
        for g in range(G):
            block = jnp.concatenate([rx2[h, g].astype(F32), jnp.zeros((96, 128), F32)], axis=0)
            b3[pl.ds(h * 3 * hrows + g, 120, stride=G), :] = block.T[:120]

    def pointwise(h, r0):
        bb = b3[part_of(h, 0, r0), :]
        bb += pltpu.roll(b3[part_of(h, 1, r0), :], 32, 1)
        bb += pltpu.roll(b3[part_of(h, 2, r0), :], 64, 1)
        bb = bb.astype(BF16)
        pre = mm(jnp.concatenate([bb, bb], axis=1), tyi[...]) + mixed[r0 : r0 + n, :]
        value, slope = gelu_parts(pre)
        out_ref[r0 : r0 + n, :] = value.astype(BF16)
        back = (cot[r0 : r0 + n, :].astype(F32) * slope).astype(BF16)
        backb[r0 : r0 + n, :] = back
        y_forward(back, h, r0)

    wait_x3 = []
    for h in range(2):
        planes_back(h)
        for r0 in chunks[h]:
            pointwise(h, r0)
        to_groups(h, sx3)
        wait_x3.append(ex_x(lambda peer: sx3.at[h, peer], rx3.at[h], 6 + h))
        rx3[h, gx] = sx3[h, gx]

    gmix = jnp.zeros((24, 128), F32)
    ecol_t = onehot((iota((rows, 128), 0) >> shift) == iota((rows, 128), 1))
    for r0 in starts:
        full = mm_nt(f_ref[r0 : r0 + n, :], backb[...])
        diag = ((iota((n, rows), 0) + r0) & (planes - 1)) == (iota((n, rows), 1) & (planes - 1))
        hi, lo = hilo(jnp.where(diag, full, 0.0))
        cols = mm(hi, ecol_t) + mm(lo, ecol_t)
        erow_t = onehot(((iota((24, n), 1) + r0) >> shift) == iota((24, n), 0))
        hi, lo = hilo(cols)
        gmix += mm(erow_t, hi) + mm(erow_t, lo)
    mgx_s[...] = gmix
    mgx_r[gx] = gmix

    wait_y3 = []
    for h in range(2):
        wait_x3[h]()
        x_forward(rx3, sy3, h)
        wait_y3.append(ex_y(lambda peer: sy3.at[h, peer], ry3.at[h], 4 + h))
        ry3[h, gy] = sy3[h, gy]

    wait_mgx = ex_x(lambda peer: mgx_s, mgx_r, 8)
    wait_mgx()
    total = mgx_r[0]
    for k in range(1, G):
        total += mgx_r[k]
    mgy_s[...] = total
    wait_mgy = ex_y(lambda peer: mgy_s, mgy_r, 6)
    mgy_r[gy] = total

    wait_gs = []
    for h in range(2):
        wait_y3[h]()
        ghi, glo = hilo(y_sum(ry3, h))
        sgs[h] = (mm(px_ref[...], ghi) + mm(px_ref[...], glo)).reshape(G, 8, 128)
        wait_gs.append(ex_x(lambda peer: sgs.at[h, peer], rgs.at[h], 9 + h))
        rgs[h, gx] = sgs[h, gx]

    wait_mgy()
    mix_scale = 1.0 / math.sqrt(D * planes * 16 * G * NY)
    part[9:12] = (((mgy_r[0] + mgy_r[1]) + (mgy_r[2] + mgy_r[3])) * mix_scale).reshape(3, 8, 128)

    norm_in = 1.0 / math.sqrt(16 * G * NY)
    norm_out = 1.0 / math.sqrt(36 * G)
    spec_scale = norm_out / norm_in / math.sqrt(D * planes)
    for h in range(2):
        wait_gs[h]()
    hi, lo = hilo(jnp.concatenate([rgs[h].reshape(8 * G, 128) for h in range(2)], axis=1))
    to_planes(mm(hi, ohg[1]) + mm(lo, ohg[1]))
    lane = iota((G, 128), 1)
    lane24 = iota((24, 128), 1) & 63
    for tri in range(3):
        block = []
        for i in range(4):
            g0 = gi[i, pl.ds(tri, G, stride=8), :]
            g1 = gi[i, pl.ds(4 + tri, G, stride=8), :]
            block += [jnp.where(lane < 64, g0, g1), jnp.where(lane < 64, g1, -g0)]
        block.append(jnp.zeros((128 - 8 * G, 128), F32))
        ahi, alo = hilo(stt[tri])
        bhi, blo = hilo(jnp.concatenate(block, axis=0))
        outer = mm(ahi, bhi) + (mm(ahi, blo) + mm(alo, bhi))
        grad = jnp.zeros((24, 128), F32)
        for kk in range(3):
            mine = (lane24 >= 20 * kk) & (lane24 < 20 * kk + 20)
            grad += jnp.where(mine, outer[24 * kk : 24 * kk + 24], 0.0)
        part[3 * tri : 3 * tri + 3] = (grad * spec_scale).reshape(3, 8, 128)

    def rs_copy(k, to):
        return pltpu.make_async_remote_copy(
            src_ref=part.at[pl.ds(to * tpr, tpr)],
            dst_ref=rsbuf.at[dp],
            send_sem=dp_s.at[0, k],
            recv_sem=dp_r.at[0, k],
            device_id={"dp": to},
            device_id_type=MESH,
        )

    def ag_copy(k, to, slot):
        return pltpu.make_async_remote_copy(
            src_ref=agsrc,
            dst_ref=agbuf.at[slot],
            send_sem=dp_s.at[1, k],
            recv_sem=dp_r.at[1, k],
            device_id={"dp": to},
            device_id_type=MESH,
        )

    @pl.when(dp != 0)
    def _():
        pl.semaphore_wait(go, 1)

    far = sorted(range(1, D), key=lambda k: -min(k % 8, 8 - k % 8))
    for k in far:
        to = lax.rem(dp + k, D)

        @pl.when(to < nred)
        def _():
            rs_copy(k, to).start()

    @pl.when(dp < nred)
    def _():
        rsbuf[dp] = part[pl.ds(dp * tpr, tpr)]
        for k in range(1, D):
            rs_copy(k, dp).wait_recv()
        tile = rsbuf[0]
        for k in range(1, D):
            tile += rsbuf[k]
        agsrc[...] = tile
        for k in far:
            ag_copy(k, lax.rem(dp + k, D), dp).start()
        agbuf[dp] = tile

    for copy in pending:
        copy.wait_send()
    for k in range(1, D):
        to = lax.rem(dp + k, D)

        @pl.when(to < nred)
        def _():
            rs_copy(k, to).wait_send()

    for k in range(1, D):
        frm = lax.rem(dp + D - k, D)

        @pl.when(frm < nred)
        def _():
            ag_copy(k, dp, frm).wait_recv()

    final = agbuf[...].reshape(TILES, 8, 128)
    mg_ref[...] = final[9:12].reshape(24, 128)[:C, :C]
    pairs = iota((40, 64), 0) == (iota((40, 64), 1) & 31) * 2 + (iota((40, 64), 1) >> 5)
    pairs = onehot(pairs)
    gap = jnp.zeros((8, 128), F32)
    for tri in range(3):
        block = final[3 * tri : 3 * tri + 3].reshape(24, 128)
        both = jnp.concatenate([block, gap, pltpu.roll(block, 64, 1), gap], axis=0)
        hi, lo = hilo(both)
        both = mm(pairs, hi) + mm(pairs, lo)
        for kk in range(3):
            piece = both if kk == 0 else pltpu.roll(both, 128 - 20 * kk, 1)
            sg_ref[tri * 3 + kk] = piece[:, :C].reshape(C, 2, C)

    @pl.when(dp < nred)
    def _():
        for k in range(1, D):
            ag_copy(k, lax.rem(dp + k, D), dp).wait_send()


def store_kernel(out, sg, mg, out_hbm, sg_hbm, mg_hbm, sems):
    step = out.shape[0] // 4
    pairs = [(sg, sg_hbm), (mg, mg_hbm)]
    pairs += [(out.at[pl.ds(k * step, step)], out_hbm.at[pl.ds(k * step, step)]) for k in range(4)]
    copies = [pltpu.make_async_copy(src, dst, sems.at[k]) for k, (src, dst) in enumerate(pairs)]
    for copy in copies:
        copy.start()
    for copy in copies:
        copy.wait()


def local(G, D, fields, cotangent, mix_weight, spectral_weight):
    rows = C * 4 * G
    cells = XL * NY
    t = tables(G)
    tpr = max(1, -(-TILES // D))
    nred = TILES // tpr
    vm = pl.BlockSpec(memory_space=pltpu.VMEM)
    hbm = pl.BlockSpec(memory_space=pl.ANY)
    V = pltpu.VMEM
    scratch = [
        V((rows, cells), BF16),
        V((2 * cells, 128), BF16),
        V((9, C, 2, C), BF16),
        V((C, C), BF16),
        V((32, 432), BF16),
        V((2, GY * 6 * G, 32 * G), BF16),
        V((48 * G, 32 * G), BF16),
        V((8 * G, 6 * G), BF16),
        V((6 * G, 8 * G), BF16),
        V((2, 32 * G, GY * 6 * G), BF16),
        V((rows, cells), BF16),
        V((256, cells), BF16),
        V((3 * rows, 128), F32),
        V((3 * rows, 128), F32),
        V((rows, cells), F32),
        V((128, 128), F32),
        V((rows, cells), BF16),
        V((2, G, 32, 128), F32),
        V((2, G, 32, 128), F32),
        V((2, G, 32, 128), F32),
        V((2, G, 32, 128), F32),
        V((2, GY, 6 * G, 128), F32),
        V((2, GY, 6 * G, 128), F32),
        V((2, GY, 6 * G, 128), BF16),
        V((2, GY, 6 * G, 128), BF16),
        V((2, 6 * G, 128), BF16),
        V((2, GY, 6 * G, 128), BF16),
        V((2, G, 32, 128), BF16),
        V((2, G, 32, 128), BF16),
        V((32, 512), BF16),
        V((G, 32, 512), BF16),
        V((432, 128), F32),
        V((4, 48 * G, 640), F32),
        V((4, 256, 640), BF16),
        V((2, 256, 512), BF16),
        V((4, 8 * G, 128), F32),
        V((G, 8, 256), F32),
        V((G, 8, 256), F32),
        V((2, G, 8, 128), F32),
        V((2, G, 8, 128), F32),
        V((3, 72, 128), F32),
        V((24, 128), F32),
        V((G, 24, 128), F32),
        V((24, 128), F32),
        V((GY, 24, 128), F32),
        V((TILES, 8, 128), F32),
        V((D, tpr, 8, 128), F32),
        V((nred, tpr, 8, 128), F32),
        V((tpr, 8, 128), F32),
        pltpu.SemaphoreType.REGULAR,
        pltpu.SemaphoreType.REGULAR,
        pltpu.SemaphoreType.DMA((32,)),
        pltpu.SemaphoreType.DMA((11, G)),
        pltpu.SemaphoreType.DMA((11, G)),
        pltpu.SemaphoreType.DMA((7, GY)),
        pltpu.SemaphoreType.DMA((7, GY)),
        pltpu.SemaphoreType.DMA((2, D)),
        pltpu.SemaphoreType.DMA((2, D)),
    ]
    out, sg, mg = pl.pallas_call(
        functools.partial(kernel, G, D),
        out_shape=(
            V((rows, cells), BF16),
            V((9, C, 2, C), F32),
            V((C, C), F32),
        ),
        in_specs=[hbm] * 12,
        out_specs=(vm, vm, vm),
        scratch_shapes=scratch,
        compiler_params=pltpu.CompilerParams(
            collective_id=0, has_side_effects=True, vmem_limit_bytes=60 * 1024 * 1024
        ),
    )(
        fields.reshape(rows, cells),
        t["tyf"],
        spectral_weight.transpose(0, 2, 1, 3),
        mix_weight,
        t["selw"],
        t["wxp"],
        t["pab"],
        t["px"],
        t["pxt"],
        t["wxi"],
        cotangent.reshape(rows, cells),
        t["tyi"],
    )
    out, sg, mg = pl.pallas_call(
        store_kernel,
        out_shape=tuple(jax.ShapeDtypeStruct(a.shape, a.dtype) for a in (out, sg, mg)),
        in_specs=[hbm] * 3,
        out_specs=(hbm,) * 3,
        scratch_shapes=[pltpu.SemaphoreType.DMA((6,))],
        compiler_params=pltpu.CompilerParams(vmem_limit_bytes=1 << 20),
    )(out, sg, mg)
    return out.reshape(fields.shape), sg.transpose(0, 2, 1, 3), mg


def solution(mesh):
    G, D = mesh.shape["gx"], mesh.shape["dp"]
    cells = P("dp", None, None, ("gx", "gy"))
    modes = P(("gx", "gy"), None, None, None)
    return jax.shard_map(
        functools.partial(local, G, D),
        mesh=mesh,
        in_specs=(cells, cells, P(), modes),
        out_specs=(cells, modes, P()),
        check_vma=False,
    )
```
